256 devices in a mesh: dp: 32 (over z, x), fsdp: 8 (over y, core).
Axes of the slice: x: 4, y: 4, z: 8, core: 2. Of those that a mesh axis runs over, the one named last changes fastest.
Arguments:
- hidden: bfloat16 [64, 256, 5120], P('dp', None, 'fsdp'), may hold values from -8 to 8
- gain: bfloat16 [5120], P('fsdp'), may hold values from 0.25 to 1.75
- head: bfloat16 [4096, 5120], P('fsdp'), may hold values from -1 to 1
- targets: int32 [64, 256], P('dp'), may hold values from 0 to 4095, as said below
- lengths: int32 [64], P('dp'), may hold values from 1 to 256, 8192 in all
- old_logp: float32 [64, 256], P('dp'), may hold values from -64 to 0
- rewards: float32 [64], P('dp'), may hold values from -6 to 6
- group_slot: int32 [64], P('dp'), may hold values from 0 to 63, each once
Outputs:
- loss: float32 [], replicated
- grad_hidden: bfloat16 [64, 256, 5120], P('dp', None, 'fsdp')
- grad_gain: float32 [5120], P('fsdp')
- grad_head_t: float32 [5120, 4096], P('dp', 'fsdp')
The draws below stay inside these ranges and needn't reach their ends.
Inputs may be any that keep to these rules, and one draw needn't show every extreme that they name: `lengths`: they sum to 8192 and one of them equals 256. `group_slot`: each value once; responses with equal group_slot // 8 answer one prompt. At position 0, different responses have different targets.
All inputs are finite; a program needn't handle non-finite values. No bound on the sum of `lengths` on one device may be relied on, other than what follows from the above.
Results may differ from the reference program's by a relative error of at most 0.018.
Values may be sent and summed in bfloat16 or wider, within the bound.
No kernel may reach another device: no remote copies, remote signals or barrier semaphores. Data moves between devices by JAX's collectives and lax.ppermute only.
A program may use at most 64 MiB of HBM per device.

```python
import math
import jax
import jax.numpy as jnp
import numpy as np
from jax import lax

D = 5120
VOC_DEV = 512
LEN = 256
GROUP = 8
RESP_DEV = 2
RESPONSES = 64
VOCAB = 4096
NGROUPS = 8
TOKENS = 16384
N_DP = 32
N_FSDP = 8


def drawn_entries(key):
    amount = RESPONSES
    order = jax.random.permutation(jax.random.fold_in(key, 7001), VOCAB).astype(jnp.int32)
    return order[:amount]


def draw_targets(key, part):
    upper_ids = drawn_entries(key)
    base = jax.random.randint(jax.random.fold_in(key, 7101), (RESPONSES, LEN), 0, VOCAB, jnp.int32)
    return base.at[:, 0].set(upper_ids)


def draw_hidden(key, part):
    base = jax.random.normal(jax.random.fold_in(key, 7201), (RESPONSES, LEN, D), jnp.float32)
    base = jnp.clip(base, -6.0, 6.0)
    return base.astype(jnp.bfloat16)


def draw_gain(key, part):
    base = jax.random.normal(jax.random.fold_in(key, 7501), (D,), jnp.float32)
    return (1.0 + 0.15 * jnp.clip(base, -5.0, 5.0)).astype(jnp.bfloat16)


def draw_head(key, part):
    spread = math.sqrt(9.0 / D)
    base = jax.random.normal(jax.random.fold_in(key, 7301), (VOCAB, D), jnp.float32) * spread
    base = jnp.clip(base, -6.0 * spread, 6.0 * spread)
    return base.astype(jnp.bfloat16)


def draw_old_logp(key, part):
    states = draw_hidden(key, part)
    gain_f = draw_gain(key, part).astype(jnp.float32)
    weights = draw_head(key, part)
    picks = draw_targets(key, part)

    def response_logp(item):
        rows_here, chosen_ids = item
        values = rows_here.astype(jnp.float32)
        inv = lax.rsqrt(jnp.mean(values * values, axis=1, keepdims=True) + 1e-06)
        normed = (values * inv * gain_f).astype(jnp.bfloat16)
        logits = lax.dot_general(normed, weights, (((1,), (1,)), ((), ())), preferred_element_type=jnp.float32)
        top = jnp.max(logits, axis=1)
        lse = top + jnp.log(jnp.sum(jnp.exp(logits - top[:, None]), axis=1))
        hits = jnp.arange(VOCAB, dtype=jnp.int32)[None, :] == chosen_ids[:, None]
        return jnp.sum(jnp.where(hits, logits, 0.0), axis=1) - lse
    logp = lax.map(response_logp, (states, picks))
    band = jax.random.randint(jax.random.fold_in(key, 7402), (RESPONSES, LEN), 0, 4, jnp.int32)
    lows = jnp.log(jnp.array([0.5, 0.88, 1.4, 3.6], jnp.float32))
    highs = jnp.log(jnp.array([0.7, 1.12, 2.5, 6.0], jnp.float32))
    lower_edge = jnp.take(lows, band)
    upper_edge = jnp.take(highs, band)
    level = jax.random.uniform(jax.random.fold_in(key, 7403), (RESPONSES, LEN), jnp.float32, 0.0, 1.0)
    logratio = lower_edge + level * (upper_edge - lower_edge)
    older = logp - logratio
    older = jnp.where(older > 0.0, logp - math.log(2.0), older)
    return jnp.clip(older, -64.0, 0.0)


def block_scale(key, dims, split, smallest, high):
    level = 1.0
    for axis_at, shards_of in split:
        heights = jax.random.uniform(jax.random.fold_in(jax.random.fold_in(key, 6), axis_at), (shards_of,), jnp.float32, smallest / len(split), high / len(split))
        level = level * jnp.repeat(jnp.exp(heights), dims[axis_at] // shards_of).reshape((-1,) + (1,) * (len(dims) - 1 - axis_at))
    return level


def length_profile(number_of, total, limit, lean):
    loads = [(1 << 20) // math.isqrt(standing ** lean) + 1 for standing in range(2, number_of + 1)]
    surplus, counts = total - limit - (number_of - 1), [1] * (number_of - 1)
    while surplus > 0:
        candidates = [i for i in range(number_of - 1) if counts[i] < limit]
        pool, budget = sum([loads[i] for i in candidates]), surplus
        for i in candidates:
            more = min(limit - counts[i], max(1, budget * loads[i] // pool), surplus)
            counts[i] = counts[i] + more
            surplus = surplus - more
    return np.array([limit] + counts)


def uneven(own_key, count, total, limit, skew):
    if count == 2:
        one = jax.random.randint(own_key, (), max(1, total - limit), min(limit, total - 1) + 1)
        return jnp.stack([one, total - one])
    sizes = jnp.asarray(length_profile(count, total, limit, skew), jnp.int32)
    couples = (count - 1) // 2
    source_of, taker = sizes[1:1 + 2 * couples:2], sizes[2:2 + 2 * couples:2]
    slack = jnp.minimum(source_of - 1, limit - taker)
    shifted = jax.random.randint(jax.random.fold_in(own_key, 1), (couples,), 0, 1 << 20) % (slack + 1)
    sizes = sizes.at[1:1 + 2 * couples:2].set(source_of - shifted).at[2:2 + 2 * couples:2].set(taker + shifted)
    return sizes[jax.random.permutation(jax.random.fold_in(own_key, 2), count)]


def normal_values(own_key, shape, scale, reach, split=(), kind=jnp.bfloat16):
    result = scale * jax.random.normal(own_key, shape, jnp.float32)
    if split:
        result = result * block_scale(own_key, shape, split, -0.22, 0.18)
    return jnp.clip(result, -reach, reach).astype(kind)


def setup_inputs(seed: int = 0) -> dict:
    key_list = jax.random.split(jax.random.key(seed), 9)
    hidden = draw_hidden(jax.random.fold_in(key_list[8], 71), 0)
    gain = draw_gain(jax.random.fold_in(key_list[8], 71), 0)
    head = draw_head(jax.random.fold_in(key_list[8], 71), 0)
    targets = draw_targets(jax.random.fold_in(key_list[8], 71), 0)
    lengths = uneven(key_list[4], RESPONSES, RESPONSES * LEN // 2, LEN, 2).astype(jnp.int32)
    old_logp = draw_old_logp(jax.random.fold_in(key_list[8], 71), 0)
    rewards = normal_values(key_list[6], (RESPONSES,), 1.0, 6.0, ((0, 32),), jnp.float32)
    group_slot = jax.random.permutation(key_list[7], RESPONSES).astype(jnp.int32)
    return {"hidden": hidden, "gain": gain, "head": head, "targets": targets, "lengths": lengths, "old_logp": old_logp, "rewards": rewards, "group_slot": group_slot}


eps_norm = 1e-06
clip_low = 0.8
clip_high = 1.2
dual_bound = 3.0

def reference(hidden, gain, head, targets, lengths, old_logp, rewards, group_slot):
    rows = RESPONSES * LEN
    h = hidden.reshape(rows, D).astype(jnp.float32)
    inv = lax.rsqrt(lax.optimization_barrier(jnp.mean(h * h, axis=1, keepdims=True)) + eps_norm)
    gain_f = gain.astype(jnp.float32)
    normed = (h * inv * gain_f).astype(jnp.bfloat16)
    logits = lax.dot_general(normed.astype(jnp.float32), head.astype(jnp.float32), (((1,), (1,)), ((), ())), preferred_element_type=jnp.float32)
    top = lax.optimization_barrier(jnp.max(logits, axis=1, keepdims=True))
    lse = top[:, 0] + jnp.log(lax.optimization_barrier(jnp.sum(jnp.exp(logits - top), axis=1)))
    flat_targets = targets.reshape(rows).astype(jnp.int32)
    hits = jnp.arange(VOCAB, dtype=jnp.int32)[None, :] == flat_targets[:, None]
    chosen = lax.optimization_barrier(jnp.sum(jnp.where(hits, logits, 0.0), axis=1))
    logp = chosen - lse
    group = group_slot // GROUP
    member = (group[:, None] == jnp.arange(NGROUPS, dtype=jnp.int32)[None, :]).astype(jnp.float32)
    group_sums = lax.optimization_barrier(jnp.sum(member * rewards[:, None], axis=0))
    adv_resp = rewards - lax.optimization_barrier(jnp.sum(member * group_sums[None, :], axis=1)) / GROUP
    adv = jnp.repeat(adv_resp, LEN)
    mask = (jnp.arange(LEN, dtype=jnp.int32)[None, :] < lengths[:, None]).astype(jnp.float32).reshape(rows)
    count = jnp.sum(lengths).astype(jnp.float32)
    ratio = jnp.exp(logp - old_logp.reshape(rows))
    first = ratio * adv
    second = jnp.clip(ratio, clip_low, clip_high) * adv
    policy = -jnp.minimum(first, second)
    policy = jnp.where(adv < 0, jnp.minimum(policy, -dual_bound * adv), policy)
    loss = jnp.sum(mask * policy) / count
    active = (first <= second) & jnp.logical_not((adv < 0) & (first < dual_bound * adv))
    grad_logp = TOKENS / count * mask * jnp.where(active, -ratio * adv, 0.0)
    probs = jnp.exp(logits - lse[:, None])
    dlogits = (grad_logp[:, None] * (hits.astype(jnp.float32) - probs)).astype(jnp.bfloat16)

    def add_block(total, index):
        piece = lax.dynamic_slice_in_dim(dlogits, index * VOC_DEV, VOC_DEV, 1)
        rows_w = lax.dynamic_slice_in_dim(head, index * VOC_DEV, VOC_DEV, 0)
        term = jnp.dot(piece.astype(jnp.float32), rows_w.astype(jnp.float32), preferred_element_type=jnp.float32)
        return (total + term.astype(jnp.bfloat16).astype(jnp.float32), None)
    dnormed, _ = lax.scan(add_block, jnp.zeros((rows, D), jnp.float32), jnp.arange(N_FSDP, dtype=jnp.int32))
    dy = dnormed * gain_f
    dots = lax.optimization_barrier(jnp.sum(h * dy, axis=1, keepdims=True))
    grad_h = inv * dy - h * inv * inv * inv * dots / D
    grad_hidden = grad_h.astype(jnp.bfloat16).reshape(RESPONSES, LEN, D)
    grad_gain = lax.optimization_barrier(jnp.sum(dnormed * h * inv, axis=0))
    per_group = RESP_DEV * LEN

    def add_group(total, index):
        left = lax.dynamic_slice_in_dim(normed, index * per_group, per_group, 0)
        right = lax.dynamic_slice_in_dim(dlogits, index * per_group, per_group, 0)
        term = lax.dot_general(left.astype(jnp.float32), right.astype(jnp.float32), (((0,), (0,)), ((), ())), preferred_element_type=jnp.float32)
        return (total + term.astype(jnp.bfloat16).astype(jnp.float32), None)
    grad_head_t, _ = lax.scan(add_group, jnp.zeros((D, VOCAB), jnp.float32), jnp.arange(N_DP, dtype=jnp.int32))
    return (loss, grad_hidden, grad_gain, grad_head_t)
```

```python
import functools

import jax
import jax.numpy as jnp
from jax import lax
from jax.experimental import pallas as pl
from jax.experimental.pallas import tpu as pltpu
from jax.sharding import Mesh
from jax.sharding import PartitionSpec as P

GROUP = 8
FSDP = ("y", "c")
DP = ("z", "x")
SIZES = {"z": 8, "x": 4, "y": 4, "c": 2}

eps_norm = 1e-06
clip_low = 0.8
clip_high = 1.2
dual_bound = 3.0

f32, bf16 = jnp.float32, jnp.bfloat16
VMEM = pltpu.VMEM


def shift(value, axis, step):
    n = SIZES[axis]
    return lax.ppermute(value, axis, [(i, (i + step) % n) for i in range(n)])


def turn(value, step):
    return lax.ppermute(
        value, "z", [(i, (i + (step if i % 2 == 0 else -step)) % 8) for i in range(8)]
    )


def params(limit=60 << 20):
    return pltpu.CompilerParams(vmem_limit_bytes=limit)


def cost(flops, nbytes, trans=0):
    return pl.CostEstimate(flops=flops, bytes_accessed=nbytes, transcendentals=trans)


def whole(space=None):
    return pl.BlockSpec(memory_space=space or VMEM)


def column(row):
    n = row.shape[1]
    return jnp.transpose(jnp.broadcast_to(row, (128, n)))[:, 0:1]


def rows_of(columns):
    n = columns[0].shape[0]
    lane = lax.broadcasted_iota(jnp.int32, (n, 128), 1)
    table = jnp.zeros((n, 128), f32)
    for k, col in enumerate(columns):
        table = jnp.where(lane == k, col, table)
    return jnp.transpose(table)[0:8, :]


def scale_kernel(at, h_ref, g_ref, keep_ref, send_ref, sq_ref, sqo_ref):
    c = at[1]
    gain = g_ref[...].astype(f32)
    mine, other = h_ref[c].astype(f32), h_ref[1 - c].astype(f32)
    send_ref[...] = (other * gain).astype(bf16)
    keep_ref[...] = (mine * gain).astype(bf16)
    sq_ref[...] = rows_of([jnp.sum(mine * mine, axis=1, keepdims=True)])
    sqo_ref[...] = rows_of([jnp.sum(other * other, axis=1, keepdims=True)])


def scale(at, hidden, gain):
    _, rows, cols = hidden.shape
    return pl.pallas_call(
        scale_kernel,
        out_shape=[jax.ShapeDtypeStruct((rows, cols), bf16)] * 2
        + [jax.ShapeDtypeStruct((8, rows), f32)] * 2,
        in_specs=[whole(pltpu.SMEM), whole(), whole()],
        out_specs=[whole()] * 4,
        compiler_params=params(),
        cost_estimate=cost(4 * hidden.size, 4 * hidden.size),
        name="scale",
    )(at, hidden, gain.reshape(1, cols))


def logits_kernel(at, *refs):
    blocks, (sq0, sq1, sq2, sq3, tgt, head_a, head_b), (lg, st, inv_ref), (acc,) = (
        refs[:8],
        refs[8:15],
        refs[15:18],
        refs[18:],
    )
    k = pl.program_id(0)
    half = head_a.shape[0]
    for j in range(8):

        @pl.when(k == j)
        def _(j=j):
            for first, head in ((0, head_a), (half, head_b)):
                part = lax.dot_general(
                    blocks[j][...], head[...], (((1,), (1,)), ((), ())), preferred_element_type=f32
                )
                if j == 0:
                    acc[:, first : first + half] = part
                else:
                    acc[:, first : first + half] += part

    @pl.when(k == 7)
    def _():
        y, c = at[0], at[1]
        total_sq = sq0[0:1, :] + sq1[0:1, :] + sq2[0:1, :] + sq3[0:1, :]
        inv = lax.rsqrt(total_sq / 5120.0 + eps_norm)
        inv_ref[...] = jnp.broadcast_to(inv, inv_ref.shape)
        target = jnp.where(c == 0, tgt[0:1, :], tgt[1:2, :]).astype(f32)
        inv_c, target_c = column(inv), column(target).astype(jnp.int32)
        logits = acc[...] * inv_c
        lg[...] = logits
        lane = lax.broadcasted_iota(jnp.int32, logits.shape, 1)
        entry = 2 * y * half + jnp.where(
            lane < half, lane + c * half, lane - half + (1 - c) * half
        )
        top = jnp.max(logits, axis=1, keepdims=True)
        power = jnp.exp(logits - top)
        st[...] = rows_of(
            [
                top,
                jnp.sum(power, axis=1, keepdims=True),
                jnp.sum(power * logits, axis=1, keepdims=True),
                jnp.sum(jnp.where(entry == target_c, logits, 0.0), axis=1, keepdims=True),
            ]
        )


def head_specs(half, cols):
    def place(k, at):
        return (0, 2 * lax.rem(at[0] + k // 2, 4) + lax.rem(at[1] + lax.rem(k, 2), 2))

    return [pl.BlockSpec((half, cols), place)] * 2


def full(shape):
    return pl.BlockSpec(shape, lambda k, at: (0,) * len(shape))


def logits_of(at, blocks, squares, targets, head_a, head_b):
    rows, cols = blocks[0].shape
    half = head_a.shape[0]
    return pl.pallas_call(
        logits_kernel,
        out_shape=[
            jax.ShapeDtypeStruct((rows, 2 * half), f32),
            jax.ShapeDtypeStruct((8, rows), f32),
            jax.ShapeDtypeStruct((8, rows), f32),
        ],
        grid_spec=pltpu.PrefetchScalarGridSpec(
            num_scalar_prefetch=1,
            grid=(8,),
            in_specs=[full((rows, cols))] * 8
            + [full((8, rows))] * 4
            + [full((2, rows))]
            + head_specs(half, cols),
            out_specs=[full((rows, 2 * half)), full((8, rows)), full((8, rows))],
            scratch_shapes=[VMEM((rows, 2 * half), f32)],
        ),
        compiler_params=params(),
        cost_estimate=cost(2 * rows * 2 * half * 8 * cols, 4 * half * 8 * cols, rows * 2 * half),
        name="logits",
    )(at, *blocks, *squares, targets, head_a, head_b)


def grads_kernel(at, *refs):
    (nums, s0, s1, s2, s3, lg, inv_ref, tgt, old, head_a, head_b) = refs[:11]
    dl_a, dl_b, small = refs[11:14]
    outs = refs[14:18]
    k = pl.program_id(0)
    half, cols = head_a.shape

    @pl.when(k == 0)
    def _():
        y, c = at[0], at[1]
        adv, length, scaling = nums[0], nums[1], nums[2]
        parts = [s0, s1, s2, s3]
        top = functools.reduce(jnp.maximum, [s[0:1, :] for s in parts])
        weight = [jnp.exp(s[0:1, :] - top) for s in parts]
        total = sum(s[1:2, :] * w for s, w in zip(parts, weight))
        first_moment = sum(s[2:3, :] * w for s, w in zip(parts, weight))
        chosen = sum(s[3:4, :] for s in parts)
        lse = top + jnp.log(total)
        inv = inv_ref[0:1, :]
        ratio = jnp.exp(chosen - lse - jnp.where(c == 0, old[0:1, :], old[1:2, :]))
        position = lax.broadcasted_iota(jnp.int32, ratio.shape, 1).astype(f32)
        mask = jnp.where(position < length, 1.0, 0.0)
        first = ratio * adv
        second = jnp.clip(ratio, clip_low, clip_high) * adv
        policy = -jnp.minimum(first, second)
        policy = jnp.where(adv < 0, jnp.minimum(policy, -dual_bound * adv), policy)
        active = (first <= second) & jnp.logical_not((adv < 0) & (first < dual_bound * adv))
        grad_logp = scaling * mask * jnp.where(active, -first, 0.0)
        kappa = inv * inv * grad_logp * (chosen - first_moment / total) / 5120.0
        small[...] = jnp.concatenate(
            [kappa, mask * policy, jnp.zeros((6, ratio.shape[1]), f32)], axis=0
        )
        target = jnp.where(c == 0, tgt[0:1, :], tgt[1:2, :]).astype(f32)
        lse_c, target_c = column(lse), column(target).astype(jnp.int32)
        scale_c = column(grad_logp * inv)
        for first_at, start, out in ((0, c, dl_a), (half, 1 - c, dl_b)):
            logits = lg[:, first_at : first_at + half]
            entry = lax.broadcasted_iota(jnp.int32, logits.shape, 1) + (2 * y + start) * half
            hit = jnp.where(entry == target_c, 1.0, 0.0)
            out[...] = (scale_c * (hit - jnp.exp(logits - lse_c))).astype(bf16)

    for j in range(8):

        @pl.when(k == j)
        def _(j=j):
            part = jnp.dot(dl_a[...], head_a[...], preferred_element_type=f32)
            part += jnp.dot(dl_b[...], head_b[...], preferred_element_type=f32)
            outs[j // 2][:, (j % 2) * cols : (j % 2 + 1) * cols] = part.astype(bf16)


def grads_of(at, nums, stats, logits, inv, targets, old_logp, head_a, head_b, cols):
    rows = logits.shape[0]
    half = head_a.shape[0]
    return pl.pallas_call(
        grads_kernel,
        out_shape=[jax.ShapeDtypeStruct((rows, half), bf16)] * 2
        + [jax.ShapeDtypeStruct((8, rows), f32)]
        + [jax.ShapeDtypeStruct((rows, 2 * cols), bf16)] * 4,
        grid_spec=pltpu.PrefetchScalarGridSpec(
            num_scalar_prefetch=1,
            grid=(8,),
            in_specs=[whole(pltpu.SMEM)]
            + [full((8, rows))] * 4
            + [full((rows, 2 * half)), full((8, rows)), full((2, rows)), full((2, rows))]
            + head_specs(half, cols),
            out_specs=[full((rows, half))] * 2
            + [full((8, rows))]
            + [full((rows, 2 * cols))] * 4,
        ),
        compiler_params=params(),
        cost_estimate=cost(2 * rows * 2 * half * 8 * cols, 4 * half * 8 * cols, rows * 2 * half),
        name="grads",
    )(at, nums, *stats, logits, inv, targets, old_logp, head_a, head_b)


def product(mine, other, dl_m, dl_o, first, width):
    dims = (((0,), (0,)), ((), ()))
    cut = slice(first, first + width)
    part = lax.dot_general(mine[...], dl_m[:, cut], dims, preferred_element_type=f32)
    return part + lax.dot_general(other[...], dl_o[:, cut], dims, preferred_element_type=f32)


def far_of(at, j, c_first):
    y, z = at[0], at[2]
    own = 2 * lax.rem(y + j // 2, 4) + lax.rem(c_first + j % 2, 2)
    return lax.rem(own - z + 8, 8)


def heads_x_kernel(at, *refs):
    mine, other, (dl_m, dl_o) = refs[:8], refs[8:16], refs[16:18]
    outs, (tmp,) = refs[18:22], refs[22:]
    x = at[3]
    step = tmp.shape[0] // 4
    for j in range(8):
        tmp[...] = product(mine[j], other[j ^ 1], dl_m, dl_o, 0, tmp.shape[1])
        place = far_of(at, j, at[1])
        for k in range(4):
            start = pl.multiple_of(lax.rem(x + k, 4) * step, step)
            outs[k][place] = tmp[pl.ds(start, step), :].astype(bf16)


def heads_z_kernel(at, *refs):
    mine, other, (dl_m, dl_o) = refs[:8], refs[8:16], refs[16:18]
    send, keep, (tmp,) = refs[18:20], refs[20:22], refs[22:]
    x, z = at[3], at[2]
    step = tmp.shape[0] // 4
    odd = lax.rem(z, 2)
    width = tmp.shape[1] // 2
    for j in range(8):
        tmp[...] = product(mine[j], other[j ^ 1], dl_m, dl_o, tmp.shape[1], tmp.shape[1])
        ahead = far_of(at, j, at[1])
        behind = lax.rem(8 - ahead, 8)
        for side in range(2):
            q = jnp.where(odd == side, ahead, behind)
            low = lax.rem(q, 4)
            sent = (low == 1) | (low == 2)
            send_at = 2 * (q // 4) + low - 1
            keep_at = jnp.where(q == 0, 0, jnp.where(q == 7, 1, jnp.where(q == 4, 2, 3)))
            for k in range(4):
                start = pl.multiple_of(lax.rem(x + k, 4) * step, step)

                @pl.when(sent)
                def _(side=side, k=k, start=start, send_at=send_at):
                    send[side][send_at, k] = tmp[
                        pl.ds(start, step), side * width : (side + 1) * width
                    ].astype(bf16)

                @pl.when(jnp.logical_not(sent))
                def _(side=side, k=k, start=start, keep_at=keep_at):
                    keep[side][keep_at, k] = tmp[
                        pl.ds(start, step), side * width : (side + 1) * width
                    ].astype(bf16)


def heads_of(at, mine, other, dl_m, dl_o, kernel, shapes, name):
    rows, cols = mine[0].shape
    half = dl_m.shape[1]
    return pl.pallas_call(
        kernel,
        out_shape=[jax.ShapeDtypeStruct(s, bf16) for s in shapes],
        in_specs=[whole(pltpu.SMEM)] + [whole()] * 18,
        out_specs=[whole()] * len(shapes),
        scratch_shapes=[VMEM((cols, half // 2), f32)],
        compiler_params=params(),
        cost_estimate=cost(2 * 2 * rows * 8 * cols * half // 2, 8 * 8 * rows * cols),
        name=name,
    )(at, *mine, *other, dl_m, dl_o)


def sum_cut_kernel(n, groups, *refs):
    ins, outs = refs[:n], refs[n:]
    for out, group in zip(outs, groups):
        for at, j in enumerate(group):
            total = ins[0][j].astype(f32)
            for other in ins[1:]:
                total = total + other[j].astype(f32)
            if len(out.shape) == len(ins[0].shape):
                out[at] = total.astype(out.dtype)
            else:
                out[...] = total.astype(out.dtype)


def sum_cut(ins, groups, name):
    shape = ins[0].shape[1:]
    outs = [
        jax.ShapeDtypeStruct(((len(g),) if len(g) > 1 else ()) + shape, bf16) for g in groups
    ]
    return pl.pallas_call(
        functools.partial(sum_cut_kernel, len(ins), groups),
        out_shape=outs,
        in_specs=[whole()] * len(ins),
        out_specs=[whole()] * len(outs),
        compiler_params=params(),
        cost_estimate=cost(len(ins) * ins[0].size, 2 * (len(ins) + 1) * ins[0].size),
        name=name,
    )(*ins)


def share_kernel(at, u0, u1, u2, u3, keep, send):
    c = at[1]
    total = u0[...].astype(f32) + u1[...].astype(f32) + u2[...].astype(f32) + u3[...].astype(f32)
    cols = keep.shape[1]
    keep[...] = total[:, :cols].astype(bf16)
    send[...] = total[:, cols:].astype(bf16)


def final_kernel(at, keep, got, h_ref, g_ref, k_mine, k_other, out, part):
    c = at[1]
    gain = g_ref[...].astype(f32)
    sums = None
    for place, u_ref, kappa in ((c, keep, k_mine), (1 - c, got, k_other)):
        u, h = u_ref[...].astype(f32), h_ref[place].astype(f32)
        out[place] = (gain * u - h * column(kappa[0:1, :])).astype(bf16)
        now = jnp.sum(u * h, axis=0, keepdims=True)
        sums = now if sums is None else sums + now
    loss = jnp.sum(k_mine[1:2, :] + k_other[1:2, :], axis=1, keepdims=True)
    part[...] = jnp.concatenate([sums, jnp.broadcast_to(loss, (1, 128))], axis=1)


def copy_for_each(value, axis):
    size = lax.axis_size(axis)
    return lax.all_to_all(
        jnp.broadcast_to(value[None], (size, *value.shape)), axis, 0, 0, tiled=True
    )


def body(hidden, gain, head, targets, lengths, old_logp, rewards, group_slot):
    resp_here, rows, cols = hidden.shape
    x, y, z, c = (lax.axis_index(a) for a in ("x", "y", "z", "c"))
    at = jnp.stack([y, c, z, x]).astype(jnp.int32)

    keep, give, sq_keep, sq_give = scale(at, hidden, gain)
    near = shift(give, "c", 1)
    sq = sq_keep + shift(sq_give, "c", 1)
    head_o = shift(head, "c", 1)

    k_prev, k_next = shift(keep, "y", 1), shift(keep, "y", -1)
    n_prev, n_next = shift(near, "y", 1), shift(near, "y", -1)
    k_far = shift(k_prev, "y", 1)
    n_far = shift(n_next, "y", -1)
    blocks = (keep, near, k_next, n_next, k_far, n_far, k_prev, n_prev)
    squares = (sq, shift(sq, "y", 1), shift(sq, "y", -1), shift(sq, "y", 2))

    groups_all = resp_here * lax.axis_size(DP) // GROUP
    group = group_slot // GROUP
    member = (group[:, None] == jnp.arange(groups_all, dtype=jnp.int32)[None, :]).astype(f32)
    local = jnp.concatenate(
        [jnp.sum(member * rewards[:, None], axis=0), jnp.sum(lengths).astype(f32)[None]]
    )
    sums = copy_for_each(local, DP).sum(axis=0)
    group_sums, count = sums[:groups_all], sums[groups_all]
    adv_resp = rewards - jnp.sum(member * group_sums[None, :], axis=1) / GROUP
    slots_all = resp_here * rows * lax.axis_size(DP)
    nums = jnp.stack(
        [
            jnp.where(c == 0, adv_resp[0], adv_resp[1]),
            jnp.where(c == 0, lengths[0], lengths[1]).astype(f32),
            slots_all / count,
            count,
        ]
    )

    logits, stats, inv = logits_of(at, blocks, squares, targets, head, head_o)
    all_stats = (stats, shift(stats, "y", 1), shift(stats, "y", -1), shift(stats, "y", 2))
    others = tuple(shift(b, "c", 1) for b in blocks)
    dl_a, dl_b, small, u0, u1, u2, u3 = grads_of(
        at, nums, all_stats, logits, inv, targets, old_logp, head, head_o, cols
    )
    small_o = shift(small, "c", 1)
    dl_o = shift(dl_b, "c", 1)

    part = cols // 4
    voc = dl_a.shape[1]
    zs = (4, 4, part, voc // 4)
    send_a, send_b, keep_a, keep_b = heads_of(
        at, blocks, others, dl_a, dl_o, heads_z_kernel, (zs,) * 4, "heads_z"
    )
    x0, x1, x2, x3 = heads_of(
        at, blocks, others, dl_a, dl_o, heads_x_kernel, ((8, part, voc // 2),) * 4, "heads_x"
    )
    got_a, got_b = turn(send_a, 1), turn(send_b, -1)
    x_in = (x0, shift(x1, "x", 1), shift(x2, "x", 2), shift(x3, "x", -1))

    u_in = (u0, shift(u1, "y", 1), shift(u2, "y", 2), shift(u3, "y", -1))

    keep2_a, send2_a = sum_cut((keep_a, got_a), ((3, 0), (2, 1)), "sum_z1a")
    keep2_b, send2_b = sum_cut((keep_b, got_b), ((3, 0), (2, 1)), "sum_z1b")
    got2_a, got2_b = turn(send2_a, -1), turn(send2_b, 1)
    send3_a, keep3_a = sum_cut((keep2_a, got2_a), ((0,), (1,)), "sum_z2a")
    send3_b, keep3_b = sum_cut((keep2_b, got2_b), ((0,), (1,)), "sum_z2b")
    got3_a, got3_b = turn(send3_a, 3), turn(send3_b, -3)
    za = sum_cut((keep3_a, got3_a), ((0,), (1,), (2,), (3,)), "sum_z3a")
    zb = sum_cut((keep3_b, got3_b), ((0,), (1,), (2,), (3,)), "sum_z3b")
    z_out = [
        sum(
            v.astype(f32)
            for v in (four[0], shift(four[1], "x", 1), shift(four[2], "x", 2), shift(four[3], "x", -1))
        )
        for four in (za, zb)
    ]

    eight = sum_cut(x_in, tuple((k,) for k in range(8)), "sum_x")
    x_out = sum(
        [eight[0].astype(f32)] + [shift(eight[k], "z", k).astype(f32) for k in range(1, 8)]
    )
    grad_head_t = jnp.concatenate([x_out] + z_out, axis=1)

    u_keep, u_send = pl.pallas_call(
        share_kernel,
        out_shape=[jax.ShapeDtypeStruct((rows, cols), bf16)] * 2,
        in_specs=[whole(pltpu.SMEM)] + [whole()] * 4,
        out_specs=[whole()] * 2,
        compiler_params=params(),
        cost_estimate=cost(4 * rows * cols * 2, 20 * rows * cols),
        name="share",
    )(at, *u_in)
    u_got = shift(u_send, "c", 1)
    grad_hidden, gain_part = pl.pallas_call(
        final_kernel,
        out_shape=[
            jax.ShapeDtypeStruct((resp_here, rows, cols), bf16),
            jax.ShapeDtypeStruct((1, cols + 128), f32),
        ],
        in_specs=[whole(pltpu.SMEM)] + [whole()] * 6,
        out_specs=[whole()] * 2,
        compiler_params=params(),
        cost_estimate=cost(8 * rows * cols * 2, 12 * rows * cols),
        name="final",
    )(at, u_keep, u_got, hidden, gain.reshape(1, cols), small, small_o)
    tail = copy_for_each(gain_part.reshape(-1, 128), DP).sum(axis=0).reshape(-1)
    return (tail[cols] / count, grad_hidden, tail[:cols], grad_head_t)


def solution(mesh):
    split = Mesh(mesh.devices.reshape(8, 4, 4, 2), ("z", "x", "y", "c"))
    return jax.shard_map(
        body,
        mesh=split,
        in_specs=(
            P(DP, None, FSDP),
            P(FSDP),
            P(FSDP, None),
            P(DP, None),
            P(DP),
            P(DP, None),
            P(DP),
            P(DP),
        ),
        out_specs=(P(), P(DP, None, FSDP), P(FSDP), P(DP, FSDP)),
        check_vma=False,
    )
```

```python
import functools

import jax
import jax.numpy as jnp
from jax import lax
from jax.experimental import pallas as pl
from jax.experimental.pallas import tpu as pltpu
from jax.sharding import Mesh
from jax.sharding import PartitionSpec as P

GROUP = 8
FSDP = ("y", "c")
DP = ("z", "x")
SIZES = {"z": 8, "x": 4, "y": 4, "c": 2}

eps_norm = 1e-06
clip_low = 0.8
clip_high = 1.2
dual_bound = 3.0

f32, bf16 = jnp.float32, jnp.bfloat16
VMEM = pltpu.VMEM


def shift(value, axis, step):
    n = SIZES[axis]
    return lax.ppermute(value, axis, [(i, (i + step) % n) for i in range(n)])


def turn(value, step):
    return lax.ppermute(
        value, "z", [(i, (i + (step if i % 2 == 0 else -step)) % 8) for i in range(8)]
    )


def params(limit=60 << 20):
    return pltpu.CompilerParams(vmem_limit_bytes=limit)


def cost(flops, nbytes, trans=0):
    return pl.CostEstimate(flops=flops, bytes_accessed=nbytes, transcendentals=trans)


def whole(space=None):
    return pl.BlockSpec(memory_space=space or VMEM)


def like(shape, kind=bf16):
    return jax.ShapeDtypeStruct(shape, kind)


def column(row):
    n = row.shape[1]
    return jnp.transpose(jnp.broadcast_to(row, (128, n)))[:, 0:1]


def rows_of(columns):
    n = columns[0].shape[0]
    lane = lax.broadcasted_iota(jnp.int32, (n, 128), 1)
    table = jnp.zeros((n, 128), f32)
    for k, col in enumerate(columns):
        table = jnp.where(lane == k, col, table)
    return jnp.transpose(table)[0:8, :]


def full(shape):
    return pl.BlockSpec(shape, lambda k, *at: (0,) * len(shape))


def logits_kernel(count, per, last, table, at, *refs):
    pieces = refs[: count * per]
    refs = refs[count * per :]
    if last:
        acc_in, sq_in, tgt = refs[:3]
        refs = refs[3:]
    head, hb = refs[:2]
    outs, (slot, acc, sq, sem) = refs[2:-4], refs[-4:]
    j = pl.program_id(0)
    rows = acc.shape[0]

    @pl.when(j == 0)
    def _():
        copies = []
        for k, piece in enumerate(pieces):
            first = 0 if k % per == 0 else pieces[k - 1].shape[0]
            copies.append(
                pltpu.make_async_copy(
                    piece, slot.at[k // per, pl.ds(first, piece.shape[0]), :], sem.at[k]
                )
            )
        for copy in copies:
            copy.start()
        if last:
            acc[...] = acc_in[...]
            sq[...] = column(sq_in[0:1, :])
        else:
            acc[...] = jnp.zeros_like(acc)
            sq[...] = jnp.zeros_like(sq)
        for copy in copies:
            copy.wait()

    gain = slot[j, 0:16, :][0:1, :].astype(f32)
    raw = slot[j, 16 : 16 + rows, :].astype(f32)
    sq[...] += jnp.sum(raw * raw, axis=1, keepdims=True)
    scaled = (raw * gain).astype(bf16)
    hb[0] = scaled
    acc[...] += lax.dot_general(
        scaled, head[...], (((1,), (1,)), ((), ())), preferred_element_type=f32
    )

    @pl.when(j == count - 1)
    def _():
        if not last:
            outs[0][...] = acc[...]
            outs[1][...] = rows_of([sq[...]])
            return
        lg, st, inv_ref = outs
        inv_c = lax.rsqrt(sq[...] / 5120.0 + eps_norm)
        inv_ref[...] = rows_of([inv_c])
        logits = acc[...] * inv_c
        lg[...] = logits
        half = logits.shape[1]
        entry = lax.broadcasted_iota(jnp.int32, logits.shape, 1) + at[0] * half
        target = column(tgt[...].astype(f32)).astype(jnp.int32)
        top = jnp.max(logits, axis=1, keepdims=True)
        power = jnp.exp(logits - top)
        found = rows_of(
            [
                top,
                jnp.sum(power, axis=1, keepdims=True),
                jnp.sum(power * logits, axis=1, keepdims=True),
                jnp.sum(jnp.where(entry == target, logits, 0.0), axis=1, keepdims=True),
            ]
        )
        for k in range(st.shape[0]):
            st[k] = found


def logits_of(table, at, blocks, head, before=None, targets=None):
    count, per = len(blocks), len(blocks[0])
    last = before is not None
    half = head.shape[0]
    cols = blocks[0][0].shape[1]
    height = sum(p.shape[0] for p in blocks[0])
    rows = height - 16
    anywhere = pl.BlockSpec(memory_space=pl.ANY)
    shapes = [like((count, rows, cols))]
    specs = [pl.BlockSpec((1, rows, cols), lambda j, *a: (j, 0, 0))]
    shapes += [like((rows, half), f32)]
    shapes += [like((8, 8, rows), f32)] if last else []
    shapes += [like((8, rows), f32)]
    extra = (*before, targets) if last else ()
    return pl.pallas_call(
        functools.partial(logits_kernel, count, per, last),
        out_shape=shapes,
        grid_spec=pltpu.PrefetchScalarGridSpec(
            num_scalar_prefetch=2,
            grid=(count,),
            in_specs=[anywhere] * (count * per)
            + [full(e.shape) for e in extra]
            + [pl.BlockSpec((half, cols), lambda j, table, at: (0, table[j]))],
            out_specs=specs + [full(s.shape) for s in shapes[1:]],
            scratch_shapes=[
                VMEM((count, height, cols), bf16),
                VMEM((rows, half), f32),
                VMEM((rows, 1), f32),
                pltpu.SemaphoreType.DMA((count * per,)),
            ],
        ),
        compiler_params=params(),
        cost_estimate=cost(2 * rows * half * count * cols, 2 * count * cols * (2 * rows + half)),
        name="logits_last" if last else "logits_first",
    )(table, at, *[p for b in blocks for p in b], *extra, head)


def turned_kernel(a, out):
    out[0] = jnp.transpose(a[0])


def turned(blocks):
    count, rows, cols = blocks.shape
    return pl.pallas_call(
        turned_kernel,
        out_shape=like((count, cols, rows)),
        grid=(count,),
        in_specs=[pl.BlockSpec((1, rows, cols), lambda j: (j, 0, 0))],
        out_specs=pl.BlockSpec((1, cols, rows), lambda j: (j, 0, 0)),
        compiler_params=params(),
        cost_estimate=cost(0, 4 * blocks.size),
        name="turned",
    )(blocks)


def policy_kernel(at, nums, st, lg, inv_ref, tgt, old, dl, small):
    half = lg.shape[1]
    rows = lg.shape[0]
    top = jnp.max(st[:, 0, :], axis=0, keepdims=True)
    weight = jnp.exp(st[:, 0, :] - top)
    total = jnp.sum(st[:, 1, :] * weight, axis=0, keepdims=True)
    moment = jnp.sum(st[:, 2, :] * weight, axis=0, keepdims=True)
    chosen = jnp.sum(st[:, 3, :], axis=0, keepdims=True)
    lse = top + jnp.log(total)
    inv = inv_ref[0:1, :]
    ratio = jnp.exp(chosen - lse - old[...])
    position = lax.broadcasted_iota(jnp.int32, ratio.shape, 1)
    second_one = position >= rows // 2
    adv = jnp.where(second_one, nums[1], nums[0])
    length = jnp.where(second_one, nums[3], nums[2])
    within = jnp.where(second_one, position - rows // 2, position).astype(f32)
    mask = jnp.where(within < length, 1.0, 0.0)
    first = ratio * adv
    second = jnp.clip(ratio, clip_low, clip_high) * adv
    policy = -jnp.minimum(first, second)
    policy = jnp.where(adv < 0, jnp.minimum(policy, -dual_bound * adv), policy)
    active = (first <= second) & jnp.logical_not((adv < 0) & (first < dual_bound * adv))
    grad_logp = nums[4] * mask * jnp.where(active, -first, 0.0)
    kappa = inv * inv * grad_logp * (chosen - moment / total) / 5120.0
    small[...] = jnp.concatenate(
        [kappa, mask * policy, jnp.zeros((6, ratio.shape[1]), f32)], axis=0
    )
    lse_c, scale_c = column(lse), column(grad_logp * inv)
    target = column(tgt[...].astype(f32)).astype(jnp.int32)
    entry = lax.broadcasted_iota(jnp.int32, lg.shape, 1) + at[0] * half
    hit = jnp.where(entry == target, 1.0, 0.0)
    dl[...] = (scale_c * (hit - jnp.exp(lg[...] - lse_c))).astype(bf16)


def policy_of(at, nums, stats, logits, inv, targets, old_logp):
    rows, half = logits.shape
    return pl.pallas_call(
        policy_kernel,
        out_shape=[like((rows, half)), like((8, rows), f32)],
        in_specs=[whole(pltpu.SMEM)] * 2 + [whole()] * 5,
        out_specs=[whole()] * 2,
        compiler_params=params(),
        cost_estimate=cost(8 * rows * half, 6 * rows * half, rows * half),
        name="policy",
    )(at, nums, stats, logits, inv, targets, old_logp)


def left_of(j, early, late):
    return jnp.where(j < 6, early[0], late[0])


def heads_x_kernel(table, at, early, late, dl, out):
    j = pl.program_id(0)
    got = jnp.dot(left_of(j, early, late), dl[...], preferred_element_type=f32).astype(bf16)
    step = got.shape[0] // 4
    for k in range(4):
        out[k, table[j]] = got[k * step : (k + 1) * step, :]


def heads_z_kernel(table, at, early, late, dl, send_a, send_b, keep_a, keep_b, tmp):
    j = pl.program_id(0)
    x, z = at[4], at[3]
    tmp[...] = jnp.dot(left_of(j, early, late), dl[...], preferred_element_type=f32)
    step = tmp.shape[0] // 4
    width = tmp.shape[1] // 2
    odd = lax.rem(z, 2)
    ahead = lax.rem(table[j] - z + 8, 8)
    behind = lax.rem(8 - ahead, 8)
    for side, send, keep in ((0, send_a, keep_a), (1, send_b, keep_b)):
        q = jnp.where(odd == side, ahead, behind)
        low = lax.rem(q, 4)
        sent = (low == 1) | (low == 2)
        send_at = jnp.where(sent, 2 * (q // 4) + low - 1, 0)
        keep_at = jnp.where(q == 0, 0, jnp.where(q == 7, 1, jnp.where(q == 4, 2, 3)))
        cut = slice(side * width, (side + 1) * width)

        @pl.when(sent)
        def _(send=send, cut=cut, send_at=send_at):
            for k in range(4):
                start = pl.multiple_of(lax.rem(x + k, 4) * step, step)
                send[send_at, k] = tmp[pl.ds(start, step), cut].astype(bf16)

        @pl.when(jnp.logical_not(sent))
        def _(keep=keep, cut=cut, keep_at=keep_at):
            for k in range(4):
                start = pl.multiple_of(lax.rem(x + k, 4) * step, step)
                keep[keep_at, k] = tmp[pl.ds(start, step), cut].astype(bf16)


def heads_of(table, at, early, late, dl, second, kernel, shapes, scratch, name):
    _, cols, rows = early.shape
    half = dl.shape[1] // 2
    return pl.pallas_call(
        kernel,
        out_shape=[like(s) for s in shapes],
        grid_spec=pltpu.PrefetchScalarGridSpec(
            num_scalar_prefetch=2,
            grid=(8,),
            in_specs=[
                pl.BlockSpec((1, cols, rows), lambda j, *a: (jnp.minimum(j, 5), 0, 0)),
                pl.BlockSpec((1, cols, rows), lambda j, *a: (jnp.maximum(j - 6, 0), 0, 0)),
                pl.BlockSpec((rows, half), lambda j, *a: (0, second)),
            ],
            out_specs=[full(s) for s in shapes],
            scratch_shapes=[VMEM((cols, half), f32)] if scratch else [],
        ),
        compiler_params=params(),
        cost_estimate=cost(2 * rows * 8 * cols * half, 16 * rows * cols + 16 * cols * half),
        name=name,
    )(table, at, early, late, dl)


def back_kernel(table, at, dl, head, send, keep):
    k = pl.program_id(0)
    part = jnp.dot(dl[...], head[...], preferred_element_type=f32).astype(bf16)

    @pl.when(k < 4)
    def _():
        send[0] = part

    @pl.when(k >= 4)
    def _():
        keep[0] = part


def back_of(table, at, dl, head, cols):
    rows, half = dl.shape
    return pl.pallas_call(
        back_kernel,
        out_shape=[like((4, rows, cols))] * 2,
        grid_spec=pltpu.PrefetchScalarGridSpec(
            num_scalar_prefetch=2,
            grid=(8,),
            in_specs=[
                full((rows, half)),
                pl.BlockSpec((half, cols), lambda k, table, at: (0, table[8 + k])),
            ],
            out_specs=[
                pl.BlockSpec((1, rows, cols), lambda k, *a: (jnp.minimum(k, 3), 0, 0)),
                pl.BlockSpec((1, rows, cols), lambda k, *a: (jnp.maximum(k - 4, 0), 0, 0)),
            ],
        ),
        compiler_params=params(),
        cost_estimate=cost(2 * rows * half * 8 * cols, 16 * half * cols + 16 * rows * cols),
        name="back",
    )(table, at, dl, head)


def sum_cut_kernel(n, groups, *refs):
    ins, outs = refs[:n], refs[n:]
    for out, group in zip(outs, groups):
        for at, j in enumerate(group):
            total = ins[0][j].astype(f32)
            for other in ins[1:]:
                total = total + other[j].astype(f32)
            if len(out.shape) == len(ins[0].shape):
                out[at] = total.astype(out.dtype)
            else:
                out[...] = total.astype(out.dtype)


def sum_cut(ins, groups, name):
    shape = ins[0].shape[1:]
    outs = [like(((len(g),) if len(g) > 1 else ()) + shape) for g in groups]
    return pl.pallas_call(
        functools.partial(sum_cut_kernel, len(ins), groups),
        out_shape=outs,
        in_specs=[whole()] * len(ins),
        out_specs=[whole()] * len(outs),
        compiler_params=params(),
        cost_estimate=cost(len(ins) * ins[0].size, 2 * (len(ins) + 1) * ins[0].size),
        name=name,
    )(*ins)


def sum_first_kernel(a, out):
    for k in range(out.shape[0]):
        total = a[0, k].astype(f32)
        for s in range(1, a.shape[0]):
            total = total + a[s, k].astype(f32)
        out[k] = total.astype(out.dtype)


def sum_first(value, name):
    return pl.pallas_call(
        sum_first_kernel,
        out_shape=like(value.shape[1:]),
        in_specs=[whole()],
        out_specs=whole(),
        compiler_params=params(),
        cost_estimate=cost(value.size, 3 * value.size),
        name=name,
    )(value)


def both_kernel(keep_a, got_a, keep_b, got_b, *outs):
    width = keep_a.shape[2]
    for k, out in enumerate(outs):
        for first, keep, got in ((0, keep_a, got_a), (width, keep_b, got_b)):
            total = keep[k].astype(f32) + got[k].astype(f32)
            out[:, first : first + width] = total.astype(bf16)


def join_kernel(from_z, s0, s1, s2, s3, out):
    width = s0.shape[1]
    total = from_z[0].astype(f32)
    for k in range(1, from_z.shape[0]):
        total = total + from_z[k].astype(f32)
    out[:, :width] = total
    out[:, width:] = (
        s0[...].astype(f32) + s1[...].astype(f32) + s2[...].astype(f32) + s3[...].astype(f32)
    )


def final_kernel(u0, u1, u2, u3, h_ref, g_ref, small, out, part):
    gain = g_ref[...].astype(f32)
    resp, rows, _ = h_ref.shape
    kappa = column(small[0:1, :])
    sums = None
    for r in range(resp):
        cut = slice(r * rows, (r + 1) * rows)
        u = sum(v[cut, :].astype(f32) for v in (u0, u1, u2, u3))
        h = h_ref[r].astype(f32)
        out[r] = (gain * u - h * kappa[cut, :]).astype(bf16)
        now = jnp.sum(u * h, axis=0, keepdims=True)
        sums = now if sums is None else sums + now
    loss = jnp.sum(small[1:2, :], axis=1, keepdims=True)
    part[...] = jnp.concatenate([sums, jnp.broadcast_to(loss, (1, 128))], axis=1)


def simple(kernel, shapes, ins, nbytes, name):
    return pl.pallas_call(
        kernel,
        out_shape=shapes,
        in_specs=[whole()] * len(ins),
        out_specs=[whole()] * len(shapes),
        compiler_params=params(),
        cost_estimate=cost(nbytes // 2, nbytes),
        name=name,
    )(*ins)


def copy_for_each(value, axis):
    size = lax.axis_size(axis)
    return lax.all_to_all(
        jnp.broadcast_to(value[None], (size, *value.shape)), axis, 0, 0, tiled=True
    )


def body(hidden, gain, head, targets, lengths, old_logp, rewards, group_slot):
    resp_here, length_max, cols = hidden.shape
    rows = resp_here * length_max
    x, y, z, c = (lax.axis_index(a) for a in ("x", "y", "z", "c"))
    order = jnp.array([0, 0, 3, 3, 1, 1, 2, 2, 0, 1, 2, 3, 0, 1, 2, 3], jnp.int32)
    other = jnp.array([0, 1] * 4 + [1] * 4 + [0] * 4, jnp.int32)
    table = (2 * ((y + order) % 4) + (c + other) % 2).astype(jnp.int32)
    at = jnp.stack([2 * y + c, y, c, z, x]).astype(jnp.int32)

    payload = jnp.concatenate(
        [jnp.broadcast_to(gain[None], (16, cols)), hidden.reshape(rows, cols)], axis=0
    )
    cut = 16 + length_max
    own_o = shift(payload, "c", 1)
    prev, following = shift(payload, "y", 1), shift(payload, "y", -1)
    far_a, far_b = shift(prev[:cut], "y", 1), shift(following[cut:], "y", -1)
    prev_o, following_o = shift(prev, "c", 1), shift(following, "c", 1)
    far_a_o, far_b_o = shift(far_a, "c", 1), shift(far_b, "c", 1)

    groups_all = resp_here * lax.axis_size(DP) // GROUP
    group = group_slot // GROUP
    member = (group[:, None] == jnp.arange(groups_all, dtype=jnp.int32)[None, :]).astype(f32)
    local = jnp.concatenate(
        [jnp.sum(member * rewards[:, None], axis=0), jnp.sum(lengths).astype(f32)[None]]
    )
    sums = copy_for_each(local, DP).sum(axis=0)
    group_sums, count = sums[:groups_all], sums[groups_all]
    adv_resp = rewards - jnp.sum(member * group_sums[None, :], axis=1) / GROUP
    slots_all = rows * lax.axis_size(DP)
    nums = jnp.concatenate([adv_resp, lengths.astype(f32), (slots_all / count)[None]])
    targets = targets.reshape(1, rows)
    old_logp = old_logp.reshape(1, rows)

    hb_early, acc, sq = logits_of(
        table, at, [(payload,), (own_o,), (prev,), (prev_o,), (following,), (following_o,)], head
    )
    early = turned(hb_early)
    hb_late, logits, stats, inv = logits_of(
        table[6:], at, [(far_a, far_b), (far_a_o, far_b_o)], head, (acc, sq), targets
    )
    all_stats = lax.all_to_all(stats, FSDP, 0, 0, tiled=True)
    late = turned(hb_late)
    dl, small = policy_of(at, nums, all_stats, logits, inv, targets, old_logp)

    part, half = cols // 4, dl.shape[1] // 2
    zs = (4, 4, part, half // 2)
    send_a, send_b, keep_a, keep_b = heads_of(
        table, at, early, late, dl, 1, heads_z_kernel, (zs,) * 4, True, "heads_z"
    )
    (to_x,) = heads_of(
        table, at, early, late, dl, 0, heads_x_kernel, ((4, 8, part, half),), False, "heads_x"
    )
    u_send, u_keep = back_of(table, at, dl, head, cols)
    got_a, got_b = turn(send_a, 1), turn(send_b, -1)
    from_x = lax.all_to_all(to_x, "x", 0, 0, tiled=True)
    u_got = shift(u_send, "c", 1)

    send2_a, keep2_a = sum_cut((keep_a, got_a), ((2, 1), (3, 0)), "sum_z1a")
    send2_b, keep2_b = sum_cut((keep_b, got_b), ((2, 1), (3, 0)), "sum_z1b")
    got2_a, got2_b = turn(send2_a, -1), turn(send2_b, 1)
    send3_a, keep3_a = sum_cut((keep2_a, got2_a), ((0,), (1,)), "sum_z2a")
    send3_b, keep3_b = sum_cut((keep2_b, got2_b), ((0,), (1,)), "sum_z2b")
    got3_a, got3_b = turn(send3_a, 3), turn(send3_b, -3)
    four = simple(
        both_kernel,
        [like((part, half))] * 4,
        (keep3_a, got3_a, keep3_b, got3_b),
        12 * keep3_a.size,
        "sum_z3",
    )
    z_parts = (four[0], shift(four[1], "x", 1), shift(four[2], "x", 2), shift(four[3], "x", -1))

    to_z = sum_first(from_x, "sum_x")
    from_z = lax.all_to_all(to_z, "z", 0, 0, tiled=True)
    (grad_head_t,) = simple(
        join_kernel,
        [like((part, 2 * half), f32)],
        (from_z, *z_parts),
        2 * from_z.size + 16 * part * half,
        "join",
    )

    u0, u1, u2, u3 = sum_cut((u_keep, u_got), ((0,), (1,), (2,), (3,)), "sum_u")
    u_all = (u0, shift(u1, "y", 1), shift(u2, "y", 2), shift(u3, "y", -1))
    grad_hidden, gain_part = simple(
        final_kernel,
        [like(hidden.shape), like((1, cols + 128), f32)],
        (*u_all, hidden, gain.reshape(1, cols), small),
        12 * rows * cols,
        "final",
    )
    tail = gain_part.reshape(-1, 128)
    tail = tail + shift(tail, "x", 1) + shift(tail, "x", 2) + shift(tail, "x", -1)
    for step in (1, -1, 3):
        tail = tail + turn(tail, step)
    tail = tail.reshape(-1)
    return (tail[cols] / count, grad_hidden, tail[:cols], grad_head_t)


def solution(mesh):
    split = Mesh(mesh.devices.reshape(8, 4, 4, 2), ("z", "x", "y", "c"))
    return jax.shard_map(
        body,
        mesh=split,
        in_specs=(
            P(DP, None, FSDP),
            P(FSDP),
            P(FSDP, None),
            P(DP, None),
            P(DP),
            P(DP, None),
            P(DP),
            P(DP),
        ),
        out_specs=(P(), P(DP, None, FSDP), P(FSDP), P(DP, FSDP)),
        check_vma=False,
    )
```

```python
import functools

import jax
import jax.numpy as jnp
from jax import lax
from jax.experimental import pallas as pl
from jax.experimental.pallas import tpu as pltpu
from jax.sharding import Mesh
from jax.sharding import PartitionSpec as P

GROUP = 8
FSDP = ("y", "c")
DP = ("z", "x")
SIZES = {"z": 8, "x": 4, "y": 4, "c": 2}

eps_norm = 1e-06
clip_low = 0.8
clip_high = 1.2
dual_bound = 3.0

f32, bf16 = jnp.float32, jnp.bfloat16
VMEM = pltpu.VMEM


def shift(value, axis, step):
    n = SIZES[axis]
    return lax.ppermute(value, axis, [(i, (i + step) % n) for i in range(n)])


def turn(value, step):
    return lax.ppermute(
        value, "z", [(i, (i + (step if i % 2 == 0 else -step)) % 8) for i in range(8)]
    )


def params(limit=60 << 20):
    return pltpu.CompilerParams(vmem_limit_bytes=limit)


def cost(flops, nbytes, trans=0):
    return pl.CostEstimate(flops=flops, bytes_accessed=nbytes, transcendentals=trans)


def whole(space=None):
    return pl.BlockSpec(memory_space=space or VMEM)


def like(shape, kind=bf16):
    return jax.ShapeDtypeStruct(shape, kind)


def column(row):
    n = row.shape[1]
    return jnp.transpose(jnp.broadcast_to(row, (128, n)))[:, 0:1]


def rows_of(columns):
    n = columns[0].shape[0]
    lane = lax.broadcasted_iota(jnp.int32, (n, 128), 1)
    table = jnp.zeros((n, 128), f32)
    for k, col in enumerate(columns):
        table = jnp.where(lane == k, col, table)
    return jnp.transpose(table)[0:8, :]


def full(shape):
    return pl.BlockSpec(shape, lambda k, *at: (0,) * len(shape))


def logits_kernel(count, per, last, at, *refs):
    pieces = refs[: count * per * 2]
    refs = refs[count * per * 2 :]
    if last:
        acc_in, sq_in, tgt = refs[:3]
        refs = refs[3:]
    head, hb = refs[:2]
    outs, (slot, acc, sq, sem) = refs[2:-4], refs[-4:]
    j = pl.program_id(0)
    rows = acc.shape[0]
    cols = slot.shape[2] // 2

    @pl.when(j == 0)
    def _():
        copies = []
        for k, piece in enumerate(pieces):
            first = 0 if k % per == 0 else pieces[k - 1].shape[0]
            side = lax.rem(at[2] + (k // per) % 2, 2)
            lanes = pl.ds(pl.multiple_of(side * cols, cols), cols)
            place = slot.at[k // (2 * per), pl.ds(first, piece.shape[0]), lanes]
            copies.append(pltpu.make_async_copy(piece, place, sem.at[k]))
        for copy in copies:
            copy.start()
        if last:
            acc[...] = acc_in[...]
            sq[...] = column(sq_in[0:1, :])
        else:
            acc[...] = jnp.zeros_like(acc)
            sq[...] = jnp.zeros_like(sq)
        for copy in copies:
            copy.wait()

    gain = slot[j, 0:16, :][0:1, :].astype(f32)
    raw = slot[j, 16 : 16 + rows, :].astype(f32)
    sq[...] += jnp.sum(raw * raw, axis=1, keepdims=True)
    scaled = (raw * gain).astype(bf16)
    hb[0] = scaled
    acc[...] += lax.dot_general(
        scaled, head[...], (((1,), (1,)), ((), ())), preferred_element_type=f32
    )

    @pl.when(j == count - 1)
    def _():
        if not last:
            outs[0][...] = acc[...]
            outs[1][...] = rows_of([sq[...]])
            return
        lg, st, inv_ref = outs
        inv_c = lax.rsqrt(sq[...] / 5120.0 + eps_norm)
        inv_ref[...] = rows_of([inv_c])
        logits = acc[...] * inv_c
        lg[...] = logits
        half = logits.shape[1]
        entry = lax.broadcasted_iota(jnp.int32, logits.shape, 1) + at[0] * half
        target = column(tgt[...].astype(f32)).astype(jnp.int32)
        top = jnp.max(logits, axis=1, keepdims=True)
        power = jnp.exp(logits - top)
        found = rows_of(
            [
                top,
                jnp.sum(power, axis=1, keepdims=True),
                jnp.sum(power * logits, axis=1, keepdims=True),
                jnp.sum(jnp.where(entry == target, logits, 0.0), axis=1, keepdims=True),
            ]
        )
        for k in range(st.shape[0]):
            st[k] = found


def logits_of(at, first, blocks, head, before=None, targets=None):
    count, per = len(blocks), len(blocks[0]) // 2
    last = before is not None
    half = head.shape[0]
    cols = 2 * blocks[0][0].shape[1]
    height = sum(p.shape[0] for p in blocks[0]) // 2
    rows = height - 16
    anywhere = pl.BlockSpec(memory_space=pl.ANY)
    shapes = [like((count, rows, cols))]
    specs = [pl.BlockSpec((1, rows, cols), lambda j, *a: (j, 0, 0))]
    shapes += [like((rows, half), f32)]
    shapes += [like((8, 8, rows), f32)] if last else []
    shapes += [like((8, rows), f32)]
    extra = (*before, targets) if last else ()
    return pl.pallas_call(
        functools.partial(logits_kernel, count, per, last),
        out_shape=shapes,
        grid_spec=pltpu.PrefetchScalarGridSpec(
            num_scalar_prefetch=1,
            grid=(count,),
            in_specs=[anywhere] * (count * per * 2)
            + [full(e.shape) for e in extra]
            + [pl.BlockSpec((half, cols), lambda j, at: (0, at[8 + first + j]))],
            out_specs=specs + [full(s.shape) for s in shapes[1:]],
            scratch_shapes=[
                VMEM((count, height, cols), bf16),
                VMEM((rows, half), f32),
                VMEM((rows, 1), f32),
                pltpu.SemaphoreType.DMA((count * per * 2,)),
            ],
        ),
        compiler_params=params(),
        cost_estimate=cost(2 * rows * half * count * cols, 2 * count * cols * (2 * rows + half)),
        name="logits_last" if last else "logits_first",
    )(at, *[p for b in blocks for p in b], *extra, head)


def policy_kernel(at, nums, st, lg, inv_ref, tgt, old, dl, small):
    half = lg.shape[1]
    rows = lg.shape[0]
    top = jnp.max(st[:, 0, :], axis=0, keepdims=True)
    weight = jnp.exp(st[:, 0, :] - top)
    total = jnp.sum(st[:, 1, :] * weight, axis=0, keepdims=True)
    moment = jnp.sum(st[:, 2, :] * weight, axis=0, keepdims=True)
    chosen = jnp.sum(st[:, 3, :], axis=0, keepdims=True)
    lse = top + jnp.log(total)
    inv = inv_ref[0:1, :]
    ratio = jnp.exp(chosen - lse - old[...])
    position = lax.broadcasted_iota(jnp.int32, ratio.shape, 1)
    second_one = position >= rows // 2
    adv = jnp.where(second_one, nums[1], nums[0])
    length = jnp.where(second_one, nums[3], nums[2])
    within = jnp.where(second_one, position - rows // 2, position).astype(f32)
    mask = jnp.where(within < length, 1.0, 0.0)
    first = ratio * adv
    second = jnp.clip(ratio, clip_low, clip_high) * adv
    policy = -jnp.minimum(first, second)
    policy = jnp.where(adv < 0, jnp.minimum(policy, -dual_bound * adv), policy)
    active = (first <= second) & jnp.logical_not((adv < 0) & (first < dual_bound * adv))
    grad_logp = nums[4] * mask * jnp.where(active, -first, 0.0)
    kappa = inv * inv * grad_logp * (chosen - moment / total) / 5120.0
    small[...] = jnp.concatenate(
        [kappa, mask * policy, jnp.zeros((6, ratio.shape[1]), f32)], axis=0
    )
    lse_c, scale_c = column(lse), column(grad_logp * inv)
    target = column(tgt[...].astype(f32)).astype(jnp.int32)
    entry = lax.broadcasted_iota(jnp.int32, lg.shape, 1) + at[0] * half
    hit = jnp.where(entry == target, 1.0, 0.0)
    dl[...] = (scale_c * (hit - jnp.exp(lg[...] - lse_c))).astype(bf16)


def policy_of(at, nums, stats, logits, inv, targets, old_logp):
    rows, half = logits.shape
    return pl.pallas_call(
        policy_kernel,
        out_shape=[like((rows, half)), like((8, rows), f32)],
        in_specs=[whole(pltpu.SMEM)] * 2 + [whole()] * 5,
        out_specs=[whole()] * 2,
        compiler_params=params(),
        cost_estimate=cost(8 * rows * half, 6 * rows * half, rows * half),
        name="policy",
    )(at, nums, stats, logits, inv, targets, old_logp)


def products_kernel(at, early, late, dl, head, to_x, send_a, send_b, keep_a, keep_b, u_send, u_keep):
    j = pl.program_id(0)
    c, z = at[2], at[3]
    scaled = jnp.where(j < 3, early[0], late[0])
    cols = scaled.shape[1] // 2
    step, half = cols // 4, dl.shape[1] // 2
    width = half // 2
    back = jnp.dot(dl[...], head[...], preferred_element_type=f32).astype(bf16)

    @pl.when(c == 0)
    def _():
        u_keep[0] = back[:, :cols]
        u_send[0] = back[:, cols:]

    @pl.when(c == 1)
    def _():
        u_send[0] = back[:, :cols]
        u_keep[0] = back[:, cols:]

    got = lax.dot_general(
        scaled, dl[...], (((0,), (0,)), ((), ())), preferred_element_type=f32
    ).astype(bf16)
    odd = lax.rem(z, 2)
    for i in range(2):
        place = 2 * at[8 + j] + i
        ahead = lax.rem(place - z + 8, 8)
        behind = lax.rem(8 - ahead, 8)
        parts = [got[i * cols + k * step : i * cols + (k + 1) * step, :] for k in range(4)]
        for k in range(4):
            to_x[k, place] = parts[k][:, :half]
        for side, send, keep in ((0, send_a, keep_a), (1, send_b, keep_b)):
            q = jnp.where(odd == side, ahead, behind)
            low = lax.rem(q, 4)
            sent = (low == 1) | (low == 2)
            send_at = jnp.where(sent, 2 * (q // 4) + low - 1, 0)
            keep_at = jnp.where(q == 0, 0, jnp.where(q == 7, 1, jnp.where(q == 4, 2, 3)))
            cut = slice(half + side * width, half + (side + 1) * width)

            @pl.when(sent)
            def _(send=send, cut=cut, send_at=send_at, parts=parts):
                for k in range(4):
                    send[send_at, k] = parts[k][:, cut]

            @pl.when(jnp.logical_not(sent))
            def _(keep=keep, cut=cut, keep_at=keep_at, parts=parts):
                for k in range(4):
                    keep[keep_at, k] = parts[k][:, cut]


def products_of(at, early, late, dl, head):
    _, rows, cols = early.shape
    half = dl.shape[1]
    step = cols // 8
    cut = like((4, 4, step, half // 4))
    shapes = [like((4, 8, step, half // 2))] + [cut] * 4 + [like((4, rows, cols // 2))] * 2
    return pl.pallas_call(
        products_kernel,
        out_shape=shapes,
        grid_spec=pltpu.PrefetchScalarGridSpec(
            num_scalar_prefetch=1,
            grid=(4,),
            in_specs=[
                pl.BlockSpec((1, rows, cols), lambda j, at: (jnp.minimum(j, 2), 0, 0)),
                full(late.shape),
                full((rows, half)),
                pl.BlockSpec((half, cols), lambda j, at: (0, at[8 + j])),
            ],
            out_specs=[full(s.shape) for s in shapes[:5]]
            + [pl.BlockSpec((1, rows, cols // 2), lambda j, at: (j, 0, 0))] * 2,
        ),
        compiler_params=params(),
        cost_estimate=cost(4 * rows * 4 * cols * half, 32 * rows * cols),
        name="products",
    )(at, early, late, dl, head)


def sum_cut_kernel(n, groups, *refs):
    ins, outs = refs[:n], refs[n:]
    for out, group in zip(outs, groups):
        for at, j in enumerate(group):
            total = ins[0][j].astype(f32)
            for other in ins[1:]:
                total = total + other[j].astype(f32)
            if len(out.shape) == len(ins[0].shape):
                out[at] = total.astype(out.dtype)
            else:
                out[...] = total.astype(out.dtype)


def sum_cut(ins, groups, name):
    shape = ins[0].shape[1:]
    outs = [like(((len(g),) if len(g) > 1 else ()) + shape) for g in groups]
    return pl.pallas_call(
        functools.partial(sum_cut_kernel, len(ins), groups),
        out_shape=outs,
        in_specs=[whole()] * len(ins),
        out_specs=[whole()] * len(outs),
        compiler_params=params(),
        cost_estimate=cost(len(ins) * ins[0].size, 2 * (len(ins) + 1) * ins[0].size),
        name=name,
    )(*ins)


def sum_first_kernel(a, out):
    for k in range(out.shape[0]):
        total = a[0, k].astype(f32)
        for s in range(1, a.shape[0]):
            total = total + a[s, k].astype(f32)
        out[k] = total.astype(out.dtype)


def sum_first(value, name):
    return pl.pallas_call(
        sum_first_kernel,
        out_shape=like(value.shape[1:]),
        in_specs=[whole()],
        out_specs=whole(),
        compiler_params=params(),
        cost_estimate=cost(value.size, 3 * value.size),
        name=name,
    )(value)


def both_kernel(at, keep_a, got_a, keep_b, got_b, *outs):
    width = keep_a.shape[2]
    for k, out in enumerate(outs):
        place = lax.rem(at[4] + k, 4)
        for first, keep, got in ((0, keep_a, got_a), (width, keep_b, got_b)):
            total = keep[place].astype(f32) + got[place].astype(f32)
            out[:, first : first + width] = total.astype(bf16)


def join_kernel(from_z, s0, s1, s2, s3, out):
    width = s0.shape[1]
    total = from_z[0].astype(f32)
    for k in range(1, from_z.shape[0]):
        total = total + from_z[k].astype(f32)
    out[:, :width] = total
    out[:, width:] = (
        s0[...].astype(f32) + s1[...].astype(f32) + s2[...].astype(f32) + s3[...].astype(f32)
    )


def final_kernel(u0, u1, u2, u3, h_ref, g_ref, small, out, part):
    gain = g_ref[...].astype(f32)
    resp, rows, _ = h_ref.shape
    kappa = column(small[0:1, :])
    sums = None
    for r in range(resp):
        cut = slice(r * rows, (r + 1) * rows)
        u = sum(v[cut, :].astype(f32) for v in (u0, u1, u2, u3))
        h = h_ref[r].astype(f32)
        out[r] = (gain * u - h * kappa[cut, :]).astype(bf16)
        now = jnp.sum(u * h, axis=0, keepdims=True)
        sums = now if sums is None else sums + now
    loss = jnp.sum(small[1:2, :], axis=1, keepdims=True)
    part[...] = jnp.concatenate([sums, jnp.broadcast_to(loss, (1, 128))], axis=1)


def simple(kernel, shapes, ins, nbytes, name):
    return pl.pallas_call(
        kernel,
        out_shape=shapes,
        in_specs=[whole(pltpu.SMEM if v.ndim == 1 else VMEM) for v in ins],
        out_specs=[whole()] * len(shapes),
        compiler_params=params(),
        cost_estimate=cost(nbytes // 2, nbytes),
        name=name,
    )(*ins)


def copy_for_each(value, axis):
    size = lax.axis_size(axis)
    return lax.all_to_all(
        jnp.broadcast_to(value[None], (size, *value.shape)), axis, 0, 0, tiled=True
    )


def after(value, *first):
    return lax.optimization_barrier((value, *first))[0]


def body(hidden, gain, head, targets, lengths, old_logp, rewards, group_slot):
    resp_here, length_max, cols = hidden.shape
    rows = resp_here * length_max
    x, y, z, c = (lax.axis_index(a) for a in ("x", "y", "z", "c"))
    chips = (y + jnp.array([0, 3, 1, 2], jnp.int32)) % 4
    at = jnp.concatenate([jnp.stack([2 * y + c, y, c, z, x, x, x, x]), chips]).astype(jnp.int32)

    payload = jnp.concatenate(
        [jnp.broadcast_to(gain[None], (16, cols)), hidden.reshape(rows, cols)], axis=0
    )
    cut = 16 + length_max
    prev, following = shift(payload, "y", 1), shift(payload, "y", -1)
    own_o = shift(payload, "c", 1)

    groups_all = resp_here * lax.axis_size(DP) // GROUP
    group = group_slot // GROUP
    member = (group[:, None] == jnp.arange(groups_all, dtype=jnp.int32)[None, :]).astype(f32)
    local = jnp.concatenate(
        [jnp.sum(member * rewards[:, None], axis=0), jnp.sum(lengths).astype(f32)[None]]
    )
    over_x = copy_for_each(local, "x").sum(axis=0)
    prev, following, over_x = lax.optimization_barrier((prev, following, over_x))

    far_a, far_b = shift(prev[:cut], "y", 1), shift(following[cut:], "y", -1)
    prev_o, following_o = shift(prev, "c", 1), shift(following, "c", 1)
    sums = copy_for_each(over_x, "z").sum(axis=0)
    group_sums, count = sums[:groups_all], sums[groups_all]
    adv_resp = rewards - jnp.sum(member * group_sums[None, :], axis=1) / GROUP
    slots_all = rows * lax.axis_size(DP)
    nums = jnp.concatenate([adv_resp, lengths.astype(f32), (slots_all / count)[None]])
    targets = targets.reshape(1, rows)
    old_logp = old_logp.reshape(1, rows)

    early, acc, sq = logits_of(
        at, 0, [(payload, own_o), (prev, prev_o), (following, following_o)], head
    )
    far_a_o, far_b_o = shift(far_a, "c", 1), shift(far_b, "c", 1)
    acc, nums, far_a_o = lax.optimization_barrier((acc, nums, far_a_o))
    late, logits, stats, inv = logits_of(
        at, 3, [(far_a, far_b, far_a_o, far_b_o)], head, (acc, sq), targets
    )
    all_stats = lax.all_to_all(stats, FSDP, 0, 0, tiled=True)
    dl, small = policy_of(at, nums, all_stats, logits, inv, targets, old_logp)
    to_x, send_a, send_b, keep_a, keep_b, u_send, u_keep = products_of(at, early, late, dl, head)
    part, half = cols // 4, dl.shape[1] // 2

    u_got = shift(u_send, "c", 1)
    got_a, got_b = turn(send_a, 1), turn(send_b, -1)
    from_x = lax.all_to_all(to_x, "x", 0, 0, tiled=True)
    u0, u1, u2, u3 = sum_cut((u_keep, u_got), ((0,), (1,), (2,), (3,)), "sum_u")
    u1, u2, u3 = shift(u1, "y", -1), shift(u2, "y", 1), shift(u3, "y", 2)

    got_a = after(got_a, u0)
    send2_a, keep2_a = sum_cut((keep_a, got_a), ((2, 1), (3, 0)), "sum_z1a")
    send2_b, keep2_b = sum_cut((keep_b, got_b), ((2, 1), (3, 0)), "sum_z1b")
    got2_a, got2_b = turn(send2_a, -1), turn(send2_b, 1)
    from_x = after(from_x, send2_a, send2_b)
    to_z = sum_first(from_x, "sum_x")
    from_z = lax.all_to_all(to_z, "z", 0, 0, tiled=True)

    got2_a, got2_b = after(got2_a, to_z), after(got2_b, to_z)
    send3_a, keep3_a = sum_cut((keep2_a, got2_a), ((0,), (1,)), "sum_z2a")
    send3_b, keep3_b = sum_cut((keep2_b, got2_b), ((0,), (1,)), "sum_z2b")
    got3_a, got3_b = turn(send3_a, 3), turn(send3_b, -3)

    u1 = after(u1, send3_a, send3_b)
    grad_hidden, gain_part = simple(
        final_kernel,
        [like(hidden.shape), like((1, cols + 128), f32)],
        (u0, u1, u2, u3, hidden, gain.reshape(1, cols), small),
        12 * rows * cols,
        "final",
    )
    tail = gain_part.reshape(-1, 128)
    tail = tail + shift(tail, "x", 1) + shift(tail, "x", 2) + shift(tail, "x", -1)

    got3_a = after(got3_a, gain_part)
    four = simple(
        both_kernel,
        [like((part, half))] * 4,
        (at, keep3_a, got3_a, keep3_b, got3_b),
        12 * keep3_a.size,
        "sum_z3",
    )
    z_parts = (four[0], shift(four[1], "x", 1), shift(four[2], "x", 2), shift(four[3], "x", -1))
    for step in (1, -1, 3):
        tail = tail + turn(tail, step)
    (grad_head_t,) = simple(
        join_kernel,
        [like((part, 2 * half), f32)],
        (from_z, *z_parts),
        2 * from_z.size + 16 * part * half,
        "join",
    )
    tail = tail.reshape(-1)
    return (tail[cols] / count, grad_hidden, tail[:cols], grad_head_t)


def solution(mesh):
    split = Mesh(mesh.devices.reshape(8, 4, 4, 2), ("z", "x", "y", "c"))
    return jax.shard_map(
        body,
        mesh=split,
        in_specs=(
            P(DP, None, FSDP),
            P(FSDP),
            P(FSDP, None),
            P(DP, None),
            P(DP),
            P(DP, None),
            P(DP),
            P(DP),
        ),
        out_specs=(P(), P(DP, None, FSDP), P(FSDP), P(DP, FSDP)),
        check_vma=False,
    )
```

```python
import functools

import jax
import jax.numpy as jnp
from jax import lax
from jax.experimental import pallas as pl
from jax.experimental.pallas import tpu as pltpu
from jax.sharding import Mesh
from jax.sharding import PartitionSpec as P

GROUP = 8
FSDP = ("y", "c")
DP = ("z", "x")
SIZES = {"z": 8, "x": 4, "y": 4, "c": 2}

eps_norm = 1e-06
clip_low = 0.8
clip_high = 1.2
dual_bound = 3.0

f32, bf16 = jnp.float32, jnp.bfloat16
VMEM = pltpu.VMEM


def shift(value, axis, step):
    n = SIZES[axis]
    return lax.ppermute(value, axis, [(i, (i + step) % n) for i in range(n)])


def turn(value, step):
    return lax.ppermute(
        value, "z", [(i, (i + (step if i % 2 == 0 else -step)) % 8) for i in range(8)]
    )


def params(limit=60 << 20):
    return pltpu.CompilerParams(vmem_limit_bytes=limit)


def cost(flops, nbytes, trans=0):
    return pl.CostEstimate(flops=flops, bytes_accessed=nbytes, transcendentals=trans)


def whole(space=None):
    return pl.BlockSpec(memory_space=space or VMEM)


def like(shape, kind=bf16):
    return jax.ShapeDtypeStruct(shape, kind)


def column(row):
    n = row.shape[1]
    return jnp.transpose(jnp.broadcast_to(row, (128, n)))[:, 0:1]


def rows_of(columns):
    n = columns[0].shape[0]
    lane = lax.broadcasted_iota(jnp.int32, (n, 128), 1)
    table = jnp.zeros((n, 128), f32)
    for k, col in enumerate(columns):
        table = jnp.where(lane == k, col, table)
    return jnp.transpose(table)[0:8, :]


def full(shape):
    return pl.BlockSpec(shape, lambda k, *at: (0,) * len(shape))


def logits_kernel(count, per, last, at, *refs):
    pieces = refs[: count * per * 2]
    refs = refs[count * per * 2 :]
    if last:
        acc_in, sq_in, tgt = refs[:3]
        refs = refs[3:]
    head, hb = refs[:2]
    outs, (slot, acc, sq, sem) = refs[2:-4], refs[-4:]
    j = pl.program_id(0)
    rows = acc.shape[0]
    cols = slot.shape[2] // 2

    @pl.when(j == 0)
    def _():
        copies = []
        for k, piece in enumerate(pieces):
            first = 0 if k % per == 0 else pieces[k - 1].shape[0]
            side = lax.rem(at[2] + (k // per) % 2, 2)
            lanes = pl.ds(pl.multiple_of(side * cols, cols), cols)
            place = slot.at[k // (2 * per), pl.ds(first, piece.shape[0]), lanes]
            copies.append(pltpu.make_async_copy(piece, place, sem.at[k]))
        for copy in copies:
            copy.start()
        if last:
            acc[...] = acc_in[...]
            sq[...] = column(sq_in[0:1, :])
        else:
            acc[...] = jnp.zeros_like(acc)
            sq[...] = jnp.zeros_like(sq)
        for copy in copies:
            copy.wait()

    gain = slot[j, 0:16, :][0:1, :].astype(f32)
    raw = slot[j, 16 : 16 + rows, :].astype(f32)
    sq[...] += jnp.sum(raw * raw, axis=1, keepdims=True)
    scaled = (raw * gain).astype(bf16)
    hb[0] = scaled
    acc[...] += lax.dot_general(
        scaled, head[...], (((1,), (1,)), ((), ())), preferred_element_type=f32
    )

    @pl.when(j == count - 1)
    def _():
        if not last:
            outs[0][...] = acc[...]
            outs[1][...] = rows_of([sq[...]])
            return
        lg, st, inv_ref = outs
        inv_c = lax.rsqrt(sq[...] / 5120.0 + eps_norm)
        inv_ref[...] = rows_of([inv_c])
        logits = acc[...] * inv_c
        lg[...] = logits
        half = logits.shape[1]
        entry = lax.broadcasted_iota(jnp.int32, logits.shape, 1) + at[0] * half
        target = column(tgt[...].astype(f32)).astype(jnp.int32)
        top = jnp.max(logits, axis=1, keepdims=True)
        power = jnp.exp(logits - top)
        found = rows_of(
            [
                top,
                jnp.sum(power, axis=1, keepdims=True),
                jnp.sum(power * logits, axis=1, keepdims=True),
                jnp.sum(jnp.where(entry == target, logits, 0.0), axis=1, keepdims=True),
            ]
        )
        for k in range(st.shape[0]):
            st[k] = found


def logits_of(at, first, blocks, head, before=None, targets=None):
    count, per = len(blocks), len(blocks[0]) // 2
    last = before is not None
    half = head.shape[0]
    cols = 2 * blocks[0][0].shape[1]
    height = sum(p.shape[0] for p in blocks[0]) // 2
    rows = height - 16
    anywhere = pl.BlockSpec(memory_space=pl.ANY)
    shapes = [like((count, rows, cols))]
    specs = [pl.BlockSpec((1, rows, cols), lambda j, *a: (j, 0, 0))]
    shapes += [like((rows, half), f32)]
    shapes += [like((8, 8, rows), f32)] if last else []
    shapes += [like((8, rows), f32)]
    extra = (*before, targets) if last else ()
    return pl.pallas_call(
        functools.partial(logits_kernel, count, per, last),
        out_shape=shapes,
        grid_spec=pltpu.PrefetchScalarGridSpec(
            num_scalar_prefetch=1,
            grid=(count,),
            in_specs=[anywhere] * (count * per * 2)
            + [full(e.shape) for e in extra]
            + [pl.BlockSpec((half, cols), lambda j, at: (0, at[8 + first + j]))],
            out_specs=specs + [full(s.shape) for s in shapes[1:]],
            scratch_shapes=[
                VMEM((count, height, cols), bf16),
                VMEM((rows, half), f32),
                VMEM((rows, 1), f32),
                pltpu.SemaphoreType.DMA((count * per * 2,)),
            ],
        ),
        compiler_params=params(),
        cost_estimate=cost(2 * rows * half * count * cols, 2 * count * cols * (2 * rows + half)),
        name="logits_last" if last else "logits_first",
    )(at, *[p for b in blocks for p in b], *extra, head)


def policy_kernel(at, nums, st, lg, inv_ref, tgt, old, dl, small):
    half = lg.shape[1]
    rows = lg.shape[0]
    top = jnp.max(st[:, 0, :], axis=0, keepdims=True)
    weight = jnp.exp(st[:, 0, :] - top)
    total = jnp.sum(st[:, 1, :] * weight, axis=0, keepdims=True)
    moment = jnp.sum(st[:, 2, :] * weight, axis=0, keepdims=True)
    chosen = jnp.sum(st[:, 3, :], axis=0, keepdims=True)
    lse = top + jnp.log(total)
    inv = inv_ref[0:1, :]
    ratio = jnp.exp(chosen - lse - old[...])
    position = lax.broadcasted_iota(jnp.int32, ratio.shape, 1)
    second_one = position >= rows // 2
    adv = jnp.where(second_one, nums[1], nums[0])
    length = jnp.where(second_one, nums[3], nums[2])
    within = jnp.where(second_one, position - rows // 2, position).astype(f32)
    mask = jnp.where(within < length, 1.0, 0.0)
    first = ratio * adv
    second = jnp.clip(ratio, clip_low, clip_high) * adv
    policy = -jnp.minimum(first, second)
    policy = jnp.where(adv < 0, jnp.minimum(policy, -dual_bound * adv), policy)
    active = (first <= second) & jnp.logical_not((adv < 0) & (first < dual_bound * adv))
    grad_logp = nums[4] * mask * jnp.where(active, -first, 0.0)
    kappa = inv * inv * grad_logp * (chosen - moment / total) / 5120.0
    small[...] = jnp.concatenate(
        [kappa, mask * policy, jnp.zeros((6, ratio.shape[1]), f32)], axis=0
    )
    lse_c, scale_c = column(lse), column(grad_logp * inv)
    target = column(tgt[...].astype(f32)).astype(jnp.int32)
    entry = lax.broadcasted_iota(jnp.int32, lg.shape, 1) + at[0] * half
    hit = jnp.where(entry == target, 1.0, 0.0)
    dl[...] = (scale_c * (hit - jnp.exp(lg[...] - lse_c))).astype(bf16)


def policy_of(at, nums, stats, logits, inv, targets, old_logp):
    rows, half = logits.shape
    return pl.pallas_call(
        policy_kernel,
        out_shape=[like((rows, half)), like((8, rows), f32)],
        in_specs=[whole(pltpu.SMEM)] * 2 + [whole()] * 5,
        out_specs=[whole()] * 2,
        compiler_params=params(),
        cost_estimate=cost(8 * rows * half, 6 * rows * half, rows * half),
        name="policy",
    )(at, nums, stats, logits, inv, targets, old_logp)


def back_kernel(at, dl, head, u_send, u_keep):
    c = at[2]
    cols = head.shape[1] // 2
    back = jnp.dot(dl[...], head[...], preferred_element_type=f32).astype(bf16)

    @pl.when(c == 0)
    def _():
        u_keep[0] = back[:, :cols]
        u_send[0] = back[:, cols:]

    @pl.when(c == 1)
    def _():
        u_send[0] = back[:, :cols]
        u_keep[0] = back[:, cols:]


def back_of(at, dl, head, cols):
    rows, half = dl.shape
    shapes = [like((4, rows, cols))] * 2
    return pl.pallas_call(
        back_kernel,
        out_shape=shapes,
        grid_spec=pltpu.PrefetchScalarGridSpec(
            num_scalar_prefetch=1,
            grid=(4,),
            in_specs=[
                full((rows, half)),
                pl.BlockSpec((half, 2 * cols), lambda j, at: (0, at[8 + j])),
            ],
            out_specs=[pl.BlockSpec((1, rows, cols), lambda j, at: (j, 0, 0))] * 2,
        ),
        compiler_params=params(),
        cost_estimate=cost(2 * rows * 8 * cols * half, 32 * rows * cols),
        name="back",
    )(at, dl, head)


def heads_kernel(at, early, late, dl, to_x, to_z):
    j = pl.program_id(0)
    scaled = jnp.where(j < 3, early[0], late[0])
    cols = scaled.shape[1] // 2
    step, half = cols // 4, dl.shape[1] // 2
    got = lax.dot_general(
        scaled, dl[...], (((0,), (0,)), ((), ())), preferred_element_type=f32
    ).astype(bf16)
    for i in range(2):
        place = 2 * at[8 + j] + i
        for k in range(4):
            part = got[i * cols + k * step : i * cols + (k + 1) * step, :]
            to_x[k, place] = part[:, :half]
            to_z[place, k] = part[:, half:]


def heads_of(at, early, late, dl):
    _, rows, cols = early.shape
    half = dl.shape[1]
    step = cols // 8
    shapes = [like((4, 8, step, half // 2)), like((8, 4, step, half // 2))]
    return pl.pallas_call(
        heads_kernel,
        out_shape=shapes,
        grid_spec=pltpu.PrefetchScalarGridSpec(
            num_scalar_prefetch=1,
            grid=(4,),
            in_specs=[
                pl.BlockSpec((1, rows, cols), lambda j, at: (jnp.minimum(j, 2), 0, 0)),
                full(late.shape),
                full((rows, half)),
            ],
            out_specs=[full(s.shape) for s in shapes],
        ),
        compiler_params=params(),
        cost_estimate=cost(2 * rows * 4 * cols * half, 24 * rows * cols),
        name="heads",
    )(at, early, late, dl)


def sum_pairs_kernel(groups, *refs):
    pairs = len(refs) // (2 + len(groups))
    ins, outs = refs[: 2 * pairs], refs[2 * pairs :]
    for p in range(pairs):
        keep, got = ins[2 * p], ins[2 * p + 1]
        for out, group in zip(outs[p * len(groups) :], groups):
            for at, j in enumerate(group):
                total = (keep[j].astype(f32) + got[j].astype(f32)).astype(out.dtype)
                if len(group) > 1:
                    out[at] = total
                else:
                    out[...] = total


def sum_pairs(ins, groups, name):
    shape = ins[0].shape[1:]
    outs = [like(((len(g),) if len(g) > 1 else ()) + shape) for g in groups] * (len(ins) // 2)
    return pl.pallas_call(
        functools.partial(sum_pairs_kernel, groups),
        out_shape=outs,
        in_specs=[whole()] * len(ins),
        out_specs=[whole()] * len(outs),
        compiler_params=params(),
        cost_estimate=cost(len(ins) * ins[0].size, 3 * len(ins) * ins[0].size),
        name=name,
    )(*ins)


def sum_first_kernel(a, out):
    for k in range(out.shape[0]):
        total = a[0, k].astype(f32)
        for s in range(1, a.shape[0]):
            total = total + a[s, k].astype(f32)
        out[k] = total.astype(out.dtype)


def sum_first(value, name):
    return pl.pallas_call(
        sum_first_kernel,
        out_shape=like(value.shape[1:]),
        in_specs=[whole()],
        out_specs=whole(),
        compiler_params=params(),
        cost_estimate=cost(value.size, 3 * value.size),
        name=name,
    )(value)


def join_kernel(from_z, from_x, out):
    width = from_x.shape[1]
    total = from_z[0].astype(f32)
    for k in range(1, from_z.shape[0]):
        total = total + from_z[k].astype(f32)
    out[:, :width] = total
    out[:, width:] = from_x[...].astype(f32)


def final_kernel(u0, u1, u2, u3, h_ref, g_ref, small, out, part):
    gain = g_ref[...].astype(f32)
    resp, rows, _ = h_ref.shape
    kappa = column(small[0:1, :])
    sums = None
    for r in range(resp):
        cut = slice(r * rows, (r + 1) * rows)
        u = sum(v[cut, :].astype(f32) for v in (u0, u1, u2, u3))
        h = h_ref[r].astype(f32)
        out[r] = (gain * u - h * kappa[cut, :]).astype(bf16)
        now = jnp.sum(u * h, axis=0, keepdims=True)
        sums = now if sums is None else sums + now
    loss = jnp.sum(small[1:2, :], axis=1, keepdims=True)
    part[...] = jnp.concatenate([sums, jnp.broadcast_to(loss, (1, 128))], axis=1)


def simple(kernel, shapes, ins, nbytes, name):
    return pl.pallas_call(
        kernel,
        out_shape=shapes,
        in_specs=[whole(pltpu.SMEM if v.ndim == 1 else VMEM) for v in ins],
        out_specs=[whole()] * len(shapes),
        compiler_params=params(),
        cost_estimate=cost(nbytes // 2, nbytes),
        name=name,
    )(*ins)


def copy_for_each(value, axis):
    size = lax.axis_size(axis)
    return lax.all_to_all(
        jnp.broadcast_to(value[None], (size, *value.shape)), axis, 0, 0, tiled=True
    )


def after(value, *first):
    return lax.optimization_barrier((value, *first))[0]


def body(hidden, gain, head, targets, lengths, old_logp, rewards, group_slot):
    resp_here, length_max, cols = hidden.shape
    rows = resp_here * length_max
    x, y, z, c = (lax.axis_index(a) for a in ("x", "y", "z", "c"))
    chips = (y + jnp.array([0, 3, 1, 2], jnp.int32)) % 4
    at = jnp.concatenate([jnp.stack([2 * y + c, y, c, z, x, x, x, x]), chips]).astype(jnp.int32)

    payload = jnp.concatenate(
        [jnp.broadcast_to(gain[None], (16, cols)), hidden.reshape(rows, cols)], axis=0
    )
    cut = 16 + length_max
    prev, following = shift(payload, "y", 1), shift(payload, "y", -1)
    own_o = shift(payload, "c", 1)

    groups_all = resp_here * lax.axis_size(DP) // GROUP
    group = group_slot // GROUP
    member = (group[:, None] == jnp.arange(groups_all, dtype=jnp.int32)[None, :]).astype(f32)
    local = jnp.concatenate(
        [jnp.sum(member * rewards[:, None], axis=0), jnp.sum(lengths).astype(f32)[None]]
    )
    over_z = copy_for_each(local, "z").sum(axis=0)
    prev, following, over_z = lax.optimization_barrier((prev, following, over_z))

    far_a, far_b = prev[:cut], following[cut:]
    far_a, far_b, prev, following = lax.optimization_barrier((far_a, far_b, prev, following))
    far_a, far_b = shift(far_a, "y", 1), shift(far_b, "y", -1)
    sums = copy_for_each(over_z, "x").sum(axis=0)
    prev_o, following_o = shift(prev, "c", 1), shift(following, "c", 1)
    early, acc, sq = logits_of(
        at, 0, [(payload, own_o), (prev, prev_o), (following, following_o)], head
    )
    far_a, far_b = after(far_a, acc), after(far_b, acc)
    far_a_o, far_b_o = shift(far_a, "c", 1), shift(far_b, "c", 1)

    group_sums, count = sums[:groups_all], sums[groups_all]
    adv_resp = rewards - jnp.sum(member * group_sums[None, :], axis=1) / GROUP
    slots_all = rows * lax.axis_size(DP)
    nums = jnp.concatenate([adv_resp, lengths.astype(f32), (slots_all / count)[None]])
    targets = targets.reshape(1, rows)
    old_logp = old_logp.reshape(1, rows)

    late, logits, stats, inv = logits_of(
        at, 3, [(far_a, far_b, far_a_o, far_b_o)], head, (acc, sq), targets
    )
    all_stats = lax.all_to_all(stats, FSDP, 0, 0, tiled=True)
    dl, small = policy_of(at, nums, all_stats, logits, inv, targets, old_logp)
    part, half = cols // 4, dl.shape[1] // 2

    u_send, u_keep = back_of(at, dl, head, cols)
    u_got = shift(u_send, "c", 1)
    to_x, to_z = heads_of(at, early, late, after(dl, u_send))
    half_z = lax.psum_scatter(to_z, "z", scatter_dimension=0, tiled=False)
    half_z = lax.psum_scatter(half_z, "x", scatter_dimension=0, tiled=False)
    from_x = lax.all_to_all(to_x, "x", 0, 0, tiled=True)
    u0, u1, u2, u3 = sum_pairs((u_keep, u_got), ((0,), (1,), (2,), (3,)), "sum_u")
    u1, u2, u3 = shift(u1, "y", -1), shift(u2, "y", 1), shift(u3, "y", 2)

    from_x = after(from_x, u1, u2, u3)
    from_z = lax.all_to_all(sum_first(from_x, "sum_x"), "z", 0, 0, tiled=True)
    grad_hidden, gain_part = simple(
        final_kernel,
        [like(hidden.shape), like((1, cols + 128), f32)],
        (u0, u1, u2, u3, hidden, gain.reshape(1, cols), small),
        12 * rows * cols,
        "final",
    )
    tail = gain_part.reshape(-1, 128)
    tail = tail + shift(tail, "x", 1) + shift(tail, "x", 2) + shift(tail, "x", -1)
    for step in (1, -1, 3):
        tail = tail + turn(tail, step)
    (grad_head_t,) = simple(
        join_kernel,
        [like((part, 2 * half), f32)],
        (from_z, half_z),
        2 * from_z.size + 16 * part * half,
        "join",
    )
    tail = tail.reshape(-1)
    return (tail[cols] / count, grad_hidden, tail[:cols], grad_head_t)


def solution(mesh):
    split = Mesh(mesh.devices.reshape(8, 4, 4, 2), ("z", "x", "y", "c"))
    return jax.shard_map(
        body,
        mesh=split,
        in_specs=(
            P(DP, None, FSDP),
            P(FSDP),
            P(FSDP, None),
            P(DP, None),
            P(DP),
            P(DP, None),
            P(DP),
            P(DP),
        ),
        out_specs=(P(), P(DP, None, FSDP), P(FSDP), P(DP, FSDP)),
        check_vma=False,
    )
```

```python
import functools

import jax
import jax.numpy as jnp
from jax import lax
from jax.experimental import pallas as pl
from jax.experimental.pallas import tpu as pltpu
from jax.sharding import Mesh
from jax.sharding import PartitionSpec as P

GROUP = 8
FSDP = ("y", "c")
DP = ("z", "x")
SIZES = {"z": 8, "x": 4, "y": 4, "c": 2}

eps_norm = 1e-06
clip_low = 0.8
clip_high = 1.2
dual_bound = 3.0

f32, bf16 = jnp.float32, jnp.bfloat16
VMEM = pltpu.VMEM


def shift(value, axis, step):
    n = SIZES[axis]
    return lax.ppermute(value, axis, [(i, (i + step) % n) for i in range(n)])


def turn(value, step):
    return lax.ppermute(
        value, "z", [(i, (i + (step if i % 2 == 0 else -step)) % 8) for i in range(8)]
    )


def params(limit=60 << 20):
    return pltpu.CompilerParams(vmem_limit_bytes=limit)


def cost(flops, nbytes, trans=0):
    return pl.CostEstimate(flops=flops, bytes_accessed=nbytes, transcendentals=trans)


def whole(space=None):
    return pl.BlockSpec(memory_space=space or VMEM)


def like(shape, kind=bf16):
    return jax.ShapeDtypeStruct(shape, kind)


def column(row):
    n = row.shape[1]
    return jnp.transpose(jnp.broadcast_to(row, (128, n)))[:, 0:1]


def rows_of(columns):
    n = columns[0].shape[0]
    lane = lax.broadcasted_iota(jnp.int32, (n, 128), 1)
    table = jnp.zeros((n, 128), f32)
    for k, col in enumerate(columns):
        table = jnp.where(lane == k, col, table)
    return jnp.transpose(table)[0:8, :]


def full(shape):
    return pl.BlockSpec(shape, lambda k, *at: (0,) * len(shape))


def local_kernel(groups, rewards, lengths, slots, out):
    lane = lax.broadcasted_iota(jnp.int32, (1, 128), 1)
    row = jnp.zeros((1, 128), f32)
    for r in range(2):
        row += jnp.where(lane == slots[r] // GROUP, rewards[r], 0.0)
        row += jnp.where(lane == groups, lengths[r].astype(f32), 0.0)
    for k in range(out.shape[0]):
        out[k] = row


def logits_kernel(count, per, last, at, *refs):
    pieces = refs[: count * per * 2]
    refs = refs[count * per * 2 :]
    if last:
        acc_in, sq_in, tgt = refs[:3]
        refs = refs[3:]
    head, hb = refs[:2]
    outs, (slot, acc, sq, sem) = refs[2:-4], refs[-4:]
    j = pl.program_id(0)
    rows = acc.shape[0]
    cols = slot.shape[2] // 2

    @pl.when(j == 0)
    def _():
        copies = []
        for k, piece in enumerate(pieces):
            first = 0 if k % per == 0 else pieces[k - 1].shape[0]
            side = lax.rem(at[2] + (k // per) % 2, 2)
            lanes = pl.ds(pl.multiple_of(side * cols, cols), cols)
            place = slot.at[k // (2 * per), pl.ds(first, piece.shape[0]), lanes]
            copies.append(pltpu.make_async_copy(piece, place, sem.at[k]))
        for copy in copies:
            copy.start()
        if last:
            acc[...] = acc_in[...]
            sq[...] = column(sq_in[0:1, :])
        else:
            acc[...] = jnp.zeros_like(acc)
            sq[...] = jnp.zeros_like(sq)
        for copy in copies:
            copy.wait()

    gain = slot[j, 0:16, :][0:1, :].astype(f32)
    raw = slot[j, 16 : 16 + rows, :].astype(f32)
    sq[...] += jnp.sum(raw * raw, axis=1, keepdims=True)
    scaled = (raw * gain).astype(bf16)
    hb[0] = scaled
    acc[...] += lax.dot_general(
        scaled, head[...], (((1,), (1,)), ((), ())), preferred_element_type=f32
    )

    @pl.when(j == count - 1)
    def _():
        if not last:
            outs[0][...] = acc[...]
            outs[1][...] = rows_of([sq[...]])
            return
        lg, st, inv_ref = outs
        inv_c = lax.rsqrt(sq[...] / 5120.0 + eps_norm)
        inv_ref[...] = rows_of([inv_c])
        logits = acc[...] * inv_c
        lg[...] = logits
        half = logits.shape[1]
        entry = lax.broadcasted_iota(jnp.int32, logits.shape, 1) + at[0] * half
        target = column(tgt[...].astype(f32)).astype(jnp.int32)
        top = jnp.max(logits, axis=1, keepdims=True)
        power = jnp.exp(logits - top)
        found = rows_of(
            [
                top,
                jnp.sum(power, axis=1, keepdims=True),
                jnp.sum(power * logits, axis=1, keepdims=True),
                jnp.sum(jnp.where(entry == target, logits, 0.0), axis=1, keepdims=True),
            ]
        )
        for k in range(st.shape[0]):
            st[k] = found


def logits_of(at, first, blocks, head, before=None, targets=None):
    count, per = len(blocks), len(blocks[0]) // 2
    last = before is not None
    half = head.shape[0]
    cols = 2 * blocks[0][0].shape[1]
    height = sum(p.shape[0] for p in blocks[0]) // 2
    rows = height - 16
    anywhere = pl.BlockSpec(memory_space=pl.ANY)
    shapes = [like((count, rows, cols))]
    specs = [pl.BlockSpec((1, rows, cols), lambda j, *a: (j, 0, 0))]
    shapes += [like((rows, half), f32)]
    shapes += [like((8, 8, rows), f32)] if last else []
    shapes += [like((8, rows), f32)]
    extra = (*before, targets) if last else ()
    return pl.pallas_call(
        functools.partial(logits_kernel, count, per, last),
        out_shape=shapes,
        grid_spec=pltpu.PrefetchScalarGridSpec(
            num_scalar_prefetch=1,
            grid=(count,),
            in_specs=[anywhere] * (count * per * 2)
            + [full(e.shape) for e in extra]
            + [pl.BlockSpec((half, cols), lambda j, at: (0, at[8 + first + j]))],
            out_specs=specs + [full(s.shape) for s in shapes[1:]],
            scratch_shapes=[
                VMEM((count, height, cols), bf16),
                VMEM((rows, half), f32),
                VMEM((rows, 1), f32),
                pltpu.SemaphoreType.DMA((count * per * 2,)),
            ],
        ),
        compiler_params=params(),
        cost_estimate=cost(1000, 1000),
        name="logits_last" if last else "logits_first",
    )(at, *[p for b in blocks for p in b], *extra, head)


def policy_kernel(groups, slots_all, at, rewards, lengths, slots, sums_ref, st, lg, inv_ref, tgt, old, dl, small):
    half = lg.shape[1]
    rows = lg.shape[0]
    sums = jnp.sum(sums_ref[:, 0, :], axis=0, keepdims=True)
    lane = lax.broadcasted_iota(jnp.int32, sums.shape, 1)

    def entry_of(k):
        return jnp.sum(jnp.where(lane == k, sums, 0.0), axis=1, keepdims=True)

    advs = [rewards[r] - entry_of(slots[r] // GROUP) / GROUP for r in range(2)]
    live = entry_of(groups)
    top = jnp.max(st[:, 0, :], axis=0, keepdims=True)
    weight = jnp.exp(st[:, 0, :] - top)
    total = jnp.sum(st[:, 1, :] * weight, axis=0, keepdims=True)
    moment = jnp.sum(st[:, 2, :] * weight, axis=0, keepdims=True)
    chosen = jnp.sum(st[:, 3, :], axis=0, keepdims=True)
    lse = top + jnp.log(total)
    inv = inv_ref[0:1, :]
    ratio = jnp.exp(chosen - lse - old[...])
    position = lax.broadcasted_iota(jnp.int32, ratio.shape, 1)
    second_one = position >= rows // 2
    adv = jnp.where(second_one, advs[1], advs[0])
    length = jnp.where(second_one, lengths[1].astype(f32), lengths[0].astype(f32))
    within = jnp.where(second_one, position - rows // 2, position).astype(f32)
    mask = jnp.where(within < length, 1.0, 0.0)
    first = ratio * adv
    second = jnp.clip(ratio, clip_low, clip_high) * adv
    policy = -jnp.minimum(first, second)
    policy = jnp.where(adv < 0, jnp.minimum(policy, -dual_bound * adv), policy)
    active = (first <= second) & jnp.logical_not((adv < 0) & (first < dual_bound * adv))
    grad_logp = slots_all / live * mask * jnp.where(active, -first, 0.0)
    kappa = inv * inv * grad_logp * (chosen - moment / total) / 5120.0
    small[...] = jnp.concatenate(
        [kappa, mask * policy / live, jnp.zeros((6, ratio.shape[1]), f32)], axis=0
    )
    lse_c, scale_c = column(lse), column(grad_logp * inv)
    target = column(tgt[...].astype(f32)).astype(jnp.int32)
    entry = lax.broadcasted_iota(jnp.int32, lg.shape, 1) + at[0] * half
    hit = jnp.where(entry == target, 1.0, 0.0)
    dl[...] = (scale_c * (hit - jnp.exp(lg[...] - lse_c))).astype(bf16)


def policy_of(groups, slots_all, at, scalars, sums, stats, logits, inv, targets, old_logp):
    rows, half = logits.shape
    return pl.pallas_call(
        functools.partial(policy_kernel, groups, float(slots_all)),
        out_shape=[like((rows, half)), like((8, rows), f32)],
        in_specs=[whole(pltpu.SMEM)] * 4 + [whole()] * 6,
        out_specs=[whole()] * 2,
        compiler_params=params(),
        cost_estimate=cost(8 * rows * half, 6 * rows * half, rows * half),
        name="policy",
    )(at, *scalars, sums, stats, logits, inv, targets, old_logp)


def back_kernel(at, dl, dl_o, head, head_o, *outs):
    total = jnp.dot(dl[...], head[...], preferred_element_type=f32)
    total += jnp.dot(dl_o[...], head_o[...], preferred_element_type=f32)
    for k, out in enumerate(outs):

        @pl.when(pl.program_id(0) == k)
        def _(out=out):
            out[...] = total.astype(bf16)


def back_of(at, dl, dl_o, head, head_o, cols):
    rows, half = dl.shape
    return pl.pallas_call(
        back_kernel,
        out_shape=[like((rows, cols))] * 4,
        grid_spec=pltpu.PrefetchScalarGridSpec(
            num_scalar_prefetch=1,
            grid=(4,),
            in_specs=[full((rows, half))] * 2
            + [pl.BlockSpec((half, cols), lambda j, at: (0, 2 * at[8 + j] + at[2]))] * 2,
            out_specs=[full((rows, cols))] * 4,
        ),
        compiler_params=params(),
        cost_estimate=cost(2 * rows * 8 * cols * half, 32 * rows * cols),
        name="back",
    )(at, dl, dl_o, head, head_o)


def heads_kernel(at, early, late, dl, to_x, to_z):
    j = pl.program_id(0)
    scaled = jnp.where(j < 3, early[0], late[0])
    cols = scaled.shape[1] // 2
    step, half = cols // 4, dl.shape[1] // 2
    got = lax.dot_general(
        scaled, dl[...], (((0,), (0,)), ((), ())), preferred_element_type=f32
    ).astype(bf16)
    for i in range(2):
        place = 2 * at[8 + j] + i
        for k in range(4):
            part = got[i * cols + k * step : i * cols + (k + 1) * step, :]
            to_x[k, place] = part[:, :half]
            to_z[place, k] = part[:, half:]


def heads_of(at, early, late, dl):
    _, rows, cols = early.shape
    half = dl.shape[1]
    step = cols // 8
    shapes = [like((4, 8, step, half // 2)), like((8, 4, step, half // 2))]
    return pl.pallas_call(
        heads_kernel,
        out_shape=shapes,
        grid_spec=pltpu.PrefetchScalarGridSpec(
            num_scalar_prefetch=1,
            grid=(4,),
            in_specs=[
                pl.BlockSpec((1, rows, cols), lambda j, at: (jnp.minimum(j, 2), 0, 0)),
                full(late.shape),
                full((rows, half)),
            ],
            out_specs=[full(s.shape) for s in shapes],
        ),
        compiler_params=params(),
        cost_estimate=cost(2 * rows * 4 * cols * half, 24 * rows * cols),
        name="heads",
    )(at, early, late, dl)


def sum_first_kernel(a, out):
    for k in range(out.shape[0]):
        total = a[0, k].astype(f32)
        for s in range(1, a.shape[0]):
            total = total + a[s, k].astype(f32)
        out[k] = total.astype(out.dtype)


def sum_first(value, name):
    return pl.pallas_call(
        sum_first_kernel,
        out_shape=like(value.shape[1:]),
        in_specs=[whole()],
        out_specs=whole(),
        compiler_params=params(),
        cost_estimate=cost(value.size, 3 * value.size),
        name=name,
    )(value)


def join_kernel(from_z, from_x, out):
    width = from_x.shape[1]
    total = from_z[0].astype(f32)
    for k in range(1, from_z.shape[0]):
        total = total + from_z[k].astype(f32)
    out[:, :width] = total
    out[:, width:] = from_x[...].astype(f32)


def final_kernel(u0, u1, u2, u3, h_ref, g_ref, small, out, part):
    gain = g_ref[...].astype(f32)
    resp, rows, _ = h_ref.shape
    kappa = column(small[0:1, :])
    sums = None
    for r in range(resp):
        cut = slice(r * rows, (r + 1) * rows)
        u = sum(v[cut, :].astype(f32) for v in (u0, u1, u2, u3))
        h = h_ref[r].astype(f32)
        out[r] = (gain * u - h * kappa[cut, :]).astype(bf16)
        now = jnp.sum(u * h, axis=0, keepdims=True)
        sums = now if sums is None else sums + now
    loss = jnp.sum(small[1:2, :], axis=1, keepdims=True)
    part[...] = jnp.concatenate([sums, jnp.broadcast_to(loss, (1, 128))], axis=1)


def simple(kernel, shapes, ins, nbytes, name, flops=None):
    return pl.pallas_call(
        kernel,
        out_shape=shapes,
        in_specs=[whole(pltpu.SMEM if v.ndim == 1 else VMEM) for v in ins],
        out_specs=[whole()] * len(shapes),
        compiler_params=params(),
        cost_estimate=cost(flops or nbytes // 2, nbytes),
        name=name,
    )(*ins)


def after(value, *first):
    return lax.optimization_barrier((value, *first))[0]


def body(hidden, gain, head, targets, lengths, old_logp, rewards, group_slot):
    resp_here, length_max, cols = hidden.shape
    rows = resp_here * length_max
    x, y, z, c = (lax.axis_index(a) for a in ("x", "y", "z", "c"))
    chips = (y + jnp.array([0, 3, 1, 2], jnp.int32)) % 4
    at = jnp.concatenate([jnp.stack([2 * y + c, y, c, z, x, x, x, x]), chips]).astype(jnp.int32)

    payload = jnp.concatenate(
        [jnp.broadcast_to(gain[None], (16, cols)), hidden.reshape(rows, cols)], axis=0
    )
    cut = 16 + length_max
    prev, following = shift(payload, "y", 1), shift(payload, "y", -1)
    own_o = shift(payload, "c", 1)

    groups_all = resp_here * lax.axis_size(DP) // GROUP
    scalars = (rewards, lengths, group_slot)
    (local,) = simple(
        functools.partial(local_kernel, groups_all),
        [like((lax.axis_size(DP), 1, 128), f32)],
        scalars,
        1 << 14,
        "local",
    )
    sums = lax.all_to_all(local, DP, 0, 0, tiled=True)
    prev, following, local = lax.optimization_barrier((prev, following, local))

    far_a, far_b = prev[:cut], following[cut:]
    far_a, far_b, prev, following = lax.optimization_barrier((far_a, far_b, prev, following))
    far_a, far_b = shift(far_a, "y", 1), shift(far_b, "y", -1)
    prev_o, following_o = shift(prev, "c", 1), shift(following, "c", 1)
    early, acc, sq = logits_of(
        at, 0, [(payload, own_o), (prev, prev_o), (following, following_o)], head
    )
    far_a, far_b = after(far_a, acc), after(far_b, acc)
    head_o = shift(after(head, acc), "c", 1)
    far_a_o, far_b_o = shift(far_a, "c", 1), shift(far_b, "c", 1)

    slots_all = rows * lax.axis_size(DP)
    targets = targets.reshape(1, rows)
    old_logp = old_logp.reshape(1, rows)

    late, logits, stats, inv = logits_of(
        at, 3, [(far_a, far_b, far_a_o, far_b_o)], head, (acc, sq), targets
    )
    all_stats = lax.all_to_all(stats, FSDP, 0, 0, tiled=True)
    dl, small = policy_of(groups_all, slots_all, at, scalars, sums, all_stats, logits, inv, targets, old_logp)
    part, half = cols // 4, dl.shape[1] // 2

    dl_o = shift(dl, "c", 1)
    to_x, to_z = heads_of(at, early, late, dl)
    half_z = lax.psum_scatter(to_z, "z", scatter_dimension=0, tiled=False)
    from_x = lax.all_to_all(to_x, "x", 0, 0, tiled=True)
    u0, u1, u2, u3 = back_of(at, after(dl, to_x), dl_o, head, head_o, cols)
    u1, u2, u3 = shift(u1, "y", -1), shift(u2, "y", 1), shift(u3, "y", 2)

    to_z = sum_first(from_x, "sum_x")
    from_z = lax.all_to_all(to_z, "z", 0, 0, tiled=True)
    half_z = after(half_z, to_z)
    u1, u2, u3, _ = lax.optimization_barrier((u1, u2, u3, half_z))
    half_z = lax.psum_scatter(half_z, "x", scatter_dimension=0, tiled=False)
    grad_hidden, gain_part = simple(
        final_kernel,
        [like(hidden.shape), like((1, cols + 128), f32)],
        (u0, u1, u2, u3, hidden, gain.reshape(1, cols), small),
        12 * rows * cols,
        "final",
        200 * 10**9,
    )
    tail = gain_part.reshape(-1, 128)
    tail = tail + shift(tail, "x", 1) + shift(tail, "x", 2) + shift(tail, "x", -1)
    for step in (1, -1, 3):
        tail = tail + turn(tail, step)
    (grad_head_t,) = simple(
        join_kernel,
        [like((part, 2 * half), f32)],
        (from_z, half_z),
        2 * from_z.size + 16 * part * half,
        "join",
    )
    tail = tail.reshape(-1)
    return (tail[cols], grad_hidden, tail[:cols], grad_head_t)


def solution(mesh):
    split = Mesh(mesh.devices.reshape(8, 4, 4, 2), ("z", "x", "y", "c"))
    return jax.shard_map(
        body,
        mesh=split,
        in_specs=(
            P(DP, None, FSDP),
            P(FSDP),
            P(FSDP, None),
            P(DP, None),
            P(DP),
            P(DP, None),
            P(DP),
            P(DP),
        ),
        out_specs=(P(), P(DP, None, FSDP), P(FSDP), P(DP, FSDP)),
        check_vma=False,
    )
```

```python
import functools

import jax
import jax.numpy as jnp
from jax import lax
from jax.experimental import pallas as pl
from jax.experimental.pallas import tpu as pltpu
from jax.sharding import Mesh
from jax.sharding import PartitionSpec as P

GROUP = 8
FSDP = ("y", "c")
DP = ("z", "x")
SIZES = {"z": 8, "x": 4, "y": 4, "c": 2}

eps_norm = 1e-06
clip_low = 0.8
clip_high = 1.2
dual_bound = 3.0

f32, bf16 = jnp.float32, jnp.bfloat16
VMEM = pltpu.VMEM


def shift(value, axis, step):
    n = SIZES[axis]
    return lax.ppermute(value, axis, [(i, (i + step) % n) for i in range(n)])


def turn(value, step):
    return lax.ppermute(
        value, "z", [(i, (i + (step if i % 2 == 0 else -step)) % 8) for i in range(8)]
    )


def across(value, axis, bit):
    return lax.ppermute(value, axis, [(i, i ^ bit) for i in range(SIZES[axis])])


def params(limit=60 << 20):
    return pltpu.CompilerParams(vmem_limit_bytes=limit)


def cost(flops, nbytes, trans=0):
    return pl.CostEstimate(flops=flops, bytes_accessed=nbytes, transcendentals=trans)


def whole(space=None):
    return pl.BlockSpec(memory_space=space or VMEM)


def like(shape, kind=bf16):
    return jax.ShapeDtypeStruct(shape, kind)


def column(row):
    n = row.shape[1]
    return jnp.transpose(jnp.broadcast_to(row, (128, n)))[:, 0:1]


def rows_of(columns):
    n = columns[0].shape[0]
    lane = lax.broadcasted_iota(jnp.int32, (n, 128), 1)
    table = jnp.zeros((n, 128), f32)
    for k, col in enumerate(columns):
        table = jnp.where(lane == k, col, table)
    return jnp.transpose(table)[0:8, :]


def full(shape):
    return pl.BlockSpec(shape, lambda k, *at: (0,) * len(shape))


def local_kernel(groups, rewards, lengths, slots, out):
    lane = lax.broadcasted_iota(jnp.int32, (1, 128), 1)
    row = jnp.zeros((1, 128), f32)
    for r in range(2):
        row += jnp.where(lane == slots[r] // GROUP, rewards[r], 0.0)
        row += jnp.where(lane == groups, lengths[r].astype(f32), 0.0)
    for k in range(out.shape[0]):
        out[k] = row


def logits_kernel(count, per, last, at, *refs):
    pieces = refs[: count * per * 2]
    refs = refs[count * per * 2 :]
    if last:
        acc_in, sq_in, tgt = refs[:3]
        refs = refs[3:]
    head, hb = refs[:2]
    outs, (slot, acc, sq, sem) = refs[2:-4], refs[-4:]
    j = pl.program_id(0)
    rows = acc.shape[0]
    cols = slot.shape[2] // 2

    @pl.when(j == 0)
    def _():
        copies = []
        for k, piece in enumerate(pieces):
            first = 0 if k % per == 0 else pieces[k - 1].shape[0]
            side = lax.rem(at[2] + (k // per) % 2, 2)
            lanes = pl.ds(pl.multiple_of(side * cols, cols), cols)
            place = slot.at[k // (2 * per), pl.ds(first, piece.shape[0]), lanes]
            copies.append(pltpu.make_async_copy(piece, place, sem.at[k]))
        for copy in copies:
            copy.start()
        if last:
            acc[...] = acc_in[...]
            sq[...] = column(sq_in[0:1, :])
        else:
            acc[...] = jnp.zeros_like(acc)
            sq[...] = jnp.zeros_like(sq)
        for copy in copies:
            copy.wait()

    gain = slot[j, 0:16, :][0:1, :].astype(f32)
    raw = slot[j, 16 : 16 + rows, :].astype(f32)
    sq[...] += jnp.sum(raw * raw, axis=1, keepdims=True)
    scaled = (raw * gain).astype(bf16)
    hb[0] = scaled
    acc[...] += lax.dot_general(
        scaled, head[...], (((1,), (1,)), ((), ())), preferred_element_type=f32
    )

    @pl.when(j == count - 1)
    def _():
        if not last:
            outs[0][...] = acc[...]
            outs[1][...] = rows_of([sq[...]])
            return
        lg, st, inv_ref = outs
        inv_c = lax.rsqrt(sq[...] / 5120.0 + eps_norm)
        inv_ref[...] = rows_of([inv_c])
        logits = acc[...] * inv_c
        lg[...] = logits
        half = logits.shape[1]
        entry = lax.broadcasted_iota(jnp.int32, logits.shape, 1) + at[0] * half
        target = column(tgt[...].astype(f32)).astype(jnp.int32)
        top = jnp.max(logits, axis=1, keepdims=True)
        power = jnp.exp(logits - top)
        found = rows_of(
            [
                top,
                jnp.sum(power, axis=1, keepdims=True),
                jnp.sum(power * logits, axis=1, keepdims=True),
                jnp.sum(jnp.where(entry == target, logits, 0.0), axis=1, keepdims=True),
            ]
        )
        for k in range(st.shape[0]):
            st[k] = found


def logits_of(at, first, blocks, head, before=None, targets=None):
    count, per = len(blocks), len(blocks[0]) // 2
    last = before is not None
    half = head.shape[0]
    cols = 2 * blocks[0][0].shape[1]
    height = sum(p.shape[0] for p in blocks[0]) // 2
    rows = height - 16
    anywhere = pl.BlockSpec(memory_space=pl.ANY)
    shapes = [like((count, rows, cols))]
    specs = [pl.BlockSpec((1, rows, cols), lambda j, *a: (j, 0, 0))]
    shapes += [like((rows, half), f32)]
    shapes += [like((8, 8, rows), f32)] if last else []
    shapes += [like((8, rows), f32)]
    extra = (*before, targets) if last else ()
    return pl.pallas_call(
        functools.partial(logits_kernel, count, per, last),
        out_shape=shapes,
        grid_spec=pltpu.PrefetchScalarGridSpec(
            num_scalar_prefetch=1,
            grid=(count,),
            in_specs=[anywhere] * (count * per * 2)
            + [full(e.shape) for e in extra]
            + [pl.BlockSpec((half, cols), lambda j, at: (0, at[8 + first + j]))],
            out_specs=specs + [full(s.shape) for s in shapes[1:]],
            scratch_shapes=[
                VMEM((count, height, cols), bf16),
                VMEM((rows, half), f32),
                VMEM((rows, 1), f32),
                pltpu.SemaphoreType.DMA((count * per * 2,)),
            ],
        ),
        compiler_params=params(),
        cost_estimate=cost(1000, 1000),
        name="logits_last" if last else "logits_first",
    )(at, *[p for b in blocks for p in b], *extra, head)


def policy_kernel(groups, slots_all, at, rewards, lengths, slots, sums_ref, st, lg, inv_ref, tgt, old, dl, small):
    half = lg.shape[1]
    rows = lg.shape[0]
    sums = jnp.sum(sums_ref[:, 0, :], axis=0, keepdims=True)
    lane = lax.broadcasted_iota(jnp.int32, sums.shape, 1)

    def entry_of(k):
        return jnp.sum(jnp.where(lane == k, sums, 0.0), axis=1, keepdims=True)

    advs = [rewards[r] - entry_of(slots[r] // GROUP) / GROUP for r in range(2)]
    live = entry_of(groups)
    top = jnp.max(st[:, 0, :], axis=0, keepdims=True)
    weight = jnp.exp(st[:, 0, :] - top)
    total = jnp.sum(st[:, 1, :] * weight, axis=0, keepdims=True)
    moment = jnp.sum(st[:, 2, :] * weight, axis=0, keepdims=True)
    chosen = jnp.sum(st[:, 3, :], axis=0, keepdims=True)
    lse = top + jnp.log(total)
    inv = inv_ref[0:1, :]
    ratio = jnp.exp(chosen - lse - old[...])
    position = lax.broadcasted_iota(jnp.int32, ratio.shape, 1)
    second_one = position >= rows // 2
    adv = jnp.where(second_one, advs[1], advs[0])
    length = jnp.where(second_one, lengths[1].astype(f32), lengths[0].astype(f32))
    within = jnp.where(second_one, position - rows // 2, position).astype(f32)
    mask = jnp.where(within < length, 1.0, 0.0)
    first = ratio * adv
    second = jnp.clip(ratio, clip_low, clip_high) * adv
    policy = -jnp.minimum(first, second)
    policy = jnp.where(adv < 0, jnp.minimum(policy, -dual_bound * adv), policy)
    active = (first <= second) & jnp.logical_not((adv < 0) & (first < dual_bound * adv))
    grad_logp = slots_all / live * mask * jnp.where(active, -first, 0.0)
    kappa = inv * inv * grad_logp * (chosen - moment / total) / 5120.0
    small[...] = jnp.concatenate(
        [kappa, mask * policy / live, jnp.zeros((6, ratio.shape[1]), f32)], axis=0
    )
    lse_c, scale_c = column(lse), column(grad_logp * inv)
    target = column(tgt[...].astype(f32)).astype(jnp.int32)
    entry = lax.broadcasted_iota(jnp.int32, lg.shape, 1) + at[0] * half
    hit = jnp.where(entry == target, 1.0, 0.0)
    dl[...] = (scale_c * (hit - jnp.exp(lg[...] - lse_c))).astype(bf16)


def policy_of(groups, slots_all, at, scalars, sums, stats, logits, inv, targets, old_logp):
    rows, half = logits.shape
    return pl.pallas_call(
        functools.partial(policy_kernel, groups, float(slots_all)),
        out_shape=[like((rows, half)), like((8, rows), f32)],
        in_specs=[whole(pltpu.SMEM)] * 4 + [whole()] * 6,
        out_specs=[whole()] * 2,
        compiler_params=params(),
        cost_estimate=cost(8 * rows * half, 6 * rows * half, rows * half),
        name="policy",
    )(at, *scalars, sums, stats, logits, inv, targets, old_logp)


def back_kernel(at, dl, dl_o, early, late, small, head, head_o, u0, u1, u2, u3, stay, go):
    j = pl.program_id(0)
    total = jnp.dot(dl[...], head[...], preferred_element_type=f32)
    total += jnp.dot(dl_o[...], head_o[...], preferred_element_type=f32)
    for k, out in enumerate((u0, u1, u2, u3)):

        @pl.when(j == k)
        def _(out=out):
            out[...] = total.astype(bf16)

    scaled = jnp.where(j < 3, early[0], late[0]).astype(f32)
    loss = jnp.sum(small[1:2, :], axis=1, keepdims=True) / 4
    line = jnp.concatenate(
        [jnp.sum(total * scaled, axis=0, keepdims=True), jnp.broadcast_to(loss, (1, 128))], axis=1
    )
    apart = at[8 + j] ^ at[1]

    @pl.when(apart % 2 == 0)
    def _():
        stay[apart // 2] = line

    @pl.when(apart % 2 == 1)
    def _():
        go[apart // 2] = line


def back_of(at, dl, dl_o, early, late, small, head, head_o, cols):
    rows, half = dl.shape
    shapes = [like((rows, cols))] * 4 + [like((2, 1, cols + 128), f32)] * 2
    return pl.pallas_call(
        back_kernel,
        out_shape=shapes,
        grid_spec=pltpu.PrefetchScalarGridSpec(
            num_scalar_prefetch=1,
            grid=(4,),
            in_specs=[full((rows, half))] * 2
            + [
                pl.BlockSpec((1, rows, cols), lambda j, at: (jnp.minimum(j, 2), 0, at[2])),
                pl.BlockSpec((1, rows, cols), lambda j, at: (0, 0, at[2])),
                full(small.shape),
            ]
            + [pl.BlockSpec((half, cols), lambda j, at: (0, 2 * at[8 + j] + at[2]))] * 2,
            out_specs=[full(s.shape) for s in shapes],
        ),
        compiler_params=params(),
        cost_estimate=cost(2 * rows * 8 * cols * half, 32 * rows * cols),
        name="back",
    )(at, dl, dl_o, early, late, small, head, head_o)


def heads_kernel(at, early, late, dl, to_x, to_z):
    j = pl.program_id(0)
    scaled = jnp.where(j < 3, early[0], late[0])
    cols = scaled.shape[1] // 2
    step, half = cols // 4, dl.shape[1] // 2
    got = lax.dot_general(
        scaled, dl[...], (((0,), (0,)), ((), ())), preferred_element_type=f32
    ).astype(bf16)
    for i in range(2):
        place = 2 * at[8 + j] + i
        for k in range(4):
            part = got[i * cols + k * step : i * cols + (k + 1) * step, :]
            to_x[k, place] = part[:, :half]
            to_z[place, k] = part[:, half:]


def heads_of(at, early, late, dl):
    _, rows, cols = early.shape
    half = dl.shape[1]
    step = cols // 8
    shapes = [like((4, 8, step, half // 2)), like((8, 4, step, half // 2))]
    return pl.pallas_call(
        heads_kernel,
        out_shape=shapes,
        grid_spec=pltpu.PrefetchScalarGridSpec(
            num_scalar_prefetch=1,
            grid=(4,),
            in_specs=[
                pl.BlockSpec((1, rows, cols), lambda j, at: (jnp.minimum(j, 2), 0, 0)),
                full(late.shape),
                full((rows, half)),
            ],
            out_specs=[full(s.shape) for s in shapes],
        ),
        compiler_params=params(),
        cost_estimate=cost(2 * rows * 4 * cols * half, 24 * rows * cols),
        name="heads",
    )(at, early, late, dl)


def sum_first_kernel(a, out):
    for k in range(out.shape[0]):
        total = a[0, k].astype(f32)
        for s in range(1, a.shape[0]):
            total = total + a[s, k].astype(f32)
        out[k] = total.astype(out.dtype)


def sum_first(value, name):
    return pl.pallas_call(
        sum_first_kernel,
        out_shape=like(value.shape[1:]),
        in_specs=[whole()],
        out_specs=whole(),
        compiler_params=params(),
        cost_estimate=cost(value.size, 3 * value.size),
        name=name,
    )(value)


def join_kernel(from_z, from_x, out):
    width = from_x.shape[1]
    total = from_z[0].astype(f32)
    for k in range(1, from_z.shape[0]):
        total = total + from_z[k].astype(f32)
    out[:, :width] = total
    out[:, width:] = from_x[...].astype(f32)


def final_kernel(u0, u1, u2, u3, h_ref, g_ref, small, out):
    gain = g_ref[...].astype(f32)
    resp, rows, _ = h_ref.shape
    kappa = column(small[0:1, :])
    for r in range(resp):
        cut = slice(r * rows, (r + 1) * rows)
        u = sum(v[cut, :].astype(f32) for v in (u0, u1, u2, u3))
        h = h_ref[r].astype(f32)
        out[r] = (gain * u - h * kappa[cut, :]).astype(bf16)


def simple(kernel, shapes, ins, nbytes, name, flops=None):
    return pl.pallas_call(
        kernel,
        out_shape=shapes,
        in_specs=[whole(pltpu.SMEM if v.ndim == 1 else VMEM) for v in ins],
        out_specs=[whole()] * len(shapes),
        compiler_params=params(),
        cost_estimate=cost(flops or nbytes // 2, nbytes),
        name=name,
    )(*ins)


def after(value, *first):
    return lax.optimization_barrier((value, *first))[0]


def body(hidden, gain, head, targets, lengths, old_logp, rewards, group_slot):
    resp_here, length_max, cols = hidden.shape
    rows = resp_here * length_max
    x, y, z, c = (lax.axis_index(a) for a in ("x", "y", "z", "c"))
    chips = (y + jnp.array([0, 3, 1, 2], jnp.int32)) % 4
    at = jnp.concatenate([jnp.stack([2 * y + c, y, c, z, x, x, x, x]), chips]).astype(jnp.int32)

    payload = jnp.concatenate(
        [jnp.broadcast_to(gain[None], (16, cols)), hidden.reshape(rows, cols)], axis=0
    )
    cut = 16 + length_max
    prev, following = shift(payload, "y", 1), shift(payload, "y", -1)
    own_o = shift(payload, "c", 1)

    groups_all = resp_here * lax.axis_size(DP) // GROUP
    scalars = (rewards, lengths, group_slot)
    (local,) = simple(
        functools.partial(local_kernel, groups_all),
        [like((lax.axis_size(DP), 1, 128), f32)],
        scalars,
        1 << 14,
        "local",
    )
    sums = lax.all_to_all(local, DP, 0, 0, tiled=True)
    prev, following, sums = lax.optimization_barrier((prev, following, sums))

    far_a, far_b = prev[:cut], following[cut:]
    far_a, far_b, prev, following = lax.optimization_barrier((far_a, far_b, prev, following))
    far_a, far_b = shift(far_a, "y", 1), shift(far_b, "y", -1)
    prev_o, following_o = shift(prev, "c", 1), shift(following, "c", 1)
    early, acc, sq = logits_of(
        at, 0, [(payload, own_o), (prev, prev_o), (following, following_o)], head
    )
    far_a, far_b = after(far_a, acc), after(far_b, acc)
    head_o = shift(after(head, acc), "c", 1)
    far_a_o, far_b_o = shift(far_a, "c", 1), shift(far_b, "c", 1)

    slots_all = rows * lax.axis_size(DP)
    targets = targets.reshape(1, rows)
    old_logp = old_logp.reshape(1, rows)

    late, logits, stats, inv = logits_of(
        at, 3, [(far_a, far_b, far_a_o, far_b_o)], head, (acc, sq), targets
    )
    all_stats = lax.all_to_all(stats, FSDP, 0, 0, tiled=True)
    dl, small = policy_of(groups_all, slots_all, at, scalars, sums, all_stats, logits, inv, targets, old_logp)
    part, half = cols // 4, dl.shape[1] // 2

    dl_o = shift(dl, "c", 1)
    to_x, to_z = heads_of(at, early, late, dl)
    half_z = lax.psum_scatter(to_z, "z", scatter_dimension=0, tiled=False)
    from_x = lax.all_to_all(to_x, "x", 0, 0, tiled=True)
    u0, u1, u2, u3, stay, go = back_of(
        at, after(dl, to_x), dl_o, early, late, small, head, head_o, cols
    )
    u1, u2, u3 = shift(u1, "y", -1), shift(u2, "y", 1), shift(u3, "y", 2)

    to_z = sum_first(from_x, "sum_x")
    half_z = after(half_z, to_z)
    to_z = after(to_z, half_z)
    from_z = lax.all_to_all(to_z, "z", 0, 0, tiled=True)
    half_z = lax.psum_scatter(half_z, "x", scatter_dimension=0, tiled=False)
    u1, u2, u3, _ = lax.optimization_barrier((u1, u2, u3, to_z))
    (grad_hidden,) = simple(
        final_kernel,
        [like(hidden.shape)],
        (u0, u1, u2, u3, hidden, gain.reshape(1, cols), small),
        12 * rows * cols,
        "final",
        200 * 10**9,
    )
    stay, go = stay.reshape(2, -1, 128), go.reshape(2, -1, 128)
    tail = stay + across(go, "y", 1)
    tail = tail[0] + across(tail[1], "y", 2)
    tail = after(tail + across(tail, "x", 1), to_z)
    tail = tail + across(tail, "x", 2)
    for step in (1, -1, 3):
        tail = tail + turn(tail, step)
    (grad_head_t,) = simple(
        join_kernel,
        [like((part, 2 * half), f32)],
        (from_z, half_z),
        2 * from_z.size + 16 * part * half,
        "join",
    )
    tail = tail.reshape(-1)
    return (tail[cols], grad_hidden, tail[:cols] / gain.astype(f32), grad_head_t)


def solution(mesh):
    split = Mesh(mesh.devices.reshape(8, 4, 4, 2), ("z", "x", "y", "c"))
    return jax.shard_map(
        body,
        mesh=split,
        in_specs=(
            P(DP, None, FSDP),
            P(FSDP),
            P(FSDP, None),
            P(DP, None),
            P(DP),
            P(DP, None),
            P(DP),
            P(DP),
        ),
        out_specs=(P(), P(DP, None, FSDP), P(FSDP), P(DP, FSDP)),
        check_vma=False,
    )
```

```python
import functools

import jax
import jax.numpy as jnp
from jax import lax
from jax.experimental import pallas as pl
from jax.experimental.pallas import tpu as pltpu
from jax.sharding import Mesh
from jax.sharding import PartitionSpec as P

GROUP = 8
FSDP = ("y", "c")
DP = ("z", "x")
SIZES = {"z": 8, "x": 4, "y": 4, "c": 2}

eps_norm = 1e-06
clip_low = 0.8
clip_high = 1.2
dual_bound = 3.0

f32, bf16 = jnp.float32, jnp.bfloat16
VMEM = pltpu.VMEM


def shift(value, axis, step):
    n = SIZES[axis]
    return lax.ppermute(value, axis, [(i, (i + step) % n) for i in range(n)])


def turn(value, step):
    return lax.ppermute(
        value, "z", [(i, (i + (step if i % 2 == 0 else -step)) % 8) for i in range(8)]
    )


def params(limit=60 << 20):
    return pltpu.CompilerParams(vmem_limit_bytes=limit)


def cost(flops, nbytes, trans=0):
    return pl.CostEstimate(flops=flops, bytes_accessed=nbytes, transcendentals=trans)


def whole(space=None):
    return pl.BlockSpec(memory_space=space or VMEM)


def like(shape, kind=bf16):
    return jax.ShapeDtypeStruct(shape, kind)


def column(row):
    n = row.shape[1]
    return jnp.transpose(jnp.broadcast_to(row, (128, n)))[:, 0:1]


def rows_of(columns):
    n = columns[0].shape[0]
    lane = lax.broadcasted_iota(jnp.int32, (n, 128), 1)
    table = jnp.zeros((n, 128), f32)
    for k, col in enumerate(columns):
        table = jnp.where(lane == k, col, table)
    return jnp.transpose(table)[0:8, :]


def full(shape):
    return pl.BlockSpec(shape, lambda k, *at: (0,) * len(shape))


def local_kernel(groups, rewards, lengths, slots, out):
    lane = lax.broadcasted_iota(jnp.int32, (1, 128), 1)
    row = jnp.zeros((1, 128), f32)
    for r in range(2):
        row += jnp.where(lane == slots[r] // GROUP, rewards[r], 0.0)
        row += jnp.where(lane == groups, lengths[r].astype(f32), 0.0)
    for k in range(out.shape[0]):
        out[k] = row


def logits_kernel(count, per, last, at, *refs):
    pieces = refs[: count * per * 2]
    refs = refs[count * per * 2 :]
    if last:
        acc_in, sq_in, tgt = refs[:3]
        refs = refs[3:]
    head, hb = refs[:2]
    outs, (slot, acc, sq, sem) = refs[2:-4], refs[-4:]
    j = pl.program_id(0)
    rows = acc.shape[0]
    cols = slot.shape[2] // 2

    @pl.when(j == 0)
    def _():
        copies = []
        for k, piece in enumerate(pieces):
            first = 0 if k % per == 0 else pieces[k - 1].shape[0]
            side = lax.rem(at[2] + (k // per) % 2, 2)
            lanes = pl.ds(pl.multiple_of(side * cols, cols), cols)
            place = slot.at[k // (2 * per), pl.ds(first, piece.shape[0]), lanes]
            copies.append(pltpu.make_async_copy(piece, place, sem.at[k]))
        for copy in copies:
            copy.start()
        if last:
            acc[...] = acc_in[...]
            sq[...] = column(sq_in[0:1, :])
        else:
            acc[...] = jnp.zeros_like(acc)
            sq[...] = jnp.zeros_like(sq)
        for copy in copies:
            copy.wait()

    gain = slot[j, 0:16, :][0:1, :].astype(f32)
    raw = slot[j, 16 : 16 + rows, :].astype(f32)
    sq[...] += jnp.sum(raw * raw, axis=1, keepdims=True)
    scaled = (raw * gain).astype(bf16)
    hb[0] = scaled
    acc[...] += lax.dot_general(
        scaled, head[...], (((1,), (1,)), ((), ())), preferred_element_type=f32
    )

    @pl.when(j == count - 1)
    def _():
        if not last:
            outs[0][...] = acc[...]
            outs[1][...] = rows_of([sq[...]])
            return
        lg, st, inv_ref = outs
        inv_c = lax.rsqrt(sq[...] / 5120.0 + eps_norm)
        inv_ref[...] = rows_of([inv_c])
        logits = acc[...] * inv_c
        lg[...] = logits
        half = logits.shape[1]
        entry = lax.broadcasted_iota(jnp.int32, logits.shape, 1) + at[0] * half
        target = column(tgt[...].astype(f32)).astype(jnp.int32)
        top = jnp.max(logits, axis=1, keepdims=True)
        power = jnp.exp(logits - top)
        found = rows_of(
            [
                top,
                jnp.sum(power, axis=1, keepdims=True),
                jnp.sum(power * logits, axis=1, keepdims=True),
                jnp.sum(jnp.where(entry == target, logits, 0.0), axis=1, keepdims=True),
            ]
        )
        for k in range(st.shape[0]):
            st[k] = found


def logits_of(at, first, blocks, head, before=None, targets=None):
    count, per = len(blocks), len(blocks[0]) // 2
    last = before is not None
    half = head.shape[0]
    cols = 2 * blocks[0][0].shape[1]
    height = sum(p.shape[0] for p in blocks[0]) // 2
    rows = height - 16
    anywhere = pl.BlockSpec(memory_space=pl.ANY)
    shapes = [like((count, rows, cols))]
    specs = [pl.BlockSpec((1, rows, cols), lambda j, *a: (j, 0, 0))]
    shapes += [like((rows, half), f32)]
    shapes += [like((8, 8, rows), f32)] if last else []
    shapes += [like((8, rows), f32)]
    extra = (*before, targets) if last else ()
    return pl.pallas_call(
        functools.partial(logits_kernel, count, per, last),
        out_shape=shapes,
        grid_spec=pltpu.PrefetchScalarGridSpec(
            num_scalar_prefetch=1,
            grid=(count,),
            in_specs=[anywhere] * (count * per * 2)
            + [full(e.shape) for e in extra]
            + [pl.BlockSpec((half, cols), lambda j, at: (0, at[8 + first + j]))],
            out_specs=specs + [full(s.shape) for s in shapes[1:]],
            scratch_shapes=[
                VMEM((count, height, cols), bf16),
                VMEM((rows, half), f32),
                VMEM((rows, 1), f32),
                pltpu.SemaphoreType.DMA((count * per * 2,)),
            ],
        ),
        compiler_params=params(),
        cost_estimate=cost(1000, 1000),
        name="logits_last" if last else "logits_first",
    )(at, *[p for b in blocks for p in b], *extra, head)


def policy_kernel(groups, slots_all, at, rewards, lengths, slots, sums_ref, st, lg, inv_ref, tgt, old, dl, small):
    half = lg.shape[1]
    rows = lg.shape[0]
    sums = jnp.sum(sums_ref[:, 0, :], axis=0, keepdims=True)
    lane = lax.broadcasted_iota(jnp.int32, sums.shape, 1)

    def entry_of(k):
        return jnp.sum(jnp.where(lane == k, sums, 0.0), axis=1, keepdims=True)

    advs = [rewards[r] - entry_of(slots[r] // GROUP) / GROUP for r in range(2)]
    live = entry_of(groups)
    top = jnp.max(st[:, 0, :], axis=0, keepdims=True)
    weight = jnp.exp(st[:, 0, :] - top)
    total = jnp.sum(st[:, 1, :] * weight, axis=0, keepdims=True)
    moment = jnp.sum(st[:, 2, :] * weight, axis=0, keepdims=True)
    chosen = jnp.sum(st[:, 3, :], axis=0, keepdims=True)
    lse = top + jnp.log(total)
    inv = inv_ref[0:1, :]
    ratio = jnp.exp(chosen - lse - old[...])
    position = lax.broadcasted_iota(jnp.int32, ratio.shape, 1)
    second_one = position >= rows // 2
    adv = jnp.where(second_one, advs[1], advs[0])
    length = jnp.where(second_one, lengths[1].astype(f32), lengths[0].astype(f32))
    within = jnp.where(second_one, position - rows // 2, position).astype(f32)
    mask = jnp.where(within < length, 1.0, 0.0)
    first = ratio * adv
    second = jnp.clip(ratio, clip_low, clip_high) * adv
    policy = -jnp.minimum(first, second)
    policy = jnp.where(adv < 0, jnp.minimum(policy, -dual_bound * adv), policy)
    active = (first <= second) & jnp.logical_not((adv < 0) & (first < dual_bound * adv))
    grad_logp = slots_all / live * mask * jnp.where(active, -first, 0.0)
    kappa = inv * inv * grad_logp * (chosen - moment / total) / 5120.0
    small[...] = jnp.concatenate(
        [kappa, mask * policy / live, jnp.zeros((6, ratio.shape[1]), f32)], axis=0
    )
    lse_c, scale_c = column(lse), column(grad_logp * inv)
    target = column(tgt[...].astype(f32)).astype(jnp.int32)
    entry = lax.broadcasted_iota(jnp.int32, lg.shape, 1) + at[0] * half
    hit = jnp.where(entry == target, 1.0, 0.0)
    dl[...] = (scale_c * (hit - jnp.exp(lg[...] - lse_c))).astype(bf16)


def policy_of(groups, slots_all, at, scalars, sums, stats, logits, inv, targets, old_logp):
    rows, half = logits.shape
    return pl.pallas_call(
        functools.partial(policy_kernel, groups, float(slots_all)),
        out_shape=[like((rows, half)), like((8, rows), f32)],
        in_specs=[whole(pltpu.SMEM)] * 4 + [whole()] * 6,
        out_specs=[whole()] * 2,
        compiler_params=params(),
        cost_estimate=cost(8 * rows * half, 6 * rows * half, rows * half),
        name="policy",
    )(at, *scalars, sums, stats, logits, inv, targets, old_logp)


def back_kernel(at, dl, dl_o, early, late, small, head, head_o, u0, u1, u2, u3, lines):
    j = pl.program_id(0)
    total = jnp.dot(dl[...], head[...], preferred_element_type=f32)
    total += jnp.dot(dl_o[...], head_o[...], preferred_element_type=f32)
    for k, out in enumerate((u0, u1, u2, u3)):

        @pl.when(j == k)
        def _(out=out):
            out[...] = total.astype(bf16)

    scaled = jnp.where(j < 3, early[0], late[0]).astype(f32)
    loss = jnp.sum(small[1:2, :], axis=1, keepdims=True) / 4
    line = jnp.concatenate(
        [jnp.sum(total * scaled, axis=0, keepdims=True), jnp.broadcast_to(loss, (1, 128))], axis=1
    )
    lines[j] = line


def back_of(at, dl, dl_o, early, late, small, head, head_o, cols):
    rows, half = dl.shape
    shapes = [like((rows, cols))] * 4 + [like((4, 1, cols + 128), f32)]
    return pl.pallas_call(
        back_kernel,
        out_shape=shapes,
        grid_spec=pltpu.PrefetchScalarGridSpec(
            num_scalar_prefetch=1,
            grid=(4,),
            in_specs=[full((rows, half))] * 2
            + [
                pl.BlockSpec((1, rows, cols), lambda j, at: (jnp.minimum(j, 2), 0, at[2])),
                pl.BlockSpec((1, rows, cols), lambda j, at: (0, 0, at[2])),
                full(small.shape),
            ]
            + [pl.BlockSpec((half, cols), lambda j, at: (0, 2 * at[8 + j] + at[2]))] * 2,
            out_specs=[full(s.shape) for s in shapes],
        ),
        compiler_params=params(),
        cost_estimate=cost(2 * rows * 8 * cols * half, 32 * rows * cols),
        name="back",
    )(at, dl, dl_o, early, late, small, head, head_o)


def heads_kernel(at, early, late, dl, to_x, to_z):
    j = pl.program_id(0)
    scaled = jnp.where(j < 3, early[0], late[0])
    cols = scaled.shape[1] // 2
    step, half = cols // 4, dl.shape[1] // 2
    got = lax.dot_general(
        scaled, dl[...], (((0,), (0,)), ((), ())), preferred_element_type=f32
    ).astype(bf16)
    for i in range(2):
        place = 2 * at[8 + j] + i
        for k in range(4):
            part = got[i * cols + k * step : i * cols + (k + 1) * step, :]
            to_x[k, place] = part[:, :half]
            to_z[place, k] = part[:, half:]


def heads_of(at, early, late, dl):
    _, rows, cols = early.shape
    half = dl.shape[1]
    step = cols // 8
    shapes = [like((4, 8, step, half // 2)), like((8, 4, step, half // 2))]
    return pl.pallas_call(
        heads_kernel,
        out_shape=shapes,
        grid_spec=pltpu.PrefetchScalarGridSpec(
            num_scalar_prefetch=1,
            grid=(4,),
            in_specs=[
                pl.BlockSpec((1, rows, cols), lambda j, at: (jnp.minimum(j, 2), 0, 0)),
                full(late.shape),
                full((rows, half)),
            ],
            out_specs=[full(s.shape) for s in shapes],
        ),
        compiler_params=params(),
        cost_estimate=cost(2 * rows * 4 * cols * half, 24 * rows * cols),
        name="heads",
    )(at, early, late, dl)


def sum_first_kernel(a, out):
    for k in range(out.shape[0]):
        total = a[0, k].astype(f32)
        for s in range(1, a.shape[0]):
            total = total + a[s, k].astype(f32)
        out[k] = total.astype(out.dtype)


def sum_first(value, name):
    return pl.pallas_call(
        sum_first_kernel,
        out_shape=like(value.shape[1:]),
        in_specs=[whole()],
        out_specs=whole(),
        compiler_params=params(),
        cost_estimate=cost(value.size, 3 * value.size),
        name=name,
    )(value)


def join_kernel(from_z, from_x, out):
    width = from_x.shape[1]
    total = from_z[0].astype(f32)
    for k in range(1, from_z.shape[0]):
        total = total + from_z[k].astype(f32)
    out[:, :width] = total
    out[:, width:] = from_x[...].astype(f32)


def final_kernel(u0, u1, u2, u3, h_ref, g_ref, small, out):
    gain = g_ref[...].astype(f32)
    resp, rows, _ = h_ref.shape
    kappa = column(small[0:1, :])
    for r in range(resp):
        cut = slice(r * rows, (r + 1) * rows)
        u = sum(v[cut, :].astype(f32) for v in (u0, u1, u2, u3))
        h = h_ref[r].astype(f32)
        out[r] = (gain * u - h * kappa[cut, :]).astype(bf16)


def simple(kernel, shapes, ins, nbytes, name, flops=None):
    return pl.pallas_call(
        kernel,
        out_shape=shapes,
        in_specs=[whole(pltpu.SMEM if v.ndim == 1 else VMEM) for v in ins],
        out_specs=[whole()] * len(shapes),
        compiler_params=params(),
        cost_estimate=cost(flops or nbytes // 2, nbytes),
        name=name,
    )(*ins)


def after(value, *first):
    return lax.optimization_barrier((value, *first))[0]


def body(hidden, gain, head, targets, lengths, old_logp, rewards, group_slot):
    resp_here, length_max, cols = hidden.shape
    rows = resp_here * length_max
    x, y, z, c = (lax.axis_index(a) for a in ("x", "y", "z", "c"))
    chips = (y + jnp.array([0, 3, 1, 2], jnp.int32)) % 4
    at = jnp.concatenate([jnp.stack([2 * y + c, y, c, z, x, x, x, x]), chips]).astype(jnp.int32)

    payload = jnp.concatenate(
        [jnp.broadcast_to(gain[None], (16, cols)), hidden.reshape(rows, cols)], axis=0
    )
    cut = 16 + length_max
    prev, following = shift(payload, "y", 1), shift(payload, "y", -1)
    own_o = shift(payload, "c", 1)

    groups_all = resp_here * lax.axis_size(DP) // GROUP
    scalars = (rewards, lengths, group_slot)
    (local,) = simple(
        functools.partial(local_kernel, groups_all),
        [like((lax.axis_size(DP), 1, 128), f32)],
        scalars,
        1 << 14,
        "local",
    )
    sums = lax.all_to_all(local, DP, 0, 0, tiled=True)
    prev, following, sums = lax.optimization_barrier((prev, following, sums))

    far_a, far_b = prev[:cut], following[cut:]
    far_a, far_b, prev, following = lax.optimization_barrier((far_a, far_b, prev, following))
    far_a, far_b = shift(far_a, "y", 1), shift(far_b, "y", -1)
    prev_o, following_o = shift(prev, "c", 1), shift(following, "c", 1)
    early, acc, sq = logits_of(
        at, 0, [(payload, own_o), (prev, prev_o), (following, following_o)], head
    )
    far_a, far_b = after(far_a, acc), after(far_b, acc)
    far_a_o, far_b_o = shift(far_a, "c", 1), shift(far_b, "c", 1)

    slots_all = rows * lax.axis_size(DP)
    targets = targets.reshape(1, rows)
    old_logp = old_logp.reshape(1, rows)

    late, logits, stats, inv = logits_of(
        at, 3, [(far_a, far_b, far_a_o, far_b_o)], head, (acc, sq), targets
    )
    head_o = shift(after(head, logits), "c", 1)
    all_stats = lax.all_to_all(stats, FSDP, 0, 0, tiled=True)
    dl, small = policy_of(groups_all, slots_all, at, scalars, sums, all_stats, logits, inv, targets, old_logp)
    part, half = cols // 4, dl.shape[1] // 2

    dl_o = shift(dl, "c", 1)
    to_x, to_z = heads_of(at, early, late, dl)
    half_z = lax.psum_scatter(to_z, "z", scatter_dimension=0, tiled=False)
    from_x = lax.all_to_all(to_x, "x", 0, 0, tiled=True)
    u0, u1, u2, u3, lines = back_of(
        at, after(dl, to_x), dl_o, early, late, small, head, head_o, cols
    )
    tail = lines[0] + shift(lines[1], "y", -1) + shift(lines[2], "y", 1) + shift(lines[3], "y", 2)
    u1, u2, u3, tail = lax.optimization_barrier((u1, u2, u3, tail))
    u1, u2, u3 = shift(u1, "y", -1), shift(u2, "y", 1), shift(u3, "y", 2)

    for step in (1, -1, 3):
        tail = tail + turn(tail, step)
    from_x = after(from_x, tail)

    to_z = sum_first(from_x, "sum_x")
    half_z = after(half_z, to_z)
    to_z = after(to_z, half_z)
    from_z = lax.all_to_all(to_z, "z", 0, 0, tiled=True)
    half_z = lax.psum_scatter(half_z, "x", scatter_dimension=0, tiled=False)
    u1, u2, u3, _ = lax.optimization_barrier((u1, u2, u3, to_z))
    (grad_hidden,) = simple(
        final_kernel,
        [like(hidden.shape)],
        (u0, u1, u2, u3, hidden, gain.reshape(1, cols), small),
        12 * rows * cols,
        "final",
        200 * 10**9,
    )
    tail = after(tail, grad_hidden)
    tail = tail + shift(tail, "x", 1) + shift(tail, "x", 2) + shift(tail, "x", -1)
    (grad_head_t,) = simple(
        join_kernel,
        [like((part, 2 * half), f32)],
        (from_z, half_z),
        2 * from_z.size + 16 * part * half,
        "join",
    )
    tail = tail.reshape(-1)
    return (tail[cols], grad_hidden, tail[:cols] / gain.astype(f32), grad_head_t)


def solution(mesh):
    split = Mesh(mesh.devices.reshape(8, 4, 4, 2), ("z", "x", "y", "c"))
    return jax.shard_map(
        body,
        mesh=split,
        in_specs=(
            P(DP, None, FSDP),
            P(FSDP),
            P(FSDP, None),
            P(DP, None),
            P(DP),
            P(DP, None),
            P(DP),
            P(DP),
        ),
        out_specs=(P(), P(DP, None, FSDP), P(FSDP), P(DP, FSDP)),
        check_vma=False,
    )
```

```python
import functools

import jax
import jax.numpy as jnp
from jax import lax
from jax.experimental import pallas as pl
from jax.experimental.pallas import tpu as pltpu
from jax.sharding import Mesh
from jax.sharding import PartitionSpec as P

GROUP = 8
FSDP = ("y", "c")
DP = ("z", "x")
SIZES = {"z": 8, "x": 4, "y": 4, "c": 2}

eps_norm = 1e-06
clip_low = 0.8
clip_high = 1.2
dual_bound = 3.0

f32, bf16 = jnp.float32, jnp.bfloat16
VMEM = pltpu.VMEM


def shift(value, axis, step):
    n = SIZES[axis]
    return lax.ppermute(value, axis, [(i, (i + step) % n) for i in range(n)])


def turn(value, step):
    return lax.ppermute(
        value, "z", [(i, (i + (step if i % 2 == 0 else -step)) % 8) for i in range(8)]
    )


def params(limit=60 << 20):
    return pltpu.CompilerParams(vmem_limit_bytes=limit)


def cost(flops, nbytes, trans=0):
    return pl.CostEstimate(flops=flops, bytes_accessed=nbytes, transcendentals=trans)


def whole(space=None):
    return pl.BlockSpec(memory_space=space or VMEM)


def like(shape, kind=bf16):
    return jax.ShapeDtypeStruct(shape, kind)


def column(row):
    n = row.shape[1]
    return jnp.transpose(jnp.broadcast_to(row, (128, n)))[:, 0:1]


def rows_of(columns):
    n = columns[0].shape[0]
    lane = lax.broadcasted_iota(jnp.int32, (n, 128), 1)
    table = jnp.zeros((n, 128), f32)
    for k, col in enumerate(columns):
        table = jnp.where(lane == k, col, table)
    return jnp.transpose(table)[0:8, :]


def full(shape):
    return pl.BlockSpec(shape, lambda k, *at: (0,) * len(shape))


def local_kernel(groups, rewards, lengths, slots, out):
    lane = lax.broadcasted_iota(jnp.int32, (1, 128), 1)
    row = jnp.zeros((1, 128), f32)
    for r in range(2):
        row += jnp.where(lane == slots[r] // GROUP, rewards[r], 0.0)
        row += jnp.where(lane == groups, lengths[r].astype(f32), 0.0)
    for k in range(out.shape[0]):
        out[k] = row


def logits_kernel(count, per, last, at, *refs):
    pieces = refs[: count * per * 2]
    refs = refs[count * per * 2 :]
    if last:
        acc_in, sq_in, tgt = refs[:3]
        refs = refs[3:]
    head, hb = refs[:2]
    outs, (slot, acc, sq, sem) = refs[2:-4], refs[-4:]
    j = pl.program_id(0)
    rows = acc.shape[0]
    cols = slot.shape[2] // 2

    @pl.when(j == 0)
    def _():
        copies = []
        for k, piece in enumerate(pieces):
            first = 0 if k % per == 0 else pieces[k - 1].shape[0]
            side = lax.rem(at[2] + (k // per) % 2, 2)
            lanes = pl.ds(pl.multiple_of(side * cols, cols), cols)
            place = slot.at[k // (2 * per), pl.ds(first, piece.shape[0]), lanes]
            copies.append(pltpu.make_async_copy(piece, place, sem.at[k]))
        for copy in copies:
            copy.start()
        if last:
            acc[...] = acc_in[...]
            sq[...] = column(sq_in[0:1, :])
        else:
            acc[...] = jnp.zeros_like(acc)
            sq[...] = jnp.zeros_like(sq)
        for copy in copies:
            copy.wait()

    gain = slot[j, 0:16, :][0:1, :].astype(f32)
    raw = slot[j, 16 : 16 + rows, :].astype(f32)
    sq[...] += jnp.sum(raw * raw, axis=1, keepdims=True)
    scaled = (raw * gain).astype(bf16)
    hb[0] = scaled
    acc[...] += lax.dot_general(
        scaled, head[...], (((1,), (1,)), ((), ())), preferred_element_type=f32
    )

    @pl.when(j == count - 1)
    def _():
        if not last:
            outs[0][...] = acc[...]
            outs[1][...] = rows_of([sq[...]])
            return
        lg, st, inv_ref = outs
        inv_c = lax.rsqrt(sq[...] / 5120.0 + eps_norm)
        inv_ref[...] = rows_of([inv_c])
        logits = acc[...] * inv_c
        lg[...] = logits
        half = logits.shape[1]
        entry = lax.broadcasted_iota(jnp.int32, logits.shape, 1) + at[0] * half
        target = column(tgt[...].astype(f32)).astype(jnp.int32)
        top = jnp.max(logits, axis=1, keepdims=True)
        power = jnp.exp(logits - top)
        found = rows_of(
            [
                top,
                jnp.sum(power, axis=1, keepdims=True),
                jnp.sum(power * logits, axis=1, keepdims=True),
                jnp.sum(jnp.where(entry == target, logits, 0.0), axis=1, keepdims=True),
            ]
        )
        for k in range(st.shape[0]):
            st[k] = found


def logits_of(at, first, blocks, head, before=None, targets=None):
    count, per = len(blocks), len(blocks[0]) // 2
    last = before is not None
    half = head.shape[0]
    cols = 2 * blocks[0][0].shape[1]
    height = sum(p.shape[0] for p in blocks[0]) // 2
    rows = height - 16
    anywhere = pl.BlockSpec(memory_space=pl.ANY)
    shapes = [like((count, rows, cols))]
    specs = [pl.BlockSpec((1, rows, cols), lambda j, *a: (j, 0, 0))]
    shapes += [like((rows, half), f32)]
    shapes += [like((8, 8, rows), f32)] if last else []
    shapes += [like((8, rows), f32)]
    extra = (*before, targets) if last else ()
    return pl.pallas_call(
        functools.partial(logits_kernel, count, per, last),
        out_shape=shapes,
        grid_spec=pltpu.PrefetchScalarGridSpec(
            num_scalar_prefetch=1,
            grid=(count,),
            in_specs=[anywhere] * (count * per * 2)
            + [full(e.shape) for e in extra]
            + [pl.BlockSpec((half, cols), lambda j, at: (0, at[8 + first + j]))],
            out_specs=specs + [full(s.shape) for s in shapes[1:]],
            scratch_shapes=[
                VMEM((count, height, cols), bf16),
                VMEM((rows, half), f32),
                VMEM((rows, 1), f32),
                pltpu.SemaphoreType.DMA((count * per * 2,)),
            ],
        ),
        compiler_params=params(),
        cost_estimate=cost(1000, 1000),
        name="logits_last" if last else "logits_first",
    )(at, *[p for b in blocks for p in b], *extra, head)


def policy_kernel(groups, slots_all, at, rewards, lengths, slots, sum0, sum1, sum2, sum3, st, lg, inv_ref, tgt, old, dl, small):
    half = lg.shape[1]
    rows = lg.shape[0]
    sums = sum0[...] + sum1[...] + sum2[...] + sum3[...]
    lane = lax.broadcasted_iota(jnp.int32, sums.shape, 1)

    def entry_of(k):
        return jnp.sum(jnp.where(lane == k, sums, 0.0), axis=1, keepdims=True)

    advs = [rewards[r] - entry_of(slots[r] // GROUP) / GROUP for r in range(2)]
    live = entry_of(groups)
    top = jnp.max(st[:, 0, :], axis=0, keepdims=True)
    weight = jnp.exp(st[:, 0, :] - top)
    total = jnp.sum(st[:, 1, :] * weight, axis=0, keepdims=True)
    moment = jnp.sum(st[:, 2, :] * weight, axis=0, keepdims=True)
    chosen = jnp.sum(st[:, 3, :], axis=0, keepdims=True)
    lse = top + jnp.log(total)
    inv = inv_ref[0:1, :]
    ratio = jnp.exp(chosen - lse - old[...])
    position = lax.broadcasted_iota(jnp.int32, ratio.shape, 1)
    second_one = position >= rows // 2
    adv = jnp.where(second_one, advs[1], advs[0])
    length = jnp.where(second_one, lengths[1].astype(f32), lengths[0].astype(f32))
    within = jnp.where(second_one, position - rows // 2, position).astype(f32)
    mask = jnp.where(within < length, 1.0, 0.0)
    first = ratio * adv
    second = jnp.clip(ratio, clip_low, clip_high) * adv
    policy = -jnp.minimum(first, second)
    policy = jnp.where(adv < 0, jnp.minimum(policy, -dual_bound * adv), policy)
    active = (first <= second) & jnp.logical_not((adv < 0) & (first < dual_bound * adv))
    grad_logp = slots_all / live * mask * jnp.where(active, -first, 0.0)
    kappa = inv * inv * grad_logp * (chosen - moment / total) / 5120.0
    small[...] = jnp.concatenate(
        [kappa, mask * policy / live, jnp.zeros((6, ratio.shape[1]), f32)], axis=0
    )
    lse_c, scale_c = column(lse), column(grad_logp * inv)
    target = column(tgt[...].astype(f32)).astype(jnp.int32)
    entry = lax.broadcasted_iota(jnp.int32, lg.shape, 1) + at[0] * half
    hit = jnp.where(entry == target, 1.0, 0.0)
    dl[...] = (scale_c * (hit - jnp.exp(lg[...] - lse_c))).astype(bf16)


def policy_of(groups, slots_all, at, scalars, sums, stats, logits, inv, targets, old_logp):
    rows, half = logits.shape
    return pl.pallas_call(
        functools.partial(policy_kernel, groups, float(slots_all)),
        out_shape=[like((rows, half)), like((8, rows), f32)],
        in_specs=[whole(pltpu.SMEM)] * 4 + [whole()] * 9,
        out_specs=[whole()] * 2,
        compiler_params=params(),
        cost_estimate=cost(8 * rows * half, 6 * rows * half, rows * half),
        name="policy",
    )(at, *scalars, *sums, stats, logits, inv, targets, old_logp)


def back_kernel(at, dl, dl_o, early, late, small, head, head_o, u0, u1, u2, u3, lines):
    j = pl.program_id(0)
    total = jnp.dot(dl[...], head[...], preferred_element_type=f32)
    total += jnp.dot(dl_o[...], head_o[...], preferred_element_type=f32)
    for k, out in enumerate((u0, u1, u2, u3)):

        @pl.when(j == k)
        def _(out=out):
            out[...] = total.astype(bf16)

    scaled = jnp.where(j < 3, early[0], late[0]).astype(f32)
    loss = jnp.sum(small[1:2, :], axis=1, keepdims=True) / 4
    line = jnp.concatenate(
        [jnp.sum(total * scaled, axis=0, keepdims=True), jnp.broadcast_to(loss, (1, 128))], axis=1
    )
    lines[j] = line


def back_of(at, dl, dl_o, early, late, small, head, head_o, cols):
    rows, half = dl.shape
    shapes = [like((rows, cols))] * 4 + [like((4, 1, cols + 128), f32)]
    return pl.pallas_call(
        back_kernel,
        out_shape=shapes,
        grid_spec=pltpu.PrefetchScalarGridSpec(
            num_scalar_prefetch=1,
            grid=(4,),
            in_specs=[full((rows, half))] * 2
            + [
                pl.BlockSpec((1, rows, cols), lambda j, at: (jnp.minimum(j, 2), 0, at[2])),
                pl.BlockSpec((1, rows, cols), lambda j, at: (0, 0, at[2])),
                full(small.shape),
            ]
            + [pl.BlockSpec((half, cols), lambda j, at: (0, 2 * at[8 + j] + at[2]))] * 2,
            out_specs=[full(s.shape) for s in shapes],
        ),
        compiler_params=params(),
        cost_estimate=cost(2 * rows * 8 * cols * half, 32 * rows * cols),
        name="back",
    )(at, dl, dl_o, early, late, small, head, head_o)


def heads_kernel(at, early, late, dl, to_x, to_z):
    j = pl.program_id(0)
    scaled = jnp.where(j < 3, early[0], late[0])
    cols = scaled.shape[1] // 2
    step, half = cols // 4, dl.shape[1] // 2
    got = lax.dot_general(
        scaled, dl[...], (((0,), (0,)), ((), ())), preferred_element_type=f32
    ).astype(bf16)
    for i in range(2):
        place = 2 * at[8 + j] + i
        for k in range(4):
            part = got[i * cols + k * step : i * cols + (k + 1) * step, :]
            to_x[k, place] = part[:, :half]
            to_z[place, k] = part[:, half:]


def heads_of(at, early, late, dl):
    _, rows, cols = early.shape
    half = dl.shape[1]
    step = cols // 8
    shapes = [like((4, 8, step, half // 2)), like((8, 4, step, half // 2))]
    return pl.pallas_call(
        heads_kernel,
        out_shape=shapes,
        grid_spec=pltpu.PrefetchScalarGridSpec(
            num_scalar_prefetch=1,
            grid=(4,),
            in_specs=[
                pl.BlockSpec((1, rows, cols), lambda j, at: (jnp.minimum(j, 2), 0, 0)),
                full(late.shape),
                full((rows, half)),
            ],
            out_specs=[full(s.shape) for s in shapes],
        ),
        compiler_params=params(),
        cost_estimate=cost(2 * rows * 4 * cols * half, 24 * rows * cols),
        name="heads",
    )(at, early, late, dl)


def sum_first_kernel(a, out):
    for k in range(out.shape[0]):
        total = a[0, k].astype(f32)
        for s in range(1, a.shape[0]):
            total = total + a[s, k].astype(f32)
        out[k] = total.astype(out.dtype)


def sum_first(value, name):
    return pl.pallas_call(
        sum_first_kernel,
        out_shape=like(value.shape[1:]),
        in_specs=[whole()],
        out_specs=whole(),
        compiler_params=params(),
        cost_estimate=cost(value.size, 3 * value.size),
        name=name,
    )(value)


def join_kernel(from_z, from_x, out):
    width = from_x.shape[1]
    total = from_z[0].astype(f32)
    for k in range(1, from_z.shape[0]):
        total = total + from_z[k].astype(f32)
    out[:, :width] = total
    out[:, width:] = from_x[...].astype(f32)


def final_kernel(u0, u1, u2, u3, h_ref, g_ref, small, out):
    gain = g_ref[...].astype(f32)
    resp, rows, _ = h_ref.shape
    kappa = column(small[0:1, :])
    for r in range(resp):
        cut = slice(r * rows, (r + 1) * rows)
        u = sum(v[cut, :].astype(f32) for v in (u0, u1, u2, u3))
        h = h_ref[r].astype(f32)
        out[r] = (gain * u - h * kappa[cut, :]).astype(bf16)


def simple(kernel, shapes, ins, nbytes, name, flops=None):
    return pl.pallas_call(
        kernel,
        out_shape=shapes,
        in_specs=[whole(pltpu.SMEM if v.ndim == 1 else VMEM) for v in ins],
        out_specs=[whole()] * len(shapes),
        compiler_params=params(),
        cost_estimate=cost(flops or nbytes // 2, nbytes),
        name=name,
    )(*ins)


def after(value, *first):
    return lax.optimization_barrier((value, *first))[0]


def body(hidden, gain, head, targets, lengths, old_logp, rewards, group_slot):
    resp_here, length_max, cols = hidden.shape
    rows = resp_here * length_max
    x, y, z, c = (lax.axis_index(a) for a in ("x", "y", "z", "c"))
    chips = (y + jnp.array([0, 3, 1, 2], jnp.int32)) % 4
    at = jnp.concatenate([jnp.stack([2 * y + c, y, c, z, x, x, x, x]), chips]).astype(jnp.int32)

    payload = jnp.concatenate(
        [jnp.broadcast_to(gain[None], (16, cols)), hidden.reshape(rows, cols)], axis=0
    )
    cut = 16 + length_max
    prev, following = shift(payload, "y", 1), shift(payload, "y", -1)
    own_o = shift(payload, "c", 1)

    groups_all = resp_here * lax.axis_size(DP) // GROUP
    scalars = (rewards, lengths, group_slot)
    (local,) = simple(
        functools.partial(local_kernel, groups_all),
        [like((lax.axis_size("z"), 1, 128), f32)],
        scalars,
        1 << 14,
        "local",
    )
    over_z = lax.all_to_all(local, "z", 0, 0, tiled=True).sum(axis=0)
    prev, following, over_z = lax.optimization_barrier((prev, following, over_z))

    far_a, far_b = prev[:cut], following[cut:]
    far_a, far_b, prev, following = lax.optimization_barrier((far_a, far_b, prev, following))
    far_a, far_b = shift(far_a, "y", 1), shift(far_b, "y", -1)
    prev_o, following_o = shift(prev, "c", 1), shift(following, "c", 1)
    early, acc, sq = logits_of(
        at, 0, [(payload, own_o), (prev, prev_o), (following, following_o)], head
    )
    far_a, far_b = after(far_a, acc), after(far_b, acc)
    far_a_o, far_b_o = shift(far_a, "c", 1), shift(far_b, "c", 1)

    slots_all = rows * lax.axis_size(DP)
    targets = targets.reshape(1, rows)
    old_logp = old_logp.reshape(1, rows)

    late, logits, stats, inv = logits_of(
        at, 3, [(far_a, far_b, far_a_o, far_b_o)], head, (acc, sq), targets
    )
    head_o = shift(after(head, logits), "c", 1)
    over_z = after(over_z, logits)
    sums = (over_z, shift(over_z, "x", 1), shift(over_z, "x", 2), shift(over_z, "x", -1))
    all_stats = lax.all_to_all(stats, FSDP, 0, 0, tiled=True)
    dl, small = policy_of(groups_all, slots_all, at, scalars, sums, all_stats, logits, inv, targets, old_logp)
    part, half = cols // 4, dl.shape[1] // 2

    dl_o = shift(dl, "c", 1)
    to_x, to_z = heads_of(at, early, late, dl)
    half_z = lax.psum_scatter(to_z, "z", scatter_dimension=0, tiled=False)
    from_x = lax.all_to_all(to_x, "x", 0, 0, tiled=True)
    u0, u1, u2, u3, lines = back_of(
        at, after(dl, to_x), dl_o, early, late, small, head, head_o, cols
    )
    u1, u2, u3 = shift(u1, "y", -1), shift(u2, "y", 1), shift(u3, "y", 2)

    for step in (1, -1, 3):
        lines = lines + turn(lines, step)
    lines = lines + shift(lines, "x", 1) + shift(lines, "x", 2) + shift(lines, "x", -1)
    from_x = after(from_x, lines)

    to_z = sum_first(from_x, "sum_x")
    half_z = after(half_z, to_z)
    to_z = after(to_z, half_z)
    from_z = lax.all_to_all(to_z, "z", 0, 0, tiled=True)
    half_z = lax.psum_scatter(half_z, "x", scatter_dimension=0, tiled=False)
    u1, u2, u3, _ = lax.optimization_barrier((u1, u2, u3, to_z))
    (grad_hidden,) = simple(
        final_kernel,
        [like(hidden.shape)],
        (u0, u1, u2, u3, hidden, gain.reshape(1, cols), small),
        12 * rows * cols,
        "final",
        200 * 10**9,
    )
    lines = after(lines, grad_hidden)
    tail = lines[0] + shift(lines[1], "y", -1) + shift(lines[2], "y", 1) + shift(lines[3], "y", 2)
    (grad_head_t,) = simple(
        join_kernel,
        [like((part, 2 * half), f32)],
        (from_z, half_z),
        2 * from_z.size + 16 * part * half,
        "join",
    )
    tail = tail.reshape(-1)
    return (tail[cols], grad_hidden, tail[:cols] / gain.astype(f32), grad_head_t)


def solution(mesh):
    split = Mesh(mesh.devices.reshape(8, 4, 4, 2), ("z", "x", "y", "c"))
    return jax.shard_map(
        body,
        mesh=split,
        in_specs=(
            P(DP, None, FSDP),
            P(FSDP),
            P(FSDP, None),
            P(DP, None),
            P(DP),
            P(DP, None),
            P(DP),
            P(DP),
        ),
        out_specs=(P(), P(DP, None, FSDP), P(FSDP), P(DP, FSDP)),
        check_vma=False,
    )
```

```python
import functools

import jax
import jax.numpy as jnp
from jax import lax
from jax.experimental import pallas as pl
from jax.experimental.pallas import tpu as pltpu
from jax.sharding import Mesh
from jax.sharding import PartitionSpec as P

GROUP = 8
FSDP = ("y", "c")
DP = ("z", "x")
SIZES = {"z": 8, "x": 4, "y": 4, "c": 2}

eps_norm = 1e-06
clip_low = 0.8
clip_high = 1.2
dual_bound = 3.0

f32, bf16 = jnp.float32, jnp.bfloat16
VMEM = pltpu.VMEM


def shift(value, axis, step):
    n = SIZES[axis]
    return lax.ppermute(value, axis, [(i, (i + step) % n) for i in range(n)])


def turn(value, step):
    return lax.ppermute(
        value, "z", [(i, (i + (step if i % 2 == 0 else -step)) % 8) for i in range(8)]
    )


def params(limit=60 << 20):
    return pltpu.CompilerParams(vmem_limit_bytes=limit)


def cost(flops, nbytes, trans=0):
    return pl.CostEstimate(flops=flops, bytes_accessed=nbytes, transcendentals=trans)


def whole(space=None):
    return pl.BlockSpec(memory_space=space or VMEM)


def like(shape, kind=bf16):
    return jax.ShapeDtypeStruct(shape, kind)


def column(row):
    n = row.shape[1]
    return jnp.transpose(jnp.broadcast_to(row, (128, n)))[:, 0:1]


def rows_of(columns):
    n = columns[0].shape[0]
    lane = lax.broadcasted_iota(jnp.int32, (n, 128), 1)
    table = jnp.zeros((n, 128), f32)
    for k, col in enumerate(columns):
        table = jnp.where(lane == k, col, table)
    return jnp.transpose(table)[0:8, :]


def full(shape):
    return pl.BlockSpec(shape, lambda k, *at: (0,) * len(shape))


def local_kernel(groups, rewards, lengths, slots, out):
    lane = lax.broadcasted_iota(jnp.int32, (1, 128), 1)
    row = jnp.zeros((1, 128), f32)
    for r in range(2):
        row += jnp.where(lane == slots[r] // GROUP, rewards[r], 0.0)
        row += jnp.where(lane == groups, lengths[r].astype(f32), 0.0)
    for k in range(out.shape[0]):
        out[k] = row


def logits_kernel(count, per, last, at, *refs):
    pieces = refs[: count * per * 2]
    refs = refs[count * per * 2 :]
    if last:
        acc_in, sq_in, tgt = refs[:3]
        refs = refs[3:]
    head, hb = refs[:2]
    outs, (slot, acc, sq, sem) = refs[2:-4], refs[-4:]
    j = pl.program_id(0)
    rows = acc.shape[0]
    cols = slot.shape[2] // 2

    @pl.when(j == 0)
    def _():
        copies = []
        for k, piece in enumerate(pieces):
            first = 0 if k % per == 0 else pieces[k - 1].shape[0]
            side = lax.rem(at[2] + (k // per) % 2, 2)
            lanes = pl.ds(pl.multiple_of(side * cols, cols), cols)
            place = slot.at[k // (2 * per), pl.ds(first, piece.shape[0]), lanes]
            copies.append(pltpu.make_async_copy(piece, place, sem.at[k]))
        for copy in copies:
            copy.start()
        if last:
            acc[...] = acc_in[...]
            sq[...] = column(sq_in[0:1, :])
        else:
            acc[...] = jnp.zeros_like(acc)
            sq[...] = jnp.zeros_like(sq)
        for copy in copies:
            copy.wait()

    gain = slot[j, 0:16, :][0:1, :].astype(f32)
    raw = slot[j, 16 : 16 + rows, :].astype(f32)
    sq[...] += jnp.sum(raw * raw, axis=1, keepdims=True)
    scaled = (raw * gain).astype(bf16)
    hb[0] = scaled
    acc[...] += lax.dot_general(
        scaled, head[...], (((1,), (1,)), ((), ())), preferred_element_type=f32
    )

    @pl.when(j == count - 1)
    def _():
        if not last:
            outs[0][...] = acc[...]
            outs[1][...] = rows_of([sq[...]])
            return
        lg, st, inv_ref = outs
        inv_c = lax.rsqrt(sq[...] / 5120.0 + eps_norm)
        inv_ref[...] = rows_of([inv_c])
        logits = acc[...] * inv_c
        lg[...] = logits
        half = logits.shape[1]
        entry = lax.broadcasted_iota(jnp.int32, logits.shape, 1) + at[0] * half
        target = column(tgt[...].astype(f32)).astype(jnp.int32)
        top = jnp.max(logits, axis=1, keepdims=True)
        power = jnp.exp(logits - top)
        found = rows_of(
            [
                top,
                jnp.sum(power, axis=1, keepdims=True),
                jnp.sum(power * logits, axis=1, keepdims=True),
                jnp.sum(jnp.where(entry == target, logits, 0.0), axis=1, keepdims=True),
            ]
        )
        for k in range(st.shape[0]):
            st[k] = found


def logits_of(at, first, blocks, head, before=None, targets=None):
    count, per = len(blocks), len(blocks[0]) // 2
    last = before is not None
    half = head.shape[0]
    cols = 2 * blocks[0][0].shape[1]
    height = sum(p.shape[0] for p in blocks[0]) // 2
    rows = height - 16
    anywhere = pl.BlockSpec(memory_space=pl.ANY)
    shapes = [like((count, rows, cols))]
    specs = [pl.BlockSpec((1, rows, cols), lambda j, *a: (j, 0, 0))]
    shapes += [like((rows, half), f32)]
    shapes += [like((8, 8, rows), f32)] if last else []
    shapes += [like((8, rows), f32)]
    extra = (*before, targets) if last else ()
    return pl.pallas_call(
        functools.partial(logits_kernel, count, per, last),
        out_shape=shapes,
        grid_spec=pltpu.PrefetchScalarGridSpec(
            num_scalar_prefetch=1,
            grid=(count,),
            in_specs=[anywhere] * (count * per * 2)
            + [full(e.shape) for e in extra]
            + [pl.BlockSpec((half, cols), lambda j, at: (0, at[8 + first + j]))],
            out_specs=specs + [full(s.shape) for s in shapes[1:]],
            scratch_shapes=[
                VMEM((count, height, cols), bf16),
                VMEM((rows, half), f32),
                VMEM((rows, 1), f32),
                pltpu.SemaphoreType.DMA((count * per * 2,)),
            ],
        ),
        compiler_params=params(),
        cost_estimate=cost(1000, 1000),
        name="logits_last" if last else "logits_first",
    )(at, *[p for b in blocks for p in b], *extra, head)


def policy_kernel(groups, slots_all, at, rewards, lengths, slots, sum0, sum1, sum2, sum3, st, lg, inv_ref, tgt, old, dl, small):
    half = lg.shape[1]
    rows = lg.shape[0]
    sums = sum0[...] + sum1[...] + sum2[...] + sum3[...]
    lane = lax.broadcasted_iota(jnp.int32, sums.shape, 1)

    def entry_of(k):
        return jnp.sum(jnp.where(lane == k, sums, 0.0), axis=1, keepdims=True)

    advs = [rewards[r] - entry_of(slots[r] // GROUP) / GROUP for r in range(2)]
    live = entry_of(groups)
    top = jnp.max(st[:, 0, :], axis=0, keepdims=True)
    weight = jnp.exp(st[:, 0, :] - top)
    total = jnp.sum(st[:, 1, :] * weight, axis=0, keepdims=True)
    moment = jnp.sum(st[:, 2, :] * weight, axis=0, keepdims=True)
    chosen = jnp.sum(st[:, 3, :], axis=0, keepdims=True)
    lse = top + jnp.log(total)
    inv = inv_ref[0:1, :]
    ratio = jnp.exp(chosen - lse - old[...])
    position = lax.broadcasted_iota(jnp.int32, ratio.shape, 1)
    second_one = position >= rows // 2
    adv = jnp.where(second_one, advs[1], advs[0])
    length = jnp.where(second_one, lengths[1].astype(f32), lengths[0].astype(f32))
    within = jnp.where(second_one, position - rows // 2, position).astype(f32)
    mask = jnp.where(within < length, 1.0, 0.0)
    first = ratio * adv
    second = jnp.clip(ratio, clip_low, clip_high) * adv
    policy = -jnp.minimum(first, second)
    policy = jnp.where(adv < 0, jnp.minimum(policy, -dual_bound * adv), policy)
    active = (first <= second) & jnp.logical_not((adv < 0) & (first < dual_bound * adv))
    grad_logp = slots_all / live * mask * jnp.where(active, -first, 0.0)
    kappa = inv * inv * grad_logp * (chosen - moment / total) / 5120.0
    small[...] = jnp.concatenate(
        [kappa, mask * policy / live, jnp.zeros((6, ratio.shape[1]), f32)], axis=0
    )
    lse_c, scale_c = column(lse), column(grad_logp * inv)
    target = column(tgt[...].astype(f32)).astype(jnp.int32)
    entry = lax.broadcasted_iota(jnp.int32, lg.shape, 1) + at[0] * half
    hit = jnp.where(entry == target, 1.0, 0.0)
    dl[...] = (scale_c * (hit - jnp.exp(lg[...] - lse_c))).astype(bf16)


def policy_of(groups, slots_all, at, scalars, sums, stats, logits, inv, targets, old_logp):
    rows, half = logits.shape
    return pl.pallas_call(
        functools.partial(policy_kernel, groups, float(slots_all)),
        out_shape=[like((rows, half)), like((8, rows), f32)],
        in_specs=[whole(pltpu.SMEM)] * 4 + [whole()] * 9,
        out_specs=[whole()] * 2,
        compiler_params=params(),
        cost_estimate=cost(8 * rows * half, 6 * rows * half, rows * half),
        name="policy",
    )(at, *scalars, *sums, stats, logits, inv, targets, old_logp)


def back_kernel(at, dl, dl_o, early, late, small, head, head_o, u0, u1, u2, u3, lines):
    j = pl.program_id(0)
    total = jnp.dot(dl[...], head[...], preferred_element_type=f32)
    total += jnp.dot(dl_o[...], head_o[...], preferred_element_type=f32)
    for k, out in enumerate((u0, u1, u2, u3)):

        @pl.when(j == k)
        def _(out=out):
            out[...] = total.astype(bf16)

    scaled = jnp.where(j < 3, early[0], late[0]).astype(f32)
    loss = jnp.sum(small[1:2, :], axis=1, keepdims=True) / 4
    line = jnp.concatenate(
        [jnp.sum(total * scaled, axis=0, keepdims=True), jnp.broadcast_to(loss, (1, 128))], axis=1
    )
    lines[j] = line


def back_of(at, dl, dl_o, early, late, small, head, head_o, cols):
    rows, half = dl.shape
    shapes = [like((rows, cols))] * 4 + [like((4, 1, cols + 128), f32)]
    return pl.pallas_call(
        back_kernel,
        out_shape=shapes,
        grid_spec=pltpu.PrefetchScalarGridSpec(
            num_scalar_prefetch=1,
            grid=(4,),
            in_specs=[full((rows, half))] * 2
            + [
                pl.BlockSpec((1, rows, cols), lambda j, at: (jnp.minimum(j, 2), 0, at[2])),
                pl.BlockSpec((1, rows, cols), lambda j, at: (0, 0, at[2])),
                full(small.shape),
            ]
            + [pl.BlockSpec((half, cols), lambda j, at: (0, 2 * at[8 + j] + at[2]))] * 2,
            out_specs=[full(s.shape) for s in shapes],
        ),
        compiler_params=params(),
        cost_estimate=cost(2 * rows * 8 * cols * half, 32 * rows * cols),
        name="back",
    )(at, dl, dl_o, early, late, small, head, head_o)


def heads_kernel(at, early, late, dl, to_x, to_z):
    j = pl.program_id(0)
    scaled = jnp.where(j < 3, early[0], late[0])
    cols = scaled.shape[1] // 2
    step, half = cols // 4, dl.shape[1] // 2
    got = lax.dot_general(
        scaled, dl[...], (((0,), (0,)), ((), ())), preferred_element_type=f32
    ).astype(bf16)
    for i in range(2):
        place = 2 * at[8 + j] + i
        for k in range(4):
            part = got[i * cols + k * step : i * cols + (k + 1) * step, :]
            to_x[k, place] = part[:, :half]
            to_z[place, k] = part[:, half:]


def heads_of(at, early, late, dl):
    _, rows, cols = early.shape
    half = dl.shape[1]
    step = cols // 8
    shapes = [like((4, 8, step, half // 2)), like((8, 4, step, half // 2))]
    return pl.pallas_call(
        heads_kernel,
        out_shape=shapes,
        grid_spec=pltpu.PrefetchScalarGridSpec(
            num_scalar_prefetch=1,
            grid=(4,),
            in_specs=[
                pl.BlockSpec((1, rows, cols), lambda j, at: (jnp.minimum(j, 2), 0, 0)),
                full(late.shape),
                full((rows, half)),
            ],
            out_specs=[full(s.shape) for s in shapes],
        ),
        compiler_params=params(),
        cost_estimate=cost(2 * rows * 4 * cols * half, 24 * rows * cols),
        name="heads",
    )(at, early, late, dl)


def sum_first_kernel(a, out):
    for k in range(out.shape[0]):
        total = a[0, k].astype(f32)
        for s in range(1, a.shape[0]):
            total = total + a[s, k].astype(f32)
        out[k] = total.astype(out.dtype)


def sum_first(value, name):
    return pl.pallas_call(
        sum_first_kernel,
        out_shape=like(value.shape[1:]),
        in_specs=[whole()],
        out_specs=whole(),
        compiler_params=params(),
        cost_estimate=cost(value.size, 3 * value.size),
        name=name,
    )(value)


def join_kernel(from_z, from_x, out):
    width = from_x.shape[1]
    total = from_z[0].astype(f32)
    for k in range(1, from_z.shape[0]):
        total = total + from_z[k].astype(f32)
    out[:, :width] = total
    out[:, width:] = from_x[...].astype(f32)


def final_kernel(u0, u1, u2, u3, h_ref, g_ref, small, out):
    gain = g_ref[...].astype(f32)
    resp, rows, _ = h_ref.shape
    kappa = column(small[0:1, :])
    for r in range(resp):
        cut = slice(r * rows, (r + 1) * rows)
        u = sum(v[cut, :].astype(f32) for v in (u0, u1, u2, u3))
        h = h_ref[r].astype(f32)
        out[r] = (gain * u - h * kappa[cut, :]).astype(bf16)


def simple(kernel, shapes, ins, nbytes, name, flops=None):
    return pl.pallas_call(
        kernel,
        out_shape=shapes,
        in_specs=[whole(pltpu.SMEM if v.ndim == 1 else VMEM) for v in ins],
        out_specs=[whole()] * len(shapes),
        compiler_params=params(),
        cost_estimate=cost(flops or nbytes // 2, nbytes),
        name=name,
    )(*ins)


def after(value, *first):
    return lax.optimization_barrier((value, *first))[0]


def body(hidden, gain, head, targets, lengths, old_logp, rewards, group_slot):
    resp_here, length_max, cols = hidden.shape
    rows = resp_here * length_max
    x, y, z, c = (lax.axis_index(a) for a in ("x", "y", "z", "c"))
    chips = (y + jnp.array([0, 3, 1, 2], jnp.int32)) % 4
    at = jnp.concatenate([jnp.stack([2 * y + c, y, c, z, x, x, x, x]), chips]).astype(jnp.int32)

    payload = jnp.concatenate(
        [jnp.broadcast_to(gain[None], (16, cols)), hidden.reshape(rows, cols)], axis=0
    )
    cut = 16 + length_max
    prev, following = shift(payload, "y", 1), shift(payload, "y", -1)
    own_o = shift(payload, "c", 1)

    groups_all = resp_here * lax.axis_size(DP) // GROUP
    scalars = (rewards, lengths, group_slot)
    (local,) = simple(
        functools.partial(local_kernel, groups_all),
        [like((lax.axis_size("z"), 1, 128), f32)],
        scalars,
        1 << 14,
        "local",
    )
    over_z = lax.all_to_all(local, "z", 0, 0, tiled=True).sum(axis=0)
    prev, following, over_z = lax.optimization_barrier((prev, following, over_z))

    far_a, far_b = prev[:cut], following[cut:]
    far_a, far_b, prev, following = lax.optimization_barrier((far_a, far_b, prev, following))
    far_a, far_b = shift(far_a, "y", 1), shift(far_b, "y", -1)
    prev_o, following_o = shift(prev, "c", 1), shift(following, "c", 1)
    early, acc, sq = logits_of(
        at, 0, [(payload, own_o), (prev, prev_o), (following, following_o)], head
    )
    far_a, far_b = after(far_a, acc), after(far_b, acc)
    far_a_o, far_b_o = shift(far_a, "c", 1), shift(far_b, "c", 1)

    slots_all = rows * lax.axis_size(DP)
    targets = targets.reshape(1, rows)
    old_logp = old_logp.reshape(1, rows)

    late, logits, stats, inv = logits_of(
        at, 3, [(far_a, far_b, far_a_o, far_b_o)], head, (acc, sq), targets
    )
    head_o = shift(after(head, logits), "c", 1)
    over_z = after(over_z, logits)
    sums = (over_z, shift(over_z, "x", 1), shift(over_z, "x", 2), shift(over_z, "x", -1))
    all_stats = lax.all_to_all(stats, FSDP, 0, 0, tiled=True)
    dl, small = policy_of(groups_all, slots_all, at, scalars, sums, all_stats, logits, inv, targets, old_logp)
    part, half = cols // 4, dl.shape[1] // 2

    dl_o = shift(dl, "c", 1)
    to_x, to_z = heads_of(at, early, late, dl)
    half_z = lax.psum_scatter(to_z, "z", scatter_dimension=0, tiled=False)
    from_x = lax.all_to_all(to_x, "x", 0, 0, tiled=True)
    u0, u1, u2, u3, lines = back_of(
        at, after(dl, to_x), dl_o, early, late, small, head, head_o, cols
    )
    tail = lines[0] + shift(lines[1], "y", -1) + shift(lines[2], "y", 1) + shift(lines[3], "y", 2)
    u1, u2, u3, tail = lax.optimization_barrier((u1, u2, u3, tail))
    u1, u2, u3 = shift(u1, "y", -1), shift(u2, "y", 1), shift(u3, "y", 2)

    for step in (1, -1, 3):
        tail = tail + turn(tail, step)
    from_x = after(from_x, tail)

    to_z = sum_first(from_x, "sum_x")
    half_z = after(half_z, to_z)
    to_z = after(to_z, half_z)
    from_z = lax.all_to_all(to_z, "z", 0, 0, tiled=True)
    half_z = lax.psum_scatter(half_z, "x", scatter_dimension=0, tiled=False)
    u1, u2, u3, _ = lax.optimization_barrier((u1, u2, u3, to_z))
    (grad_hidden,) = simple(
        final_kernel,
        [like(hidden.shape)],
        (u0, u1, u2, u3, hidden, gain.reshape(1, cols), small),
        12 * rows * cols,
        "final",
        200 * 10**9,
    )
    tail = after(tail, grad_hidden)
    tail = tail + shift(tail, "x", 1) + shift(tail, "x", 2) + shift(tail, "x", -1)
    (grad_head_t,) = simple(
        join_kernel,
        [like((part, 2 * half), f32)],
        (from_z, half_z),
        2 * from_z.size + 16 * part * half,
        "join",
    )
    tail = tail.reshape(-1)
    return (tail[cols], grad_hidden, tail[:cols] / gain.astype(f32), grad_head_t)


def solution(mesh):
    split = Mesh(mesh.devices.reshape(8, 4, 4, 2), ("z", "x", "y", "c"))
    return jax.shard_map(
        body,
        mesh=split,
        in_specs=(
            P(DP, None, FSDP),
            P(FSDP),
            P(FSDP, None),
            P(DP, None),
            P(DP),
            P(DP, None),
            P(DP),
            P(DP),
        ),
        out_specs=(P(), P(DP, None, FSDP), P(FSDP), P(DP, FSDP)),
        check_vma=False,
    )
```

```python
import functools

import jax
import jax.numpy as jnp
from jax import lax
from jax.experimental import pallas as pl
from jax.experimental.pallas import tpu as pltpu
from jax.sharding import Mesh
from jax.sharding import PartitionSpec as P

GROUP = 8
FSDP = ("y", "c")
DP = ("z", "x")
SIZES = {"z": 8, "x": 4, "y": 4, "c": 2}

eps_norm = 1e-06
clip_low = 0.8
clip_high = 1.2
dual_bound = 3.0

f32, bf16 = jnp.float32, jnp.bfloat16
VMEM = pltpu.VMEM


def shift(value, axis, step):
    n = SIZES[axis]
    return lax.ppermute(value, axis, [(i, (i + step) % n) for i in range(n)])


def turn(value, step):
    return lax.ppermute(
        value, "z", [(i, (i + (step if i % 2 == 0 else -step)) % 8) for i in range(8)]
    )


def params(limit=60 << 20):
    return pltpu.CompilerParams(vmem_limit_bytes=limit)


def cost(flops, nbytes, trans=0):
    return pl.CostEstimate(flops=flops, bytes_accessed=nbytes, transcendentals=trans)


def whole(space=None):
    return pl.BlockSpec(memory_space=space or VMEM)


def like(shape, kind=bf16):
    return jax.ShapeDtypeStruct(shape, kind)


def column(row):
    n = row.shape[1]
    return jnp.transpose(jnp.broadcast_to(row, (128, n)))[:, 0:1]


def rows_of(columns):
    n = columns[0].shape[0]
    lane = lax.broadcasted_iota(jnp.int32, (n, 128), 1)
    table = jnp.zeros((n, 128), f32)
    for k, col in enumerate(columns):
        table = jnp.where(lane == k, col, table)
    return jnp.transpose(table)[0:8, :]


def full(shape):
    return pl.BlockSpec(shape, lambda k, *at: (0,) * len(shape))


def local_kernel(groups, rewards, lengths, slots, out):
    lane = lax.broadcasted_iota(jnp.int32, (1, 128), 1)
    row = jnp.zeros((1, 128), f32)
    for r in range(2):
        row += jnp.where(lane == slots[r] // GROUP, rewards[r], 0.0)
        row += jnp.where(lane == groups, lengths[r].astype(f32), 0.0)
    for k in range(out.shape[0]):
        out[k] = row


def logits_kernel(count, per, last, at, *refs):
    pieces = refs[: count * per * 2]
    refs = refs[count * per * 2 :]
    if last:
        acc_in, sq_in, tgt = refs[:3]
        refs = refs[3:]
    head, hb = refs[:2]
    outs, (slot, acc, sq, sem) = refs[2:-4], refs[-4:]
    j = pl.program_id(0)
    rows = acc.shape[0]
    cols = slot.shape[2] // 2

    @pl.when(j == 0)
    def _():
        copies = []
        for k, piece in enumerate(pieces):
            first = 0 if k % per == 0 else pieces[k - 1].shape[0]
            side = lax.rem(at[2] + (k // per) % 2, 2)
            lanes = pl.ds(pl.multiple_of(side * cols, cols), cols)
            place = slot.at[k // (2 * per), pl.ds(first, piece.shape[0]), lanes]
            copies.append(pltpu.make_async_copy(piece, place, sem.at[k]))
        for copy in copies:
            copy.start()
        if last:
            acc[...] = acc_in[...]
            sq[...] = column(sq_in[0:1, :])
        else:
            acc[...] = jnp.zeros_like(acc)
            sq[...] = jnp.zeros_like(sq)
        for copy in copies:
            copy.wait()

    gain = slot[j, 0:16, :][0:1, :].astype(f32)
    raw = slot[j, 16 : 16 + rows, :].astype(f32)
    sq[...] += jnp.sum(raw * raw, axis=1, keepdims=True)
    scaled = (raw * gain).astype(bf16)
    hb[0] = scaled
    acc[...] += lax.dot_general(
        scaled, head[...], (((1,), (1,)), ((), ())), preferred_element_type=f32
    )

    @pl.when(j == count - 1)
    def _():
        if not last:
            outs[0][...] = acc[...]
            outs[1][...] = rows_of([sq[...]])
            return
        lg, st, inv_ref = outs
        inv_c = lax.rsqrt(sq[...] / 5120.0 + eps_norm)
        inv_ref[...] = rows_of([inv_c])
        logits = acc[...] * inv_c
        lg[...] = logits
        half = logits.shape[1]
        entry = lax.broadcasted_iota(jnp.int32, logits.shape, 1) + at[0] * half
        target = column(tgt[...].astype(f32)).astype(jnp.int32)
        top = jnp.max(logits, axis=1, keepdims=True)
        power = jnp.exp(logits - top)
        found = rows_of(
            [
                top,
                jnp.sum(power, axis=1, keepdims=True),
                jnp.sum(power * logits, axis=1, keepdims=True),
                jnp.sum(jnp.where(entry == target, logits, 0.0), axis=1, keepdims=True),
            ]
        )
        for k in range(st.shape[0]):
            st[k] = found


def logits_of(at, first, blocks, head, before=None, targets=None):
    count, per = len(blocks), len(blocks[0]) // 2
    last = before is not None
    half = head.shape[0]
    cols = 2 * blocks[0][0].shape[1]
    height = sum(p.shape[0] for p in blocks[0]) // 2
    rows = height - 16
    anywhere = pl.BlockSpec(memory_space=pl.ANY)
    shapes = [like((count, rows, cols))]
    specs = [pl.BlockSpec((1, rows, cols), lambda j, *a: (j, 0, 0))]
    shapes += [like((rows, half), f32)]
    shapes += [like((8, 8, rows), f32)] if last else []
    shapes += [like((8, rows), f32)]
    extra = (*before, targets) if last else ()
    return pl.pallas_call(
        functools.partial(logits_kernel, count, per, last),
        out_shape=shapes,
        grid_spec=pltpu.PrefetchScalarGridSpec(
            num_scalar_prefetch=1,
            grid=(count,),
            in_specs=[anywhere] * (count * per * 2)
            + [full(e.shape) for e in extra]
            + [pl.BlockSpec((half, cols), lambda j, at: (0, at[8 + first + j]))],
            out_specs=specs + [full(s.shape) for s in shapes[1:]],
            scratch_shapes=[
                VMEM((count, height, cols), bf16),
                VMEM((rows, half), f32),
                VMEM((rows, 1), f32),
                pltpu.SemaphoreType.DMA((count * per * 2,)),
            ],
        ),
        compiler_params=params(),
        cost_estimate=cost(1000, 1000),
        name="logits_last" if last else "logits_first",
    )(at, *[p for b in blocks for p in b], *extra, head)


def policy_kernel(groups, slots_all, at, rewards, lengths, slots, sums_ref, st, lg, inv_ref, tgt, old, dl, small):
    half = lg.shape[1]
    rows = lg.shape[0]
    sums = jnp.sum(sums_ref[:, 0, :], axis=0, keepdims=True)
    lane = lax.broadcasted_iota(jnp.int32, sums.shape, 1)

    def entry_of(k):
        return jnp.sum(jnp.where(lane == k, sums, 0.0), axis=1, keepdims=True)

    advs = [rewards[r] - entry_of(slots[r] // GROUP) / GROUP for r in range(2)]
    live = entry_of(groups)
    top = jnp.max(st[:, 0, :], axis=0, keepdims=True)
    weight = jnp.exp(st[:, 0, :] - top)
    total = jnp.sum(st[:, 1, :] * weight, axis=0, keepdims=True)
    moment = jnp.sum(st[:, 2, :] * weight, axis=0, keepdims=True)
    chosen = jnp.sum(st[:, 3, :], axis=0, keepdims=True)
    lse = top + jnp.log(total)
    inv = inv_ref[0:1, :]
    ratio = jnp.exp(chosen - lse - old[...])
    position = lax.broadcasted_iota(jnp.int32, ratio.shape, 1)
    second_one = position >= rows // 2
    adv = jnp.where(second_one, advs[1], advs[0])
    length = jnp.where(second_one, lengths[1].astype(f32), lengths[0].astype(f32))
    within = jnp.where(second_one, position - rows // 2, position).astype(f32)
    mask = jnp.where(within < length, 1.0, 0.0)
    first = ratio * adv
    second = jnp.clip(ratio, clip_low, clip_high) * adv
    policy = -jnp.minimum(first, second)
    policy = jnp.where(adv < 0, jnp.minimum(policy, -dual_bound * adv), policy)
    active = (first <= second) & jnp.logical_not((adv < 0) & (first < dual_bound * adv))
    grad_logp = slots_all / live * mask * jnp.where(active, -first, 0.0)
    kappa = inv * inv * grad_logp * (chosen - moment / total) / 5120.0
    small[...] = jnp.concatenate(
        [kappa, mask * policy / live, jnp.zeros((6, ratio.shape[1]), f32)], axis=0
    )
    lse_c, scale_c = column(lse), column(grad_logp * inv)
    target = column(tgt[...].astype(f32)).astype(jnp.int32)
    entry = lax.broadcasted_iota(jnp.int32, lg.shape, 1) + at[0] * half
    hit = jnp.where(entry == target, 1.0, 0.0)
    dl[...] = (scale_c * (hit - jnp.exp(lg[...] - lse_c))).astype(bf16)


def policy_of(groups, slots_all, at, scalars, sums, stats, logits, inv, targets, old_logp):
    rows, half = logits.shape
    return pl.pallas_call(
        functools.partial(policy_kernel, groups, float(slots_all)),
        out_shape=[like((rows, half)), like((8, rows), f32)],
        in_specs=[whole(pltpu.SMEM)] * 4 + [whole()] * 6,
        out_specs=[whole()] * 2,
        compiler_params=params(),
        cost_estimate=cost(8 * rows * half, 6 * rows * half, rows * half),
        name="policy",
    )(at, *scalars, sums, stats, logits, inv, targets, old_logp)


def back_kernel(at, dl, dl_o, early, late, small, head, head_o, u0, u1, u2, u3, lines):
    j = pl.program_id(0)
    total = jnp.dot(dl[...], head[...], preferred_element_type=f32)
    total += jnp.dot(dl_o[...], head_o[...], preferred_element_type=f32)
    for k, out in enumerate((u0, u1, u2, u3)):

        @pl.when(j == k)
        def _(out=out):
            out[...] = total.astype(bf16)

    scaled = jnp.where(j < 3, early[0], late[0]).astype(f32)
    loss = jnp.sum(small[1:2, :], axis=1, keepdims=True) / 4
    line = jnp.concatenate(
        [jnp.sum(total * scaled, axis=0, keepdims=True), jnp.broadcast_to(loss, (1, 128))], axis=1
    )
    lines[j] = line


def back_of(at, dl, dl_o, early, late, small, head, head_o, cols):
    rows, half = dl.shape
    shapes = [like((rows, cols))] * 4 + [like((4, 1, cols + 128), f32)]
    return pl.pallas_call(
        back_kernel,
        out_shape=shapes,
        grid_spec=pltpu.PrefetchScalarGridSpec(
            num_scalar_prefetch=1,
            grid=(4,),
            in_specs=[full((rows, half))] * 2
            + [
                pl.BlockSpec((1, rows, cols), lambda j, at: (jnp.minimum(j, 2), 0, at[2])),
                pl.BlockSpec((1, rows, cols), lambda j, at: (0, 0, at[2])),
                full(small.shape),
            ]
            + [pl.BlockSpec((half, cols), lambda j, at: (0, 2 * at[8 + j] + at[2]))] * 2,
            out_specs=[full(s.shape) for s in shapes],
        ),
        compiler_params=params(),
        cost_estimate=cost(2 * rows * 8 * cols * half, 32 * rows * cols),
        name="back",
    )(at, dl, dl_o, early, late, small, head, head_o)


def heads_kernel(at, early, late, dl, to_x, to_z):
    j = pl.program_id(0)
    scaled = jnp.where(j < 3, early[0], late[0])
    cols = scaled.shape[1] // 2
    step, half = cols // 4, dl.shape[1] // 2
    got = lax.dot_general(
        scaled, dl[...], (((0,), (0,)), ((), ())), preferred_element_type=f32
    ).astype(bf16)
    for i in range(2):
        place = 2 * at[8 + j] + i
        for k in range(4):
            part = got[i * cols + k * step : i * cols + (k + 1) * step, :]
            to_x[k, place] = part[:, :half]
            to_z[place, k] = part[:, half:]


def heads_of(at, early, late, dl):
    _, rows, cols = early.shape
    half = dl.shape[1]
    step = cols // 8
    shapes = [like((4, 8, step, half // 2)), like((8, 4, step, half // 2))]
    return pl.pallas_call(
        heads_kernel,
        out_shape=shapes,
        grid_spec=pltpu.PrefetchScalarGridSpec(
            num_scalar_prefetch=1,
            grid=(4,),
            in_specs=[
                pl.BlockSpec((1, rows, cols), lambda j, at: (jnp.minimum(j, 2), 0, 0)),
                full(late.shape),
                full((rows, half)),
            ],
            out_specs=[full(s.shape) for s in shapes],
        ),
        compiler_params=params(),
        cost_estimate=cost(2 * rows * 4 * cols * half, 24 * rows * cols),
        name="heads",
    )(at, early, late, dl)


def sum_first_kernel(a, out):
    for k in range(out.shape[0]):
        total = a[0, k].astype(f32)
        for s in range(1, a.shape[0]):
            total = total + a[s, k].astype(f32)
        out[k] = total.astype(out.dtype)


def sum_first(value, name):
    return pl.pallas_call(
        sum_first_kernel,
        out_shape=like(value.shape[1:]),
        in_specs=[whole()],
        out_specs=whole(),
        compiler_params=params(),
        cost_estimate=cost(value.size, 3 * value.size),
        name=name,
    )(value)


def join_kernel(from_z, from_x, out):
    width = from_x.shape[1]
    total = from_z[0].astype(f32)
    for k in range(1, from_z.shape[0]):
        total = total + from_z[k].astype(f32)
    out[:, :width] = total
    out[:, width:] = from_x[...].astype(f32)


def final_kernel(u0, u1, u2, u3, h_ref, g_ref, small, out):
    gain = g_ref[...].astype(f32)
    resp, rows, _ = h_ref.shape
    kappa = column(small[0:1, :])
    for r in range(resp):
        cut = slice(r * rows, (r + 1) * rows)
        u = sum(v[cut, :].astype(f32) for v in (u0, u1, u2, u3))
        h = h_ref[r].astype(f32)
        out[r] = (gain * u - h * kappa[cut, :]).astype(bf16)


def simple(kernel, shapes, ins, nbytes, name, flops=None):
    return pl.pallas_call(
        kernel,
        out_shape=shapes,
        in_specs=[whole(pltpu.SMEM if v.ndim == 1 else VMEM) for v in ins],
        out_specs=[whole()] * len(shapes),
        compiler_params=params(),
        cost_estimate=cost(flops or nbytes // 2, nbytes),
        name=name,
    )(*ins)


def after(value, *first):
    return lax.optimization_barrier((value, *first))[0]


def body(hidden, gain, head, targets, lengths, old_logp, rewards, group_slot):
    resp_here, length_max, cols = hidden.shape
    rows = resp_here * length_max
    x, y, z, c = (lax.axis_index(a) for a in ("x", "y", "z", "c"))
    chips = (y + jnp.array([0, 3, 1, 2], jnp.int32)) % 4
    at = jnp.concatenate([jnp.stack([2 * y + c, y, c, z, x, x, x, x]), chips]).astype(jnp.int32)

    payload = jnp.concatenate(
        [jnp.broadcast_to(gain[None], (16, cols)), hidden.reshape(rows, cols)], axis=0
    )
    cut = 16 + length_max
    prev, following = shift(payload, "y", 1), shift(payload, "y", -1)
    own_o = shift(payload, "c", 1)

    groups_all = resp_here * lax.axis_size(DP) // GROUP
    scalars = (rewards, lengths, group_slot)
    (local,) = simple(
        functools.partial(local_kernel, groups_all),
        [like((lax.axis_size(DP), 1, 128), f32)],
        scalars,
        1 << 14,
        "local",
    )
    sums = lax.all_to_all(local, DP, 0, 0, tiled=True)
    prev, following, sums = lax.optimization_barrier((prev, following, sums))

    far_a, far_b = prev[:cut], following[cut:]
    far_a, far_b, prev, following = lax.optimization_barrier((far_a, far_b, prev, following))
    far_a, far_b = shift(far_a, "y", 1), shift(far_b, "y", -1)
    prev_o, following_o = shift(prev, "c", 1), shift(following, "c", 1)
    early, acc, sq = logits_of(
        at, 0, [(payload, own_o), (prev, prev_o), (following, following_o)], head
    )
    far_a, far_b = after(far_a, acc), after(far_b, acc)
    far_a_o, far_b_o = shift(far_a, "c", 1), shift(far_b, "c", 1)

    slots_all = rows * lax.axis_size(DP)
    targets = targets.reshape(1, rows)
    old_logp = old_logp.reshape(1, rows)

    late, logits, stats, inv = logits_of(
        at, 3, [(far_a, far_b, far_a_o, far_b_o)], head, (acc, sq), targets
    )
    head_o = shift(after(head, logits), "c", 1)
    all_stats = lax.all_to_all(stats, FSDP, 0, 0, tiled=True)
    dl, small = policy_of(groups_all, slots_all, at, scalars, sums, all_stats, logits, inv, targets, old_logp)
    part, half = cols // 4, dl.shape[1] // 2

    dl_o = shift(dl, "c", 1)
    to_x, to_z = heads_of(at, early, late, dl)
    half_z = lax.psum_scatter(to_z, "z", scatter_dimension=0, tiled=False)
    from_x = lax.all_to_all(to_x, "x", 0, 0, tiled=True)
    u0, u1, u2, u3, lines = back_of(
        at, after(dl, to_x), dl_o, early, late, small, head, head_o, cols
    )
    tail = lines[0] + shift(lines[1], "y", -1) + shift(lines[2], "y", 1) + shift(lines[3], "y", 2)
    u1, u2, u3, tail = lax.optimization_barrier((u1, u2, u3, tail))
    u1, u2, u3 = shift(u1, "y", -1), shift(u2, "y", 1), shift(u3, "y", 2)

    for step in (1, -1, 3):
        tail = tail + turn(tail, step)
    from_x = after(from_x, tail, half_z)

    to_z = sum_first(from_x, "sum_x")
    from_z = lax.all_to_all(to_z, "z", 0, 0, tiled=True)
    half_z = lax.psum_scatter(half_z, "x", scatter_dimension=0, tiled=False)
    u1, u2, u3, _ = lax.optimization_barrier((u1, u2, u3, to_z))
    (grad_hidden,) = simple(
        final_kernel,
        [like(hidden.shape)],
        (u0, u1, u2, u3, hidden, gain.reshape(1, cols), small),
        12 * rows * cols,
        "final",
        200 * 10**9,
    )
    tail = after(tail, grad_hidden)
    tail = tail + shift(tail, "x", 1) + shift(tail, "x", 2) + shift(tail, "x", -1)
    (grad_head_t,) = simple(
        join_kernel,
        [like((part, 2 * half), f32)],
        (from_z, half_z),
        2 * from_z.size + 16 * part * half,
        "join",
    )
    tail = tail.reshape(-1)
    return (tail[cols], grad_hidden, tail[:cols] / gain.astype(f32), grad_head_t)


def solution(mesh):
    split = Mesh(mesh.devices.reshape(8, 4, 4, 2), ("z", "x", "y", "c"))
    return jax.shard_map(
        body,
        mesh=split,
        in_specs=(
            P(DP, None, FSDP),
            P(FSDP),
            P(FSDP, None),
            P(DP, None),
            P(DP),
            P(DP, None),
            P(DP),
            P(DP),
        ),
        out_specs=(P(), P(DP, None, FSDP), P(FSDP), P(DP, FSDP)),
        check_vma=False,
    )
```

```python
import functools

import jax
import jax.numpy as jnp
from jax import lax
from jax.experimental import pallas as pl
from jax.experimental.pallas import tpu as pltpu
from jax.sharding import Mesh
from jax.sharding import PartitionSpec as P

GROUP = 8
FSDP = ("y", "c")
DP = ("z", "x")
SIZES = {"z": 8, "x": 4, "y": 4, "c": 2}

eps_norm = 1e-06
clip_low = 0.8
clip_high = 1.2
dual_bound = 3.0

f32, bf16 = jnp.float32, jnp.bfloat16
VMEM = pltpu.VMEM


def shift(value, axis, step):
    n = SIZES[axis]
    return lax.ppermute(value, axis, [(i, (i + step) % n) for i in range(n)])


def turn(value, step):
    return lax.ppermute(
        value, "z", [(i, (i + (step if i % 2 == 0 else -step)) % 8) for i in range(8)]
    )


def params(limit=60 << 20):
    return pltpu.CompilerParams(vmem_limit_bytes=limit)


def cost(flops, nbytes, trans=0):
    return pl.CostEstimate(flops=flops, bytes_accessed=nbytes, transcendentals=trans)


def whole(space=None):
    return pl.BlockSpec(memory_space=space or VMEM)


def like(shape, kind=bf16):
    return jax.ShapeDtypeStruct(shape, kind)


def column(row):
    n = row.shape[1]
    return jnp.transpose(jnp.broadcast_to(row, (128, n)))[:, 0:1]


def rows_of(columns):
    n = columns[0].shape[0]
    lane = lax.broadcasted_iota(jnp.int32, (n, 128), 1)
    table = jnp.zeros((n, 128), f32)
    for k, col in enumerate(columns):
        table = jnp.where(lane == k, col, table)
    return jnp.transpose(table)[0:8, :]


def full(shape):
    return pl.BlockSpec(shape, lambda k, *at: (0,) * len(shape))


def local_kernel(groups, rewards, lengths, slots, out):
    lane = lax.broadcasted_iota(jnp.int32, (1, 128), 1)
    row = jnp.zeros((1, 128), f32)
    for r in range(2):
        row += jnp.where(lane == slots[r] // GROUP, rewards[r], 0.0)
        row += jnp.where(lane == groups, lengths[r].astype(f32), 0.0)
    for k in range(out.shape[0]):
        out[k] = row


def logits_kernel(count, per, last, at, *refs):
    pieces = refs[: count * per * 2]
    refs = refs[count * per * 2 :]
    if last:
        acc_in, sq_in, tgt = refs[:3]
        refs = refs[3:]
    head, hb = refs[:2]
    outs, (slot, acc, sq, sem) = refs[2:-4], refs[-4:]
    j = pl.program_id(0)
    rows = acc.shape[0]
    cols = slot.shape[2] // 2

    @pl.when(j == 0)
    def _():
        copies = []
        for k, piece in enumerate(pieces):
            first = 0 if k % per == 0 else pieces[k - 1].shape[0]
            side = lax.rem(at[2] + (k // per) % 2, 2)
            lanes = pl.ds(pl.multiple_of(side * cols, cols), cols)
            place = slot.at[k // (2 * per), pl.ds(first, piece.shape[0]), lanes]
            copies.append(pltpu.make_async_copy(piece, place, sem.at[k]))
        for copy in copies:
            copy.start()
        if last:
            acc[...] = acc_in[...]
            sq[...] = column(sq_in[0:1, :])
        else:
            acc[...] = jnp.zeros_like(acc)
            sq[...] = jnp.zeros_like(sq)
        for copy in copies:
            copy.wait()

    gain = slot[j, 0:16, :][0:1, :].astype(f32)
    raw = slot[j, 16 : 16 + rows, :].astype(f32)
    sq[...] += jnp.sum(raw * raw, axis=1, keepdims=True)
    scaled = (raw * gain).astype(bf16)
    hb[0] = scaled
    acc[...] += lax.dot_general(
        scaled, head[...], (((1,), (1,)), ((), ())), preferred_element_type=f32
    )

    @pl.when(j == count - 1)
    def _():
        if not last:
            outs[0][...] = acc[...]
            outs[1][...] = rows_of([sq[...]])
            return
        lg, st, inv_ref = outs
        inv_c = lax.rsqrt(sq[...] / 5120.0 + eps_norm)
        inv_ref[...] = rows_of([inv_c])
        logits = acc[...] * inv_c
        lg[...] = logits
        half = logits.shape[1]
        entry = lax.broadcasted_iota(jnp.int32, logits.shape, 1) + at[0] * half
        target = column(tgt[...].astype(f32)).astype(jnp.int32)
        top = jnp.max(logits, axis=1, keepdims=True)
        power = jnp.exp(logits - top)
        found = rows_of(
            [
                top,
                jnp.sum(power, axis=1, keepdims=True),
                jnp.sum(power * logits, axis=1, keepdims=True),
                jnp.sum(jnp.where(entry == target, logits, 0.0), axis=1, keepdims=True),
            ]
        )
        for k in range(st.shape[0]):
            st[k] = found


def logits_of(at, first, blocks, head, before=None, targets=None):
    count, per = len(blocks), len(blocks[0]) // 2
    last = before is not None
    half = head.shape[0]
    cols = 2 * blocks[0][0].shape[1]
    height = sum(p.shape[0] for p in blocks[0]) // 2
    rows = height - 16
    anywhere = pl.BlockSpec(memory_space=pl.ANY)
    shapes = [like((count, rows, cols))]
    specs = [pl.BlockSpec((1, rows, cols), lambda j, *a: (j, 0, 0))]
    shapes += [like((rows, half), f32)]
    shapes += [like((8, 8, rows), f32)] if last else []
    shapes += [like((8, rows), f32)]
    extra = (*before, targets) if last else ()
    return pl.pallas_call(
        functools.partial(logits_kernel, count, per, last),
        out_shape=shapes,
        grid_spec=pltpu.PrefetchScalarGridSpec(
            num_scalar_prefetch=1,
            grid=(count,),
            in_specs=[anywhere] * (count * per * 2)
            + [full(e.shape) for e in extra]
            + [pl.BlockSpec((half, cols), lambda j, at: (0, at[8 + first + j]))],
            out_specs=specs + [full(s.shape) for s in shapes[1:]],
            scratch_shapes=[
                VMEM((count, height, cols), bf16),
                VMEM((rows, half), f32),
                VMEM((rows, 1), f32),
                pltpu.SemaphoreType.DMA((count * per * 2,)),
            ],
        ),
        compiler_params=params(),
        cost_estimate=cost(1000, 1000),
        name="logits_last" if last else "logits_first",
    )(at, *[p for b in blocks for p in b], *extra, head)


def policy_kernel(groups, slots_all, at, rewards, lengths, slots, sum0, sum1, sum2, sum3, st, lg, inv_ref, tgt, old, dl, small):
    half = lg.shape[1]
    rows = lg.shape[0]
    sums = sum0[...] + sum1[...] + sum2[...] + sum3[...]
    lane = lax.broadcasted_iota(jnp.int32, sums.shape, 1)

    def entry_of(k):
        return jnp.sum(jnp.where(lane == k, sums, 0.0), axis=1, keepdims=True)

    advs = [rewards[r] - entry_of(slots[r] // GROUP) / GROUP for r in range(2)]
    live = entry_of(groups)
    top = jnp.max(st[:, 0, :], axis=0, keepdims=True)
    weight = jnp.exp(st[:, 0, :] - top)
    total = jnp.sum(st[:, 1, :] * weight, axis=0, keepdims=True)
    moment = jnp.sum(st[:, 2, :] * weight, axis=0, keepdims=True)
    chosen = jnp.sum(st[:, 3, :], axis=0, keepdims=True)
    lse = top + jnp.log(total)
    inv = inv_ref[0:1, :]
    ratio = jnp.exp(chosen - lse - old[...])
    position = lax.broadcasted_iota(jnp.int32, ratio.shape, 1)
    second_one = position >= rows // 2
    adv = jnp.where(second_one, advs[1], advs[0])
    length = jnp.where(second_one, lengths[1].astype(f32), lengths[0].astype(f32))
    within = jnp.where(second_one, position - rows // 2, position).astype(f32)
    mask = jnp.where(within < length, 1.0, 0.0)
    first = ratio * adv
    second = jnp.clip(ratio, clip_low, clip_high) * adv
    policy = -jnp.minimum(first, second)
    policy = jnp.where(adv < 0, jnp.minimum(policy, -dual_bound * adv), policy)
    active = (first <= second) & jnp.logical_not((adv < 0) & (first < dual_bound * adv))
    grad_logp = slots_all / live * mask * jnp.where(active, -first, 0.0)
    kappa = inv * inv * grad_logp * (chosen - moment / total) / 5120.0
    small[...] = jnp.concatenate(
        [kappa, mask * policy / live, jnp.zeros((6, ratio.shape[1]), f32)], axis=0
    )
    lse_c, scale_c = column(lse), column(grad_logp * inv)
    target = column(tgt[...].astype(f32)).astype(jnp.int32)
    entry = lax.broadcasted_iota(jnp.int32, lg.shape, 1) + at[0] * half
    hit = jnp.where(entry == target, 1.0, 0.0)
    dl[...] = (scale_c * (hit - jnp.exp(lg[...] - lse_c))).astype(bf16)


def policy_of(groups, slots_all, at, scalars, sums, stats, logits, inv, targets, old_logp):
    rows, half = logits.shape
    return pl.pallas_call(
        functools.partial(policy_kernel, groups, float(slots_all)),
        out_shape=[like((rows, half)), like((8, rows), f32)],
        in_specs=[whole(pltpu.SMEM)] * 4 + [whole()] * 9,
        out_specs=[whole()] * 2,
        compiler_params=params(),
        cost_estimate=cost(8 * rows * half, 6 * rows * half, rows * half),
        name="policy",
    )(at, *scalars, *sums, stats, logits, inv, targets, old_logp)


def back_kernel(at, dl, dl_o, early, late, small, head, head_o, u0, u1, u2, u3, lines):
    j = pl.program_id(0)
    total = jnp.dot(dl[...], head[...], preferred_element_type=f32)
    total += jnp.dot(dl_o[...], head_o[...], preferred_element_type=f32)
    for k, out in enumerate((u0, u1, u2, u3)):

        @pl.when(j == k)
        def _(out=out):
            out[...] = total.astype(bf16)

    scaled = jnp.where(j < 3, early[0], late[0]).astype(f32)
    loss = jnp.sum(small[1:2, :], axis=1, keepdims=True) / 4
    line = jnp.concatenate(
        [jnp.sum(total * scaled, axis=0, keepdims=True), jnp.broadcast_to(loss, (1, 128))], axis=1
    )
    lines[j] = line


def back_of(at, dl, dl_o, early, late, small, head, head_o, cols):
    rows, half = dl.shape
    shapes = [like((rows, cols))] * 4 + [like((4, 1, cols + 128), f32)]
    return pl.pallas_call(
        back_kernel,
        out_shape=shapes,
        grid_spec=pltpu.PrefetchScalarGridSpec(
            num_scalar_prefetch=1,
            grid=(4,),
            in_specs=[full((rows, half))] * 2
            + [
                pl.BlockSpec((1, rows, cols), lambda j, at: (jnp.minimum(j, 2), 0, at[2])),
                pl.BlockSpec((1, rows, cols), lambda j, at: (0, 0, at[2])),
                full(small.shape),
            ]
            + [pl.BlockSpec((half, cols), lambda j, at: (0, 2 * at[8 + j] + at[2]))] * 2,
            out_specs=[full(s.shape) for s in shapes],
        ),
        compiler_params=params(),
        cost_estimate=cost(2 * rows * 8 * cols * half, 32 * rows * cols),
        name="back",
    )(at, dl, dl_o, early, late, small, head, head_o)


def heads_kernel(at, early, late, dl, to_x, to_z):
    j = pl.program_id(0)
    scaled = jnp.where(j < 3, early[0], late[0])
    cols = scaled.shape[1] // 2
    step, half = cols // 4, dl.shape[1] // 2
    got = lax.dot_general(
        scaled, dl[...], (((0,), (0,)), ((), ())), preferred_element_type=f32
    ).astype(bf16)
    for i in range(2):
        place = 2 * at[8 + j] + i
        for k in range(4):
            part = got[i * cols + k * step : i * cols + (k + 1) * step, :]
            to_x[k, place] = part[:, :half]
            to_z[place, k] = part[:, half:]


def heads_of(at, early, late, dl):
    _, rows, cols = early.shape
    half = dl.shape[1]
    step = cols // 8
    shapes = [like((4, 8, step, half // 2)), like((8, 4, step, half // 2))]
    return pl.pallas_call(
        heads_kernel,
        out_shape=shapes,
        grid_spec=pltpu.PrefetchScalarGridSpec(
            num_scalar_prefetch=1,
            grid=(4,),
            in_specs=[
                pl.BlockSpec((1, rows, cols), lambda j, at: (jnp.minimum(j, 2), 0, 0)),
                full(late.shape),
                full((rows, half)),
            ],
            out_specs=[full(s.shape) for s in shapes],
        ),
        compiler_params=params(),
        cost_estimate=cost(2 * rows * 4 * cols * half, 24 * rows * cols),
        name="heads",
    )(at, early, late, dl)


def sum_first_kernel(a, out):
    for k in range(out.shape[0]):
        total = a[0, k].astype(f32)
        for s in range(1, a.shape[0]):
            total = total + a[s, k].astype(f32)
        out[k] = total.astype(out.dtype)


def sum_first(value, name):
    return pl.pallas_call(
        sum_first_kernel,
        out_shape=like(value.shape[1:]),
        in_specs=[whole()],
        out_specs=whole(),
        compiler_params=params(),
        cost_estimate=cost(value.size, 3 * value.size),
        name=name,
    )(value)


def join_kernel(from_z, from_x, out):
    width = from_x.shape[1]
    total = from_z[0].astype(f32)
    for k in range(1, from_z.shape[0]):
        total = total + from_z[k].astype(f32)
    out[:, :width] = total
    out[:, width:] = from_x[...].astype(f32)


def final_kernel(u0, u1, u2, u3, h_ref, g_ref, small, out):
    gain = g_ref[...].astype(f32)
    resp, rows, _ = h_ref.shape
    kappa = column(small[0:1, :])
    for r in range(resp):
        cut = slice(r * rows, (r + 1) * rows)
        u = sum(v[cut, :].astype(f32) for v in (u0, u1, u2, u3))
        h = h_ref[r].astype(f32)
        out[r] = (gain * u - h * kappa[cut, :]).astype(bf16)


def simple(kernel, shapes, ins, nbytes, name, flops=None):
    return pl.pallas_call(
        kernel,
        out_shape=shapes,
        in_specs=[whole(pltpu.SMEM if v.ndim == 1 else VMEM) for v in ins],
        out_specs=[whole()] * len(shapes),
        compiler_params=params(),
        cost_estimate=cost(flops or nbytes // 2, nbytes),
        name=name,
    )(*ins)


def after(value, *first):
    return lax.optimization_barrier((value, *first))[0]


def body(hidden, gain, head, targets, lengths, old_logp, rewards, group_slot):
    resp_here, length_max, cols = hidden.shape
    rows = resp_here * length_max
    x, y, z, c = (lax.axis_index(a) for a in ("x", "y", "z", "c"))
    chips = (y + jnp.array([0, 3, 1, 2], jnp.int32)) % 4
    at = jnp.concatenate([jnp.stack([2 * y + c, y, c, z, x, x, x, x]), chips]).astype(jnp.int32)

    payload = jnp.concatenate(
        [jnp.broadcast_to(gain[None], (16, cols)), hidden.reshape(rows, cols)], axis=0
    )
    cut = 16 + length_max
    prev, following = shift(payload, "y", 1), shift(payload, "y", -1)
    own_o = shift(payload, "c", 1)

    groups_all = resp_here * lax.axis_size(DP) // GROUP
    scalars = (rewards, lengths, group_slot)
    (local,) = simple(
        functools.partial(local_kernel, groups_all),
        [like((lax.axis_size("z"), 1, 128), f32)],
        scalars,
        1 << 14,
        "local",
    )
    over_z = lax.all_to_all(local, "z", 0, 0, tiled=True).sum(axis=0)
    prev, following, over_z = lax.optimization_barrier((prev, following, over_z))

    far_a, far_b = prev[:cut], following[cut:]
    far_a, far_b, prev, following = lax.optimization_barrier((far_a, far_b, prev, following))
    far_a, far_b = shift(far_a, "y", 1), shift(far_b, "y", -1)
    prev_o, following_o = shift(prev, "c", 1), shift(following, "c", 1)
    early, acc, sq = logits_of(
        at, 0, [(payload, own_o), (prev, prev_o), (following, following_o)], head
    )
    far_a, far_b = after(far_a, acc), after(far_b, acc)
    far_a_o, far_b_o = shift(far_a, "c", 1), shift(far_b, "c", 1)

    slots_all = rows * lax.axis_size(DP)
    targets = targets.reshape(1, rows)
    old_logp = old_logp.reshape(1, rows)

    late, logits, stats, inv = logits_of(
        at, 3, [(far_a, far_b, far_a_o, far_b_o)], head, (acc, sq), targets
    )
    head_o = shift(after(head, logits), "c", 1)
    over_z = after(over_z, logits)
    sums = (over_z, shift(over_z, "x", 1), shift(over_z, "x", 2), shift(over_z, "x", -1))
    all_stats = lax.all_to_all(stats, FSDP, 0, 0, tiled=True)
    dl, small = policy_of(groups_all, slots_all, at, scalars, sums, all_stats, logits, inv, targets, old_logp)
    part, half = cols // 4, dl.shape[1] // 2

    dl_o = shift(dl, "c", 1)
    to_x, to_z = heads_of(at, early, late, dl)
    half_z = lax.psum_scatter(to_z, "z", scatter_dimension=0, tiled=False)
    from_x = lax.all_to_all(to_x, "x", 0, 0, tiled=True)
    u0, u1, u2, u3, lines = back_of(
        at, after(dl, to_x), dl_o, early, late, small, head, head_o, cols
    )
    tail = lines[0] + shift(lines[1], "y", -1) + shift(lines[2], "y", 1) + shift(lines[3], "y", 2)
    u1, u2, u3, tail = lax.optimization_barrier((u1, u2, u3, tail))
    u1, u2, u3 = shift(u1, "y", -1), shift(u2, "y", 1), shift(u3, "y", 2)

    for step in (1, -1, 3):
        tail = tail + turn(tail, step)
    from_x = after(from_x, tail, half_z)

    to_z = sum_first(from_x, "sum_x")
    from_z = lax.all_to_all(to_z, "z", 0, 0, tiled=True)
    half_z = lax.psum_scatter(half_z, "x", scatter_dimension=0, tiled=False)
    u1, u2, u3, _ = lax.optimization_barrier((u1, u2, u3, to_z))
    (grad_hidden,) = simple(
        final_kernel,
        [like(hidden.shape)],
        (u0, u1, u2, u3, hidden, gain.reshape(1, cols), small),
        12 * rows * cols,
        "final",
        200 * 10**9,
    )
    tail = after(tail, grad_hidden)
    tail = tail + shift(tail, "x", 1) + shift(tail, "x", 2) + shift(tail, "x", -1)
    (grad_head_t,) = simple(
        join_kernel,
        [like((part, 2 * half), f32)],
        (from_z, half_z),
        2 * from_z.size + 16 * part * half,
        "join",
    )
    tail = tail.reshape(-1)
    return (tail[cols], grad_hidden, tail[:cols] / gain.astype(f32), grad_head_t)


def solution(mesh):
    split = Mesh(mesh.devices.reshape(8, 4, 4, 2), ("z", "x", "y", "c"))
    return jax.shard_map(
        body,
        mesh=split,
        in_specs=(
            P(DP, None, FSDP),
            P(FSDP),
            P(FSDP, None),
            P(DP, None),
            P(DP),
            P(DP, None),
            P(DP),
            P(DP),
        ),
        out_specs=(P(), P(DP, None, FSDP), P(FSDP), P(DP, FSDP)),
        check_vma=False,
    )
```
